512 devices in a mesh: pool: 64 (over z, y), mp: 8 (over x, core).
Axes of the slice: x: 4, y: 8, z: 8, core: 2. Of those that a mesh axis runs over, the one named last changes fastest.
Arguments:
- hidden: float32 [64, 2048], P('pool', 'mp'), may hold values from -40 to 40
- norm_gain: float32 [2048], replicated, may hold values from 0.5 to 2
- w_query: bfloat16 [2048, 2048], P(None, 'mp'), may hold values from -0.75 to 0.75
- w_keyval: bfloat16 [2048, 1024], P(None, 'mp'), may hold values from -0.75 to 0.75
- w_out: bfloat16 [2048, 2048], P('mp'), may hold values from -0.125 to 0.125
- kv_cache: bfloat16 [6144, 8, 128, 128], P('pool', 'mp'), may hold values from -900 to 900
- block_slot: int32 [64, 128], replicated, may hold values from 0 to 6143, as said below
- lengths: int32 [64], replicated, may hold values from 1 to 16384, as said below
Outputs:
- layer_out: float32 [64, 2048], P('pool', 'mp')
- new_kv: bfloat16 [64, 1024], P('pool', 'mp')
The draws below stay inside these ranges and needn't reach their ends.
Inputs may be any that keep to these rules, and one draw needn't show every extreme that they name: `lengths`: some request holds exactly 16384 tokens in every draw. `block_slot`: A slot number s lies on index s // 96 of pool, at its slot s % 96. Entries of live blocks (b * 128 < lengths[r]) are all distinct; entries of other blocks are arbitrary slot numbers and must be ignored. The live blocks number exactly 4128 in all.
All inputs are finite; a program needn't handle non-finite values.
Results may differ from the reference program's by a relative error of at most 0.029.
Values may be sent and summed in bfloat16 or wider, within the bound.
No kernel may reach another device: no remote copies, remote signals or barrier semaphores. Data moves between devices by JAX's collectives and lax.ppermute only.
A program may use at most 64 MiB of HBM per device.

```python
import math
import jax
import jax.numpy as jnp
from jax import lax

D = 2048
HEADS = 32
KVH = 8
HD = 64
BLK = 128
MAXLEN = 16384
MAXB = 128
REQS = 64
CACHE_SLOTS = 6144


def cache_layout(key):
    key_list = jax.random.split(jax.random.fold_in(key, 11), 5)
    half_reqs = REQS // 2
    first_half = jax.random.randint(key_list[0], (half_reqs,), 1, MAXB + 1)
    first_half = first_half.at[0].set(MAXB)
    sorted_counts = jnp.concatenate([first_half, MAXB + 1 - first_half])
    req_order = jax.random.permutation(key_list[1], REQS)
    block_counts = jnp.zeros((REQS,), jnp.int32).at[req_order].set(sorted_counts.astype(jnp.int32))
    tail_len = jax.random.randint(key_list[2], (REQS,), 1, BLK + 1)
    req_lengths = (block_counts - 1) * BLK + tail_len
    req_lengths = req_lengths.at[req_order[0]].set(MAXLEN)
    offsets = jnp.cumsum(block_counts) - block_counts
    slot_order = jax.random.permutation(key_list[3], CACHE_SLOTS)
    slot_index = offsets[:, None] + jnp.arange(MAXB)[None, :]
    is_live = jnp.arange(MAXB)[None, :] < block_counts[:, None]
    taken = slot_order[jnp.minimum(slot_index, CACHE_SLOTS - 1)]
    filler = jax.random.randint(key_list[4], (REQS, MAXB), 0, CACHE_SLOTS)
    slot_table = jnp.where(is_live, taken, filler)
    partner = req_order[half_reqs]
    slot_table = slot_table.at[partner, MAXB - 1].set(CACHE_SLOTS - 1)
    slot_table = slot_table.at[partner, MAXB - 2].set(0)
    return (req_lengths.astype(jnp.int32), slot_table.astype(jnp.int32))


def draw_lengths(key, part):
    return cache_layout(key)[0]


def draw_block_slot(key, part):
    return cache_layout(key)[1]


def draw_kv_cache(key, part):
    key_list = jax.random.split(jax.random.fold_in(key, 23), 1)
    shape_all = (CACHE_SLOTS, KVH, BLK, 2 * HD)
    result = jnp.clip(jax.random.normal(key_list[0], shape_all, jnp.float32), -4.0, 4.0) * 6.0
    return result.astype(jnp.bfloat16)


def draw_hidden(key, part):
    key_list = jax.random.split(jax.random.fold_in(key, 31), 3)
    row_scale = jnp.exp(jax.random.uniform(key_list[1], (REQS, 1), jnp.float32, jnp.log(0.3), jnp.log(3.0)))
    col_scale = jnp.exp(jax.random.uniform(key_list[2], (1, D), jnp.float32, jnp.log(0.3), jnp.log(3.0)))
    base = jnp.clip(jax.random.normal(key_list[0], (REQS, D), jnp.float32), -4.0, 4.0)
    return (base * row_scale * col_scale).astype(jnp.float32)


def shard_levels(own_key, dims, cuts, low, largest):
    def one(axis_at, blocks):
        steps = jax.random.uniform(jax.random.fold_in(jax.random.fold_in(own_key, 6), axis_at), (blocks,), jnp.float32, low / len(cuts), largest / len(cuts))
        return jnp.repeat(jnp.exp(steps), dims[axis_at] // blocks).reshape((-1,) + (1,) * (len(dims) - axis_at - 1))

    gain = one(*cuts[0])
    for cut in cuts[1:]:
        gain = gain * one(*cut)
    return gain


def bell_draw(rng, extent, spread, limit, shards=(), dtype=jnp.bfloat16):
    level = shard_levels(rng, extent, shards, -0.22, 0.18) if shards else 1.0
    drawn = jax.random.normal(rng, extent, jnp.float32) * spread * level
    return jnp.minimum(jnp.maximum(drawn, -limit), limit).astype(dtype)


def setup_inputs(seed: int = 0) -> dict:
    splits = jax.random.split(jax.random.key(seed), 9)
    hidden = draw_hidden(jax.random.fold_in(splits[8], 71), 0)
    norm_gain = jnp.clip(jnp.exp(jax.random.uniform(splits[1], (D,), jnp.float32, math.log(0.5), math.log(2.0))), 0.5, 2.0)
    w_query = bell_draw(splits[2], (D, HEADS * HD), (D // 32) ** -0.5, 0.75, ((1, 8),))
    w_keyval = bell_draw(splits[3], (D, KVH * 2 * HD), (D // 32) ** -0.5, 0.75, ((1, 8),))
    w_out = bell_draw(splits[4], (HEADS * HD, D), (HEADS * HD) ** -0.5, 0.125, ((0, 8),))
    kv_cache = draw_kv_cache(jax.random.fold_in(splits[8], 71), 0)
    block_slot = draw_block_slot(jax.random.fold_in(splits[8], 71), 0)
    lengths = draw_lengths(jax.random.fold_in(splits[8], 71), 0)
    return dict(hidden=hidden, norm_gain=norm_gain, w_query=w_query, w_keyval=w_keyval, w_out=w_out, kv_cache=kv_cache, block_slot=block_slot, lengths=lengths)


EPSILON = 1e-05
RESIDUAL_SCALE = 0.22
SCORE_SCALE = 0.015625
ROPE_BASE = 10000000.0
MASKED = -1e+30

def rotate(values, positions):
    half_dim = values.shape[-1] // 2
    inverse = ROPE_BASE ** (-jnp.arange(half_dim).astype(jnp.float32) * 2.0 / values.shape[-1])
    angles = positions[:, None] * inverse[None, :]
    cosine = jnp.cos(angles)[:, None, :]
    sine_part = jnp.sin(angles)[:, None, :]
    front_half = values[..., :half_dim]
    back_half = values[..., half_dim:]
    return jnp.concatenate([front_half * cosine - back_half * sine_part, back_half * cosine + front_half * sine_part], -1)

def reference(hidden, norm_gain, w_query, w_keyval, w_out, kv_cache, block_slot, lengths):
    requests = hidden.shape[0]
    variance = lax.optimization_barrier(jnp.mean(hidden * hidden, axis=-1, keepdims=True))
    normed = (hidden * lax.rsqrt(variance + EPSILON) * norm_gain).astype(jnp.bfloat16)
    queries = jnp.dot(normed, w_query, preferred_element_type=jnp.float32).reshape(requests, HEADS, HD)
    key_value = jnp.dot(normed, w_keyval, preferred_element_type=jnp.float32).reshape(requests, KVH, 2, HD)
    positions = lengths.astype(jnp.float32)
    queries = rotate(queries, positions).astype(jnp.bfloat16)
    new_key = rotate(key_value[:, :, 0], positions).astype(jnp.bfloat16)
    new_value = key_value[:, :, 1].astype(jnp.bfloat16)
    new_kv = jnp.stack([new_key, new_value], 2).reshape(requests, KVH * 2 * HD)
    group_size = HEADS // KVH
    token_pos = jnp.arange(MAXB)[:, None] * BLK + jnp.arange(BLK)[None, :]

    def attend(request_items):
        query_req, slot_row, length, key_req, value_req = request_items
        blocks = kv_cache[slot_row]
        query_wide = query_req.reshape(KVH, group_size, HD).astype(jnp.float32)
        keys_wide = blocks[..., :HD].astype(jnp.float32)
        values_wide = blocks[..., HD:].astype(jnp.float32)
        scores = jnp.einsum('kgd,bktd->kgbt', query_wide, keys_wide) * SCORE_SCALE
        token_live = token_pos < length
        scores = jnp.where(token_live, scores, MASKED)
        block_max = lax.optimization_barrier(jnp.max(scores, axis=-1))
        weights = jnp.where(token_live, jnp.exp(scores - block_max[..., None]), 0.0).astype(jnp.bfloat16)
        weight_wide = weights.astype(jnp.float32)
        block_sum = lax.optimization_barrier(jnp.sum(weight_wide, axis=-1))
        block_out = jnp.einsum('kgbt,bktd->kgbd', weight_wide, values_wide)
        block_live = jnp.arange(MAXB) * BLK < length
        block_max = jnp.where(block_live, block_max, MASKED)
        self_score = lax.optimization_barrier(jnp.sum(query_wide * key_req.astype(jnp.float32)[:, None, :], -1)) * SCORE_SCALE
        overall = jnp.maximum(lax.optimization_barrier(jnp.max(block_max, axis=-1)), self_score)
        block_w = jnp.where(block_live, jnp.exp(block_max - overall[..., None]), 0.0)
        self_w = jnp.exp(self_score - overall)
        numerator = lax.optimization_barrier(jnp.sum(block_w[..., None] * block_out, axis=2)) + self_w[..., None] * value_req.astype(jnp.float32)[:, None, :]
        denominator = lax.optimization_barrier(jnp.sum(block_w * block_sum, axis=-1)) + self_w
        return (numerator / denominator[..., None]).reshape(HEADS * HD)
    attended = lax.map(attend, (queries, block_slot, lengths, new_key, new_value))
    mixed_rows = jnp.dot(attended.astype(jnp.bfloat16), w_out, preferred_element_type=jnp.float32)
    layer_out = hidden + RESIDUAL_SCALE * mixed_rows
    return (layer_out, new_kv)
```

```python
import jax
import jax.numpy as jnp
from jax import lax
from jax.experimental import pallas as pl
from jax.experimental.pallas import tpu as pltpu
from jax.sharding import PartitionSpec as P

EPSILON = 1e-05
RESIDUAL_SCALE = 0.22
SCORE_SCALE = 0.015625
ROPE_BASE = 10000000.0
MASKED = -1e30

F32 = jnp.float32
BF16 = jnp.bfloat16
VMEM = pl.BlockSpec(memory_space=pltpu.VMEM)
SMEM = pl.BlockSpec(memory_space=pltpu.SMEM)


def lanes(shape):
    return lax.broadcasted_iota(jnp.int32, shape, len(shape) - 1)


def rows_of(shape):
    return lax.broadcasted_iota(jnp.int32, shape, 0)


def rope(x, cosine, sine, half):
    wide = x.shape[-1]
    ahead = pltpu.roll(x, wide - half, 1)
    behind = pltpu.roll(x, half, 1)
    first = lanes(x.shape) % (2 * half) < half
    return x * cosine + jnp.where(first, ahead, behind) * sine


def table_kernel(slots_here, block_len, base_ref, lengths_ref, slot_ref, out_ref):
    requests, blocks = slot_ref.shape
    base = base_ref[0]
    sub = lax.broadcasted_iota(jnp.int32, (8, blocks), 0)
    lane = lax.broadcasted_iota(jnp.int32, (8, blocks), 1)
    wanted, payload = [], []
    for v in range(requests // 8):
        length = jnp.zeros((8, blocks), jnp.int32)
        for i in range(8):
            length = jnp.where(sub == i, lengths_ref[8 * v + i], length)
        limit = length - lane * block_len
        here = slot_ref[pl.ds(8 * v, 8), :] - base
        wanted.append(jnp.where(limit > 0, here, -1))
        payload.append((sub + 8 * v) * 256 + jnp.minimum(limit, block_len))
    for tile in range(slots_here // 8):
        picked = jnp.zeros((8, blocks), jnp.int32)
        for i in range(8):
            found = jnp.zeros((8, blocks), jnp.int32)
            for w, p in zip(wanted, payload):
                found = jnp.where(w == 8 * tile + i, p, found)
            picked = jnp.where(sub == i, jnp.max(found, axis=0, keepdims=True), picked)
        out_ref[pl.ds(8 * tile, 8), :] = jnp.broadcast_to(
            jnp.max(picked.astype(F32), axis=1, keepdims=True), (8, blocks)
        ).astype(jnp.int32)


def normalise(rows_ref, gain_ref):
    chunks, wide = rows_ref.shape
    x = rows_ref[...]
    total = jnp.sum(jnp.sum(x * x, axis=1, keepdims=True), axis=0, keepdims=True)
    scale = lax.rsqrt(total * (1.0 / (chunks * wide)) + EPSILON)
    return (x * scale * gain_ref[...]).astype(BF16)


def project(normed, weight_ref):
    chunks, wide = normed.shape
    out = jnp.zeros((chunks, weight_ref.shape[1]), F32)
    row = rows_of(out.shape)
    for j in range(chunks):
        part = jnp.dot(
            normed, weight_ref[pl.ds(j * wide, wide), :], preferred_element_type=F32
        )
        out = out + jnp.where(row == j, part, 0.0)
    return jnp.sum(out, axis=0, keepdims=True)


def query_kernel(half, rows_ref, gain_ref, w_ref, cos_ref, sin_ref, out_ref, normed_ref):
    normed = normalise(rows_ref, gain_ref)
    normed_ref[...] = normed
    query = jnp.broadcast_to(project(normed, w_ref), (8, w_ref.shape[1]))
    query = rope(query, cos_ref[...], sin_ref[...], half).astype(BF16).astype(F32)
    for v in range(out_ref.shape[0] // 8):
        out_ref[pl.ds(8 * v, 8), :] = query


def keyval_kernel(
    half, normed_ref, w_ref, cos_ref, sin_ref, query_ref, kv_ref, self_ref, value_ref
):
    head_dim = 2 * half
    keyval = jnp.broadcast_to(project(normed_ref[...], w_ref), (8, w_ref.shape[1]))
    wide = keyval.shape[-1]
    turned = rope(keyval, cos_ref[:, :wide], sin_ref[:, :wide], half)
    is_key = lanes(keyval.shape) < head_dim
    both = jnp.where(is_key, turned, keyval).astype(BF16)
    kv_ref[...] = both[:1]
    both = both.astype(F32)
    swapped = pltpu.roll(both, head_dim, 1)
    key = jnp.where(is_key, both, swapped)
    value = jnp.where(is_key, swapped, both)
    for c in range(self_ref.shape[1] // wide):
        product = query_ref[:8, pl.ds(c * wide, wide)] * key
        low = jnp.sum(jnp.where(is_key, product, 0.0), axis=1, keepdims=True)
        high = jnp.sum(jnp.where(is_key, 0.0, product), axis=1, keepdims=True)
        self_ref[:, pl.ds(c * wide, wide)] = jnp.where(is_key, low, high) * SCORE_SCALE
        value_ref[:, pl.ds(c * wide, wide)] = value


def attend_kernel(
    head_dim, tab_ref, query_ref, kv_ref, out_ref, q_s, score_s, max_s, sum_s, acc_s
):
    slots_here, block_len, wide = kv_ref.shape
    requests = query_ref.shape[0]
    groups = query_ref.shape[1] // head_dim
    is_key = lanes((requests, wide)) < head_dim
    q_s[...] = jnp.zeros_like(q_s)
    for h in range(groups):
        chunk = query_ref[:, pl.ds((h // 2) * wide, wide)]
        if h % 2:
            chunk = pltpu.roll(chunk, head_dim, 1)
        q_s[:, h, :] = jnp.where(is_key, chunk, 0.0)
    max_s[...] = jnp.full_like(max_s, MASKED)
    sum_s[...] = jnp.zeros_like(sum_s)
    acc_s[...] = jnp.zeros_like(acc_s)
    token = lanes((8, block_len))
    step = 8

    def score(i, carry):
        for u in range(step):
            s = i * step + u
            entry = tab_ref[s]
            r = entry // 256
            limit = entry % 256
            q = q_s[r].astype(BF16)
            scores = lax.dot_general(
                q, kv_ref[s], (((1,), (1,)), ((), ())), preferred_element_type=F32
            )
            scores = jnp.where(token < limit, scores * SCORE_SCALE, MASKED)
            score_s[s] = scores
            top = jnp.broadcast_to(jnp.max(scores, axis=1, keepdims=True), scores.shape)
            max_s[r] = jnp.maximum(max_s[r], top)
        return carry

    lax.fori_loop(0, slots_here // step, score, 0)

    def gather(i, carry):
        for u in range(step):
            s = i * step + u
            entry = tab_ref[s]
            r = entry // 256
            limit = entry % 256
            weight = jnp.where(token < limit, jnp.exp(score_s[s] - max_s[r]), 0.0).astype(BF16)
            out = jnp.dot(weight, kv_ref[s], preferred_element_type=F32)
            total = jnp.sum(weight.astype(F32), axis=1, keepdims=True)
            acc_s[r] = acc_s[r] + out
            sum_s[r] = sum_s[r] + jnp.broadcast_to(total, out.shape)
        return carry

    lax.fori_loop(0, slots_here // step, gather, 0)

    for c in range(groups // 2):
        low = pltpu.roll(acc_s[:, 2 * c, :], head_dim, 1)
        out_ref[:, pl.ds(c * wide, wide)] = jnp.where(is_key, low, acc_s[:, 2 * c + 1, :])
    tail = jnp.zeros((requests, wide), F32)
    lane = lanes((requests, wide))
    for h in range(groups):
        tail = jnp.where(lane == h, max_s[:, h, :], tail)
        tail = jnp.where(lane == groups + h, sum_s[:, h, :], tail)
    out_ref[:, pl.ds(groups // 2 * wide, wide)] = tail


def combine_kernel(head_dim, got_ref, self_ref, value_ref, w_ref, out_ref):
    wide = 2 * head_dim
    parts = got_ref.shape[0]
    inner = self_ref.shape[1]
    groups = inner // head_dim
    tail = got_ref[:, pl.ds(inner, wide)]
    is_low = lanes((parts, wide)) < head_dim
    attended = []
    for c in range(inner // wide):
        here = pl.ds(c * wide, wide)
        tops = jnp.where(is_low, tail[:, 2 * c : 2 * c + 1], tail[:, 2 * c + 1 : 2 * c + 2])
        at = groups + 2 * c
        sums = jnp.where(is_low, tail[:, at : at + 1], tail[:, at + 1 : at + 2])
        own = self_ref[:1, here]
        overall = jnp.maximum(jnp.max(tops, axis=0, keepdims=True), own)
        weight = jnp.exp(tops - overall)
        own_weight = jnp.exp(own - overall)
        numerator = jnp.sum(weight * got_ref[:, here], axis=0, keepdims=True)
        denominator = jnp.sum(weight * sums, axis=0, keepdims=True)
        numerator = numerator + own_weight * value_ref[:1, here]
        attended.append(numerator / (denominator + own_weight))
    row = jnp.broadcast_to(jnp.concatenate(attended, axis=1), (8, inner)).astype(BF16)
    chunks, step = out_ref.shape
    for j in range(chunks):
        part = jnp.dot(row, w_ref[:, pl.ds(j * step, step)], preferred_element_type=F32)
        out_ref[pl.ds(j, 1), :] = part[:1]


def per_device(hidden, norm_gain, w_query, w_keyval, w_out, kv_cache, block_slot, lengths):
    slots_here, _, block_len, wide = kv_cache.shape
    head_dim = wide // 2
    half = head_dim // 2
    inner = w_query.shape[1]
    groups = inner // head_dim
    requests = block_slot.shape[0]
    shards = lax.axis_size("mp")
    features = hidden.shape[1]
    pool_index = lax.axis_index("pool")

    rows = lax.all_to_all(
        jnp.broadcast_to(hidden, (shards, features)), "mp", split_axis=0, concat_axis=0, tiled=True
    )

    position = lax.dynamic_slice_in_dim(lengths, pool_index, 1).astype(F32)
    lane = jnp.arange(inner, dtype=jnp.int32) % head_dim
    inverse = ROPE_BASE ** (-(lane % half).astype(F32) * 2.0 / head_dim)
    angle = (position[0] * inverse)[None, :]
    cosine = jnp.cos(angle)
    sine = jnp.where(lane[None, :] < half, -jnp.sin(angle), jnp.sin(angle))

    table = pl.pallas_call(
        lambda *refs: table_kernel(slots_here, block_len, *refs),
        out_shape=jax.ShapeDtypeStruct((slots_here, block_slot.shape[1]), jnp.int32),
        in_specs=[SMEM, SMEM, VMEM],
        out_specs=VMEM,
        name="slot_table",
    )((pool_index * slots_here).reshape(1).astype(jnp.int32), lengths, block_slot)[:, 0]

    query, normed = pl.pallas_call(
        lambda *refs: query_kernel(half, *refs),
        out_shape=(
            jax.ShapeDtypeStruct((requests, inner), F32),
            jax.ShapeDtypeStruct((shards, features), BF16),
        ),
        in_specs=[VMEM] * 5,
        out_specs=(VMEM, VMEM),
        name="query",
    )(rows, norm_gain.reshape(shards, features), w_query, cosine, sine)

    all_queries = lax.all_to_all(query, "pool", split_axis=0, concat_axis=0, tiled=True)

    new_kv, own_score, own_value = pl.pallas_call(
        lambda *refs: keyval_kernel(half, *refs),
        out_shape=(
            jax.ShapeDtypeStruct((1, wide), BF16),
            jax.ShapeDtypeStruct((8, inner), F32),
            jax.ShapeDtypeStruct((8, inner), F32),
        ),
        in_specs=[VMEM] * 5,
        out_specs=(VMEM, VMEM, VMEM),
        name="keyval",
    )(normed, w_keyval, cosine, sine, query)

    per_request = (requests, 8, wide)
    partial = pl.pallas_call(
        lambda *refs: attend_kernel(head_dim, *refs),
        out_shape=jax.ShapeDtypeStruct((requests, inner + wide), F32),
        in_specs=[SMEM, VMEM, VMEM],
        out_specs=VMEM,
        scratch_shapes=[
            pltpu.VMEM(per_request, F32),
            pltpu.VMEM((slots_here, 8, block_len), F32),
            pltpu.VMEM(per_request, F32),
            pltpu.VMEM(per_request, F32),
            pltpu.VMEM(per_request, F32),
        ],
        name="attend",
    )(table, all_queries, kv_cache.reshape(slots_here, block_len, wide))

    got = lax.all_to_all(partial, "pool", split_axis=0, concat_axis=0, tiled=True)

    mixed = pl.pallas_call(
        lambda *refs: combine_kernel(head_dim, *refs),
        out_shape=jax.ShapeDtypeStruct((shards, features), F32),
        in_specs=[VMEM] * 4,
        out_specs=VMEM,
        name="combine",
    )(got, own_score, own_value, w_out)

    spread = lax.all_to_all(mixed, "mp", split_axis=0, concat_axis=0, tiled=True)
    return (hidden + RESIDUAL_SCALE * jnp.sum(spread, axis=0, keepdims=True), new_kv)


def solution(mesh):
    return jax.shard_map(
        per_device,
        mesh=mesh,
        in_specs=(
            P("pool", "mp"),
            P(),
            P(None, "mp"),
            P(None, "mp"),
            P("mp", None),
            P("pool", "mp", None, None),
            P(),
            P(),
        ),
        out_specs=(P("pool", "mp"), P("pool", "mp")),
        check_vma=False,
    )
```

```python
import functools
import math

import jax
import jax.numpy as jnp
from jax import lax
from jax.experimental import pallas as pl
from jax.experimental.pallas import tpu as pltpu
from jax.sharding import PartitionSpec as P

EPSILON = 1e-05
RESIDUAL_SCALE = 0.22
SCORE_SCALE = 0.015625
ROPE_BASE = 10000000.0
MASKED = -1e30

F32 = jnp.float32
BF16 = jnp.bfloat16
VMEM = pl.BlockSpec(memory_space=pltpu.VMEM)
SMEM = pl.BlockSpec(memory_space=pltpu.SMEM)
HBM = pl.BlockSpec(memory_space=pltpu.HBM)

GROUP = 4


def far(x):
    return pltpu.with_memory_space_constraint(x, pltpu.HBM)


def lanes(shape):
    return lax.broadcasted_iota(jnp.int32, shape, len(shape) - 1)


def subs(shape):
    return lax.broadcasted_iota(jnp.int32, shape, len(shape) - 2)


def call(body, name, out_shape, in_specs, scratch=(), limit=4 << 20):
    many = isinstance(out_shape, tuple)
    return pl.pallas_call(
        body,
        out_shape=out_shape,
        in_specs=in_specs,
        out_specs=(VMEM,) * len(out_shape) if many else VMEM,
        scratch_shapes=list(scratch),
        compiler_params=pltpu.CompilerParams(vmem_limit_bytes=limit),
        name=name,
    )


def sine_cosine(angle):
    turn = jnp.floor(angle * (2.0 / math.pi) + 0.5)
    x = ((angle - turn * 1.5703125) - turn * 4.837512969970703e-4) - turn * 7.54978995489188e-8
    z = x * x
    sine = ((-1.9515295891e-4 * z + 8.3321608736e-3) * z - 1.6666654611e-1) * z * x + x
    cosine = ((2.443315711809948e-5 * z - 1.388731625493765e-3) * z + 4.166664568298827e-2) * z * z
    cosine = cosine - 0.5 * z + 1.0
    quadrant = turn.astype(jnp.int32) & 3
    odd = (quadrant & 1) == 1
    out_sine = jnp.where(odd, cosine, sine)
    out_cosine = jnp.where(odd, sine, cosine)
    out_sine = jnp.where(quadrant >= 2, -out_sine, out_sine)
    out_cosine = jnp.where((quadrant == 1) | (quadrant == 2), -out_cosine, out_cosine)
    return out_sine, out_cosine


def rotation(position, head_dim, width):
    half = head_dim // 2
    lane = lanes((8, width))
    pair = lane % half
    inverse = jnp.zeros((8, width), F32)
    for i in range(half):
        inverse = jnp.where(pair == i, ROPE_BASE ** (-2.0 * i / head_dim), inverse)
    sine, cosine = sine_cosine(position.astype(F32) * inverse)
    return cosine, jnp.where(lane % head_dim < half, -sine, sine)


def rope(x, cosine, sine, half):
    ahead = pltpu.roll(x, x.shape[1] - half, 1)
    behind = pltpu.roll(x, half, 1)
    first = lanes(x.shape) % (2 * half) < half
    return x * cosine + jnp.where(first, ahead, behind) * sine


def normalise(rows_ref, gain_ref):
    count = rows_ref.shape[0]
    x = rows_ref[...]
    total = jnp.sum(jnp.sum(x * x, axis=0, keepdims=True), axis=1, keepdims=True)
    scale = lax.rsqrt(total * (1.0 / x.size) + EPSILON)
    half = count // 2
    even = pl.ds(0, half, stride=2)
    odd = pl.ds(1, half, stride=2)
    left = rows_ref[even, :] * scale * gain_ref[even, :]
    right = rows_ref[odd, :] * scale * gain_ref[odd, :]
    return jnp.concatenate([left, right], axis=1)


def project(normed, weight_ref):
    chunks, wide = normed.shape
    row = subs(normed.shape)
    out = None
    for j in range(chunks):
        part = jnp.dot(
            jnp.where(row == j, normed, 0.0).astype(BF16),
            weight_ref[pl.ds(j * wide, wide), :],
            preferred_element_type=F32,
        )
        out = part if out is None else out + part
    return jnp.broadcast_to(jnp.sum(out, axis=0, keepdims=True), out.shape)


def fetch(sources, targets, sems):
    copies = [pltpu.make_async_copy(s, t, sems.at[i]) for i, (s, t) in enumerate(zip(sources, targets))]
    for copy in copies:
        copy.start()
    return copies


def prepare_kernel(
    head_dim, place_ref, lengths_ref, w_ref, gain_ref, held_w_ref, held_gain_ref, cos_ref, sin_ref, sems
):
    copies = fetch((w_ref, gain_ref), (held_w_ref, held_gain_ref), sems)
    cos_ref[...], sin_ref[...] = rotation(lengths_ref[place_ref[0]], head_dim, 2 * head_dim)
    for copy in copies:
        copy.wait()


def query_kernel(head_dim, rows_ref, gain_ref, w_ref, cos_ref, sin_ref, out_ref):
    wide = 2 * head_dim
    cosine, sine = cos_ref[...], sin_ref[...]
    query = project(normalise(rows_ref, gain_ref), w_ref)
    row = subs((8, wide)) % GROUP
    tile = jnp.zeros((8, wide), F32)
    for c in range(GROUP // 2):
        part = rope(query[:, c * wide : (c + 1) * wide], cosine, sine, head_dim // 2)
        tile = jnp.where(row == 2 * c, part, tile)
        tile = jnp.where(row == 2 * c + 1, pltpu.roll(part, head_dim, 1), tile)
    tile = tile.astype(BF16).astype(F32) * SCORE_SCALE
    tile = jnp.where(lanes(tile.shape) < head_dim, tile, 0.0)
    for v in range(out_ref.shape[0] // 8):
        out_ref[pl.ds(8 * v, 8), :] = tile


def keyval_kernel(head_dim, rows_ref, gain_ref, cos_ref, sin_ref, query_ref, w_ref, w_out_ref, *rest):
    kv_ref, own_ref, held_ref, near_ref, sems = rest
    copies = fetch((w_ref, w_out_ref), (near_ref, held_ref), sems)
    normed = normalise(rows_ref, gain_ref)
    copies[0].wait()
    keyval = project(normed, near_ref)
    is_key = lanes(keyval.shape) < head_dim
    turned = rope(keyval, cos_ref[...], sin_ref[...], head_dim // 2)
    both = jnp.where(is_key, turned, keyval).astype(BF16)
    kv_ref[...] = both[:1]
    both = both.astype(F32)
    score = jnp.sum(query_ref[:8, :] * both, axis=1, keepdims=True)
    own_ref[...] = jnp.where(is_key, score, both)
    copies[1].wait()


def table_kernel(
    slots_here, block_len, place_ref, lengths_ref, slot_ref, *rest
):
    kv_ref, out_ref, held_ref, sems = rest
    copies = fetch((kv_ref,), (held_ref,), sems)
    requests, blocks = slot_ref.shape
    base = place_ref[0] * slots_here
    sub = subs((8, blocks))
    lane = lanes((8, blocks))
    wanted, payload = [], []
    for v in range(requests // 8):
        length = jnp.zeros((8, blocks), jnp.int32)
        for i in range(8):
            length = jnp.where(sub == i, lengths_ref[8 * v + i], length)
        limit = length - lane * block_len
        here = slot_ref[pl.ds(8 * v, 8), :] - base
        wanted.append(jnp.where(limit > 0, here, -1))
        payload.append((sub + 8 * v) * 256 + jnp.minimum(limit, block_len))
    for tile in range(slots_here // 8):
        picked = jnp.zeros((8, blocks), jnp.int32)
        for i in range(8):
            found = jnp.zeros((8, blocks), jnp.int32)
            for w, p in zip(wanted, payload):
                found = jnp.where(w == 8 * tile + i, p, found)
            picked = jnp.where(sub == i, jnp.max(found, axis=0, keepdims=True), picked)
        out_ref[pl.ds(8 * tile, 8), :] = jnp.broadcast_to(
            jnp.max(picked.astype(F32), axis=1, keepdims=True), (8, blocks)
        ).astype(jnp.int32)
    for copy in copies:
        copy.wait()


def attend_kernel(tab_ref, query_ref, kv_ref, out_ref, q_s, score_s, max_s, sum_s, acc_s):
    slots_here, block_len, wide = kv_ref.shape
    requests = query_ref.shape[0] // GROUP
    low = subs((8, wide)) < GROUP
    token = lanes((8, block_len))
    lane = lanes((8, wide))
    for v in range(requests // 2):
        tile = query_ref[pl.ds(8 * v, 8), :]
        other = pltpu.roll(tile, GROUP, 0)
        q_s[2 * v] = jnp.where(low, tile, other)
        q_s[2 * v + 1] = jnp.where(low, other, tile)
    max_s[...] = jnp.full_like(max_s, MASKED)
    sum_s[...] = jnp.zeros_like(sum_s)
    acc_s[...] = jnp.zeros_like(acc_s)

    def pair(p):
        a, b = tab_ref[2 * p], tab_ref[2 * p + 1]
        live = token < jnp.where(low, a & 255, b & 255)
        keys = kv_ref[pl.ds(2 * p, 2)].reshape(2 * block_len, wide)
        return lax.shift_right_logical(a, 8), lax.shift_right_logical(b, 8), live, keys

    for p in range(slots_here // 2):
        ra, rb, live, keys = pair(p)
        query = jnp.where(low, q_s[ra], q_s[rb]).astype(BF16)
        scores = lax.dot_general(
            query, keys, (((1,), (1,)), ((), ())), preferred_element_type=F32
        )
        scores = jnp.where(low, scores[:, :block_len], scores[:, block_len:])
        scores = jnp.where(live, scores, MASKED)
        score_s[p] = scores
        top = jnp.broadcast_to(jnp.max(scores, axis=1, keepdims=True), scores.shape)
        max_s[ra] = jnp.maximum(max_s[ra], jnp.where(low, top, MASKED))
        max_s[rb] = jnp.maximum(max_s[rb], jnp.where(low, MASKED, top))

    for r in range(requests):
        top = max_s[r]
        max_s[r] = jnp.maximum(top, pltpu.roll(top, GROUP, 0))

    for p in range(slots_here // 2):
        ra, rb, live, values = pair(p)
        top = jnp.where(low, max_s[ra], max_s[rb])
        weight = jnp.where(live, jnp.exp(score_s[p] - top), 0.0).astype(BF16).astype(F32)
        both = jnp.concatenate(
            [jnp.where(low, weight, 0.0), jnp.where(low, 0.0, weight)], axis=1
        ).astype(BF16)
        out = jnp.dot(both, values, preferred_element_type=F32)
        total = jnp.broadcast_to(jnp.sum(weight, axis=1, keepdims=True), out.shape)
        acc_s[ra] = acc_s[ra] + jnp.where(low, out, 0.0)
        acc_s[rb] = acc_s[rb] + jnp.where(low, 0.0, out)
        sum_s[ra] = sum_s[ra] + jnp.where(low, total, 0.0)
        sum_s[rb] = sum_s[rb] + jnp.where(low, 0.0, total)

    for v in range(requests // 2):
        tiles = []
        for r in (2 * v, 2 * v + 1):
            out = acc_s[r] + pltpu.roll(acc_s[r], GROUP, 0)
            total = sum_s[r] + pltpu.roll(sum_s[r], GROUP, 0)
            tiles.append(
                jnp.where(lane < wide // 4, max_s[r], jnp.where(lane < wide // 2, total, out))
            )
        out_ref[pl.ds(8 * v, 8), :] = jnp.where(low, tiles[0], tiles[1])


def combine_kernel(got_ref, own_ref, w_ref, out_ref):
    rows, wide = got_ref.shape
    lane = lanes((8, wide))
    row = subs((8, wide))
    parts = [got_ref[pl.ds(8 * v, 8), :] for v in range(rows // 8)]
    top = parts[0]
    for part in parts[1:]:
        top = jnp.maximum(top, part)
    own = own_ref[...]
    top = jnp.maximum(jnp.maximum(top, pltpu.roll(top, GROUP, 0)), own)
    mixed = jnp.zeros((8, wide), F32)
    for part in parts:
        weight = jnp.exp(part - top)
        mixed = mixed + jnp.broadcast_to(weight[:, :1], part.shape) * part
    mixed = mixed + pltpu.roll(mixed, GROUP, 0)
    own_weight = jnp.exp(own - top)
    mixed = mixed + jnp.broadcast_to(own_weight[:, :1], own.shape) * jnp.where(
        lane < wide // 2, 1.0, own
    )
    attended = mixed / jnp.broadcast_to(mixed[:, wide // 4 : wide // 4 + 1], mixed.shape)
    swapped = pltpu.roll(attended, wide // 2, 1)
    placed = jnp.where(
        row % 2 == 0,
        jnp.where(lane < wide // 2, swapped, 0.0),
        jnp.where(lane < wide // 2, 0.0, attended),
    )
    chunks = [
        jnp.sum(jnp.where(row // 2 == c, placed, 0.0), axis=0, keepdims=True)
        for c in range(GROUP // 2)
    ]
    line = jnp.broadcast_to(jnp.concatenate(chunks, axis=1), (8, GROUP // 2 * wide)).astype(BF16)
    for v in range(out_ref.shape[0] // 8):
        part = jnp.dot(
            line, w_ref[:, pl.ds(8 * v * wide, 8 * wide)], preferred_element_type=F32
        )
        tile = jnp.zeros((8, wide), F32)
        for k in range(8):
            tile = jnp.where(row == k, part[:, k * wide : (k + 1) * wide], tile)
        out_ref[pl.ds(8 * v, 8), :] = tile


def exchange(x, axis, parts):
    shape = x.shape
    x = x.reshape(parts, shape[0] // parts, shape[1])
    return lax.all_to_all(x, axis, split_axis=0, concat_axis=0, tiled=True).reshape(shape)


def per_device(hidden, norm_gain, w_query, w_keyval, w_out, kv_cache, block_slot, lengths):
    slots_here, _, block_len, wide = kv_cache.shape
    head_dim = wide // 2
    requests = block_slot.shape[0]
    shards = lax.axis_size("mp")
    pools = lax.axis_size("pool")
    features = hidden.shape[1]
    lines = features // wide
    place = lax.axis_index("pool").astype(jnp.int32).reshape(1)
    rows = exchange(
        jnp.broadcast_to(hidden.reshape(1, lines, wide), (shards, lines, wide)).reshape(-1, wide),
        "mp",
        shards,
    )
    gain = norm_gain.reshape(shards * lines, wide)

    turn = jax.ShapeDtypeStruct((8, wide), F32)
    w_query, w_keyval, w_out, gain = (far(x) for x in (w_query, w_keyval, w_out, gain))
    held_query, held_gain, cosine, sine = call(
        functools.partial(prepare_kernel, head_dim),
        "prepare",
        (
            jax.ShapeDtypeStruct(w_query.shape, BF16),
            jax.ShapeDtypeStruct(gain.shape, F32),
            turn,
            turn,
        ),
        [SMEM, SMEM, HBM, HBM],
        [pltpu.SemaphoreType.DMA((2,))],
    )(place, lengths, w_query, gain)

    query = call(
        functools.partial(query_kernel, head_dim),
        "query",
        jax.ShapeDtypeStruct((requests * GROUP, wide), F32),
        [VMEM] * 5,
    )(rows, held_gain, held_query, cosine, sine)

    queries = exchange(query, "pool", pools)

    cache = far(kv_cache.reshape(slots_here, block_len, wide))
    table, held_cache = call(
        functools.partial(table_kernel, slots_here, block_len),
        "slot_table",
        (
            jax.ShapeDtypeStruct((slots_here, block_slot.shape[1]), jnp.int32),
            jax.ShapeDtypeStruct(cache.shape, BF16),
        ),
        [SMEM, SMEM, VMEM, HBM],
        [pltpu.SemaphoreType.DMA((1,))],
        limit=8 << 20,
    )(place, lengths, block_slot, cache)
    table = table[:, 0]

    new_kv, own, held_out = call(
        functools.partial(keyval_kernel, head_dim),
        "keyval",
        (
            jax.ShapeDtypeStruct((1, wide), BF16),
            turn,
            jax.ShapeDtypeStruct(w_out.shape, BF16),
        ),
        [VMEM] * 5 + [HBM] * 2,
        [pltpu.VMEM(w_keyval.shape, BF16), pltpu.SemaphoreType.DMA((2,))],
    )(rows, held_gain, cosine, sine, query, w_keyval, w_out)

    per_request = pltpu.VMEM((requests, 8, wide), F32)
    partial = call(
        attend_kernel,
        "attend",
        jax.ShapeDtypeStruct((requests * GROUP, wide), F32),
        [SMEM, VMEM, VMEM],
        [
            per_request,
            pltpu.VMEM((slots_here // 2, 8, block_len), F32),
            per_request,
            per_request,
            per_request,
        ],
        limit=12 << 20,
    )(table, queries, held_cache)

    got = exchange(partial, "pool", pools)

    mixed = call(
        combine_kernel,
        "combine",
        jax.ShapeDtypeStruct((shards * lines, wide), F32),
        [VMEM, VMEM, VMEM],
    )(got, own, held_out)

    spread = exchange(mixed, "mp", shards)
    total = jnp.sum(spread.reshape(shards, features), axis=0, keepdims=True)
    return (hidden + RESIDUAL_SCALE * total, new_kv)


def solution(mesh):
    return jax.shard_map(
        per_device,
        mesh=mesh,
        in_specs=(
            P("pool", "mp"),
            P(),
            P(None, "mp"),
            P(None, "mp"),
            P("mp", None),
            P("pool", "mp", None, None),
            P(),
            P(),
        ),
        out_specs=(P("pool", "mp"), P("pool", "mp")),
        check_vma=False,
    )
```

```python
import functools
import math

import jax
import jax.numpy as jnp
from jax import lax
from jax.experimental import pallas as pl
from jax.experimental.pallas import tpu as pltpu
from jax.sharding import PartitionSpec as P

EPSILON = 1e-05
RESIDUAL_SCALE = 0.22
SCORE_SCALE = 0.015625
ROPE_BASE = 10000000.0
MASKED = -1e30

F32 = jnp.float32
BF16 = jnp.bfloat16
VMEM = pl.BlockSpec(memory_space=pltpu.VMEM)
SMEM = pl.BlockSpec(memory_space=pltpu.SMEM)
HBM = pl.BlockSpec(memory_space=pltpu.HBM)

GROUP = 4


def far(x):
    return pltpu.with_memory_space_constraint(x, pltpu.HBM)


def lanes(shape):
    return lax.broadcasted_iota(jnp.int32, shape, len(shape) - 1)


def subs(shape):
    return lax.broadcasted_iota(jnp.int32, shape, len(shape) - 2)


def call(body, name, out_shape, in_specs, scratch=(), limit=4 << 20):
    many = isinstance(out_shape, tuple)
    return pl.pallas_call(
        body,
        out_shape=out_shape,
        in_specs=in_specs,
        out_specs=(VMEM,) * len(out_shape) if many else VMEM,
        scratch_shapes=list(scratch),
        compiler_params=pltpu.CompilerParams(vmem_limit_bytes=limit),
        name=name,
    )


def sine_cosine(angle):
    turn = jnp.floor(angle * (2.0 / math.pi) + 0.5)
    x = ((angle - turn * 1.5703125) - turn * 4.837512969970703e-4) - turn * 7.54978995489188e-8
    z = x * x
    sine = ((-1.9515295891e-4 * z + 8.3321608736e-3) * z - 1.6666654611e-1) * z * x + x
    cosine = ((2.443315711809948e-5 * z - 1.388731625493765e-3) * z + 4.166664568298827e-2) * z * z
    cosine = cosine - 0.5 * z + 1.0
    quadrant = turn.astype(jnp.int32) & 3
    odd = (quadrant & 1) == 1
    out_sine = jnp.where(odd, cosine, sine)
    out_cosine = jnp.where(odd, sine, cosine)
    out_sine = jnp.where(quadrant >= 2, -out_sine, out_sine)
    out_cosine = jnp.where((quadrant == 1) | (quadrant == 2), -out_cosine, out_cosine)
    return out_sine, out_cosine


def rotation(position, head_dim, width):
    half = head_dim // 2
    lane = lanes((8, width))
    pair = lane % half
    inverse = jnp.zeros((8, width), F32)
    for i in range(half):
        inverse = jnp.where(pair == i, ROPE_BASE ** (-2.0 * i / head_dim), inverse)
    sine, cosine = sine_cosine(position.astype(F32) * inverse)
    return cosine, jnp.where(lane % head_dim < half, -sine, sine)


def rope(x, cosine, sine, half):
    ahead = pltpu.roll(x, x.shape[1] - half, 1)
    behind = pltpu.roll(x, half, 1)
    first = lanes(x.shape) % (2 * half) < half
    return x * cosine + jnp.where(first, ahead, behind) * sine


def normalise(rows_ref, gain_ref):
    count = rows_ref.shape[0]
    x = rows_ref[...]
    total = jnp.sum(jnp.sum(x * x, axis=0, keepdims=True), axis=1, keepdims=True)
    scale = lax.rsqrt(total * (1.0 / x.size) + EPSILON)
    half = count // 2
    even = pl.ds(0, half, stride=2)
    odd = pl.ds(1, half, stride=2)
    left = rows_ref[even, :] * scale * gain_ref[even, :]
    right = rows_ref[odd, :] * scale * gain_ref[odd, :]
    return jnp.concatenate([left, right], axis=1)


def project(normed, weight_ref):
    chunks, wide = normed.shape
    row = subs(normed.shape)
    out = None
    for j in range(chunks):
        part = jnp.dot(
            jnp.where(row == j, normed, 0.0).astype(BF16),
            weight_ref[pl.ds(j * wide, wide), :],
            preferred_element_type=F32,
        )
        out = part if out is None else out + part
    return jnp.broadcast_to(jnp.sum(out, axis=0, keepdims=True), out.shape)


def fetch(sources, targets, sems):
    copies = [pltpu.make_async_copy(s, t, sems.at[i]) for i, (s, t) in enumerate(zip(sources, targets))]
    for copy in copies:
        copy.start()
    return copies


def prepare_kernel(
    head_dim, place_ref, lengths_ref, w_ref, gain_ref, cache_ref, *rest
):
    held_w_ref, held_gain_ref, held_cache_ref, cos_ref, sin_ref, sems = rest
    first = cache_ref.at[pl.ds(0, held_cache_ref.shape[0])]
    copies = fetch((w_ref, gain_ref, first), (held_w_ref, held_gain_ref, held_cache_ref), sems)
    cos_ref[...], sin_ref[...] = rotation(lengths_ref[place_ref[0]], head_dim, 2 * head_dim)
    for copy in copies:
        copy.wait()


def query_kernel(head_dim, rows_ref, gain_ref, w_ref, cos_ref, sin_ref, out_ref):
    wide = 2 * head_dim
    cosine, sine = cos_ref[...], sin_ref[...]
    query = project(normalise(rows_ref, gain_ref), w_ref)
    row = subs((8, wide)) % GROUP
    tile = jnp.zeros((8, wide), F32)
    for c in range(GROUP // 2):
        part = rope(query[:, c * wide : (c + 1) * wide], cosine, sine, head_dim // 2)
        tile = jnp.where(row == 2 * c, part, tile)
        tile = jnp.where(row == 2 * c + 1, pltpu.roll(part, head_dim, 1), tile)
    tile = tile.astype(BF16).astype(F32) * SCORE_SCALE
    tile = jnp.where(lanes(tile.shape) < head_dim, tile, 0.0).astype(BF16)
    for v in range(out_ref.shape[0] // 8):
        out_ref[pl.ds(8 * v, 8), :] = tile


def keyval_kernel(
    head_dim, rows_ref, gain_ref, cos_ref, sin_ref, query_ref, w_ref, kv_ref, own_ref
):
    keyval = project(normalise(rows_ref, gain_ref), w_ref)
    is_key = lanes(keyval.shape) < head_dim
    turned = rope(keyval, cos_ref[...], sin_ref[...], head_dim // 2)
    both = jnp.where(is_key, turned, keyval).astype(BF16)
    kv_ref[...] = both[:1]
    both = both.astype(F32)
    score = jnp.sum(query_ref[:8, :].astype(F32) * both, axis=1, keepdims=True)
    own_ref[...] = jnp.where(is_key, score, both)


def table_kernel(
    slots_here, block_len, place_ref, lengths_ref, slot_ref, cache_ref, out_ref, held_ref, sems
):
    count = held_ref.shape[0]
    copies = fetch((cache_ref.at[pl.ds(slots_here - count, count)],), (held_ref,), sems)
    requests, blocks = slot_ref.shape
    base = place_ref[0] * slots_here
    sub = subs((8, blocks))
    lane = lanes((8, blocks))
    wanted, payload = [], []
    for v in range(requests // 8):
        length = jnp.zeros((8, blocks), jnp.int32)
        for i in range(8):
            length = jnp.where(sub == i, lengths_ref[8 * v + i], length)
        limit = length - lane * block_len
        here = slot_ref[pl.ds(8 * v, 8), :] - base
        wanted.append(jnp.where(limit > 0, here, -1))
        payload.append((sub + 8 * v) * 256 + jnp.minimum(limit, block_len))
    for tile in range(slots_here // 8):
        picked = jnp.zeros((8, blocks), jnp.int32)
        for i in range(8):
            found = jnp.zeros((8, blocks), jnp.int32)
            for w, p in zip(wanted, payload):
                found = jnp.where(w == 8 * tile + i, p, found)
            picked = jnp.where(sub == i, jnp.max(found, axis=0, keepdims=True), picked)
        out_ref[pl.ds(8 * tile, 8), :] = jnp.broadcast_to(
            jnp.max(picked.astype(F32), axis=1, keepdims=True), (8, blocks)
        ).astype(jnp.int32)
    copies[0].wait()


def attend_kernel(
    tab_ref, query_ref, first_ref, second_ref, w_ref, out_ref, held_ref, q_s, score_s, max_s, sum_s, acc_s, sems
):
    copies = fetch((w_ref,), (held_ref,), sems)
    half, block_len, wide = first_ref.shape
    slots_here = 2 * half
    requests = query_ref.shape[0] // GROUP
    low = subs((8, wide)) < GROUP
    token = lanes((8, block_len))
    lane = lanes((8, wide))
    for v in range(requests // 2):
        tile = query_ref[pl.ds(8 * v, 8), :].astype(F32)
        other = pltpu.roll(tile, GROUP, 0)
        q_s[2 * v] = jnp.where(low, tile, other)
        q_s[2 * v + 1] = jnp.where(low, other, tile)
    max_s[...] = jnp.full_like(max_s, MASKED)
    sum_s[...] = jnp.zeros_like(sum_s)
    acc_s[...] = jnp.zeros_like(acc_s)

    def pair(p):
        a, b = tab_ref[2 * p], tab_ref[2 * p + 1]
        live = token < jnp.where(low, a & 255, b & 255)
        held, at = (first_ref, 2 * p) if 2 * p < half else (second_ref, 2 * p - half)
        keys = held[pl.ds(at, 2)].reshape(2 * block_len, wide)
        return lax.shift_right_logical(a, 8), lax.shift_right_logical(b, 8), live, keys

    for p in range(slots_here // 2):
        ra, rb, live, keys = pair(p)
        query = jnp.where(low, q_s[ra], q_s[rb]).astype(BF16)
        scores = lax.dot_general(
            query, keys, (((1,), (1,)), ((), ())), preferred_element_type=F32
        )
        scores = jnp.where(low, scores[:, :block_len], scores[:, block_len:])
        scores = jnp.where(live, scores, MASKED)
        score_s[p] = scores
        top = jnp.broadcast_to(jnp.max(scores, axis=1, keepdims=True), scores.shape)
        max_s[ra] = jnp.maximum(max_s[ra], jnp.where(low, top, MASKED))
        max_s[rb] = jnp.maximum(max_s[rb], jnp.where(low, MASKED, top))

    for r in range(requests):
        top = max_s[r]
        max_s[r] = jnp.maximum(top, pltpu.roll(top, GROUP, 0))

    for p in range(slots_here // 2):
        ra, rb, live, values = pair(p)
        top = jnp.where(low, max_s[ra], max_s[rb])
        weight = jnp.where(live, jnp.exp(score_s[p] - top), 0.0).astype(BF16).astype(F32)
        both = jnp.concatenate(
            [jnp.where(low, weight, 0.0), jnp.where(low, 0.0, weight)], axis=1
        ).astype(BF16)
        out = jnp.dot(both, values, preferred_element_type=F32)
        total = jnp.broadcast_to(jnp.sum(weight, axis=1, keepdims=True), out.shape)
        acc_s[ra] = acc_s[ra] + jnp.where(low, out, 0.0)
        acc_s[rb] = acc_s[rb] + jnp.where(low, 0.0, out)
        sum_s[ra] = sum_s[ra] + jnp.where(low, total, 0.0)
        sum_s[rb] = sum_s[rb] + jnp.where(low, 0.0, total)

    for v in range(requests // 2):
        tiles = []
        for r in (2 * v, 2 * v + 1):
            out = acc_s[r] + pltpu.roll(acc_s[r], GROUP, 0)
            total = sum_s[r] + pltpu.roll(sum_s[r], GROUP, 0)
            tiles.append(
                jnp.where(lane < wide // 4, max_s[r], jnp.where(lane < wide // 2, total, out))
            )
        out_ref[pl.ds(8 * v, 8), :] = jnp.where(low, tiles[0], tiles[1])
    copies[0].wait()


def combine_kernel(got_ref, own_ref, w_ref, out_ref):
    rows, wide = got_ref.shape
    lane = lanes((8, wide))
    row = subs((8, wide))
    parts = [got_ref[pl.ds(8 * v, 8), :] for v in range(rows // 8)]
    top = parts[0]
    for part in parts[1:]:
        top = jnp.maximum(top, part)
    own = own_ref[...]
    top = jnp.maximum(jnp.maximum(top, pltpu.roll(top, GROUP, 0)), own)
    mixed = jnp.zeros((8, wide), F32)
    for part in parts:
        weight = jnp.exp(part - top)
        mixed = mixed + jnp.broadcast_to(weight[:, :1], part.shape) * part
    mixed = mixed + pltpu.roll(mixed, GROUP, 0)
    own_weight = jnp.exp(own - top)
    mixed = mixed + jnp.broadcast_to(own_weight[:, :1], own.shape) * jnp.where(
        lane < wide // 2, 1.0, own
    )
    attended = mixed / jnp.broadcast_to(mixed[:, wide // 4 : wide // 4 + 1], mixed.shape)
    swapped = pltpu.roll(attended, wide // 2, 1)
    placed = jnp.where(
        row % 2 == 0,
        jnp.where(lane < wide // 2, swapped, 0.0),
        jnp.where(lane < wide // 2, 0.0, attended),
    )
    chunks = [
        jnp.sum(jnp.where(row // 2 == c, placed, 0.0), axis=0, keepdims=True)
        for c in range(GROUP // 2)
    ]
    line = jnp.broadcast_to(jnp.concatenate(chunks, axis=1), (8, GROUP // 2 * wide)).astype(BF16)
    for v in range(out_ref.shape[0] // 8):
        part = jnp.dot(
            line, w_ref[:, pl.ds(8 * v * wide, 8 * wide)], preferred_element_type=F32
        )
        tile = jnp.zeros((8, wide), F32)
        for k in range(8):
            tile = jnp.where(row == k, part[:, k * wide : (k + 1) * wide], tile)
        out_ref[pl.ds(8 * v, 8), :] = tile


def exchange(x, axis, parts):
    shape = x.shape
    x = x.reshape(parts, shape[0] // parts, shape[1])
    return lax.all_to_all(x, axis, split_axis=0, concat_axis=0, tiled=True).reshape(shape)


def per_device(hidden, norm_gain, w_query, w_keyval, w_out, kv_cache, block_slot, lengths):
    slots_here, _, block_len, wide = kv_cache.shape
    head_dim = wide // 2
    requests = block_slot.shape[0]
    shards = lax.axis_size("mp")
    pools = lax.axis_size("pool")
    features = hidden.shape[1]
    lines = features // wide
    place = lax.axis_index("pool").astype(jnp.int32).reshape(1)
    rows = exchange(
        jnp.broadcast_to(hidden.reshape(1, lines, wide), (shards, lines, wide)).reshape(-1, wide),
        "mp",
        shards,
    )
    gain = norm_gain.reshape(shards * lines, wide)

    turn = jax.ShapeDtypeStruct((8, wide), F32)
    w_query, w_keyval, w_out, gain = (far(x) for x in (w_query, w_keyval, w_out, gain))
    cache = far(kv_cache.reshape(slots_here, block_len, wide))
    lengths, block_slot = far(lengths), far(block_slot)
    half_cache = jax.ShapeDtypeStruct((slots_here // 2, block_len, wide), BF16)
    held_query, held_gain, first_cache, cosine, sine = call(
        functools.partial(prepare_kernel, head_dim),
        "prepare",
        (
            jax.ShapeDtypeStruct(w_query.shape, BF16),
            jax.ShapeDtypeStruct(gain.shape, F32),
            half_cache,
            turn,
            turn,
        ),
        [SMEM, SMEM, HBM, HBM, HBM],
        [pltpu.SemaphoreType.DMA((3,))],
        limit=8 << 20,
    )(place, lengths, w_query, gain, cache)

    query = call(
        functools.partial(query_kernel, head_dim),
        "query",
        jax.ShapeDtypeStruct((requests * GROUP, wide), BF16),
        [VMEM] * 5,
    )(rows, held_gain, held_query, cosine, sine)

    queries = exchange(query, "pool", pools)

    table, second_cache = call(
        functools.partial(table_kernel, slots_here, block_len),
        "slot_table",
        (jax.ShapeDtypeStruct((slots_here, block_slot.shape[1]), jnp.int32), half_cache),
        [SMEM, SMEM, VMEM, HBM],
        [pltpu.SemaphoreType.DMA((1,))],
    )(place, lengths, block_slot, cache)
    table = table[:, 0]

    new_kv, own = call(
        functools.partial(keyval_kernel, head_dim),
        "keyval",
        (jax.ShapeDtypeStruct((1, wide), BF16), turn),
        [VMEM] * 6,
    )(rows, held_gain, cosine, sine, query, w_keyval)
    table, own = lax.optimization_barrier((table, own))

    per_request = pltpu.VMEM((requests, 8, wide), F32)
    partial, held_out = call(
        attend_kernel,
        "attend",
        (
            jax.ShapeDtypeStruct((requests * GROUP, wide), F32),
            jax.ShapeDtypeStruct(w_out.shape, BF16),
        ),
        [SMEM, VMEM, VMEM, VMEM, HBM],
        [
            per_request,
            pltpu.VMEM((slots_here // 2, 8, block_len), F32),
            per_request,
            per_request,
            per_request,
            pltpu.SemaphoreType.DMA((1,)),
        ],
        limit=12 << 20,
    )(table, queries, first_cache, second_cache, w_out)

    got = exchange(partial, "pool", pools)

    mixed = call(
        combine_kernel,
        "combine",
        jax.ShapeDtypeStruct((shards * lines, wide), F32),
        [VMEM, VMEM, VMEM],
    )(got, own, held_out)

    spread = exchange(mixed, "mp", shards)
    total = jnp.sum(spread.reshape(shards, features), axis=0, keepdims=True)
    return (hidden + RESIDUAL_SCALE * total, new_kv)


def solution(mesh):
    return jax.shard_map(
        per_device,
        mesh=mesh,
        in_specs=(
            P("pool", "mp"),
            P(),
            P(None, "mp"),
            P(None, "mp"),
            P("mp", None),
            P("pool", "mp", None, None),
            P(),
            P(),
        ),
        out_specs=(P("pool", "mp"), P("pool", "mp")),
        check_vma=False,
    )
```

```python
import functools
import math

import jax
import jax.numpy as jnp
from jax import lax
from jax.experimental import pallas as pl
from jax.experimental.pallas import tpu as pltpu
from jax.sharding import PartitionSpec as P

EPSILON = 1e-05
RESIDUAL_SCALE = 0.22
SCORE_SCALE = 0.015625
ROPE_BASE = 10000000.0
MASKED = -1e30

F32 = jnp.float32
BF16 = jnp.bfloat16
VMEM = pl.BlockSpec(memory_space=pltpu.VMEM)
SMEM = pl.BlockSpec(memory_space=pltpu.SMEM)
HBM = pl.BlockSpec(memory_space=pltpu.HBM)

GROUP = 4

FIRST = 44


def far(x):
    return pltpu.with_memory_space_constraint(x, pltpu.HBM)


def lanes(shape):
    return lax.broadcasted_iota(jnp.int32, shape, len(shape) - 1)


def subs(shape):
    return lax.broadcasted_iota(jnp.int32, shape, len(shape) - 2)


def call(body, name, out_shape, in_specs, scratch=(), limit=4 << 20):
    many = isinstance(out_shape, tuple)
    return pl.pallas_call(
        body,
        out_shape=out_shape,
        in_specs=in_specs,
        out_specs=(VMEM,) * len(out_shape) if many else VMEM,
        scratch_shapes=list(scratch),
        compiler_params=pltpu.CompilerParams(vmem_limit_bytes=limit),
        name=name,
    )


def sine_cosine(angle):
    turn = jnp.floor(angle * (2.0 / math.pi) + 0.5)
    x = ((angle - turn * 1.5703125) - turn * 4.837512969970703e-4) - turn * 7.54978995489188e-8
    z = x * x
    sine = ((-1.9515295891e-4 * z + 8.3321608736e-3) * z - 1.6666654611e-1) * z * x + x
    cosine = ((2.443315711809948e-5 * z - 1.388731625493765e-3) * z + 4.166664568298827e-2) * z * z
    cosine = cosine - 0.5 * z + 1.0
    quadrant = turn.astype(jnp.int32) & 3
    odd = (quadrant & 1) == 1
    out_sine = jnp.where(odd, cosine, sine)
    out_cosine = jnp.where(odd, sine, cosine)
    out_sine = jnp.where(quadrant >= 2, -out_sine, out_sine)
    out_cosine = jnp.where((quadrant == 1) | (quadrant == 2), -out_cosine, out_cosine)
    return out_sine, out_cosine


def rotation(position, head_dim, width):
    half = head_dim // 2
    lane = lanes((8, width))
    pair = lane % half
    inverse = jnp.zeros((8, width), F32)
    for i in range(half):
        inverse = jnp.where(pair == i, ROPE_BASE ** (-2.0 * i / head_dim), inverse)
    sine, cosine = sine_cosine(position.astype(F32) * inverse)
    return cosine, jnp.where(lane % head_dim < half, -sine, sine)


def rope(x, cosine, sine, half):
    ahead = pltpu.roll(x, x.shape[1] - half, 1)
    behind = pltpu.roll(x, half, 1)
    first = lanes(x.shape) % (2 * half) < half
    return x * cosine + jnp.where(first, ahead, behind) * sine


def normalise(rows_ref, gain_ref):
    count = rows_ref.shape[0]
    x = rows_ref[...]
    total = jnp.sum(jnp.sum(x * x, axis=0, keepdims=True), axis=1, keepdims=True)
    scale = lax.rsqrt(total * (1.0 / x.size) + EPSILON)
    half = count // 2
    even = pl.ds(0, half, stride=2)
    odd = pl.ds(1, half, stride=2)
    left = rows_ref[even, :] * scale * gain_ref[even, :]
    right = rows_ref[odd, :] * scale * gain_ref[odd, :]
    return jnp.concatenate([left, right], axis=1)


def project(normed, weight_ref):
    chunks, wide = normed.shape
    row = subs(normed.shape)
    out = None
    for j in range(chunks):
        part = jnp.dot(
            jnp.where(row == j, normed, 0.0).astype(BF16),
            weight_ref[pl.ds(j * wide, wide), :],
            preferred_element_type=F32,
        )
        out = part if out is None else out + part
    return jnp.broadcast_to(jnp.sum(out, axis=0, keepdims=True), out.shape)


def fetch(sources, targets, sems):
    copies = [pltpu.make_async_copy(s, t, sems.at[i]) for i, (s, t) in enumerate(zip(sources, targets))]
    for copy in copies:
        copy.start()
    return copies


def prepare_kernel(
    head_dim, place_ref, lengths_ref, w_ref, gain_ref, cache_ref, *rest
):
    held_w_ref, held_gain_ref, held_cache_ref, cos_ref, sin_ref, sems = rest
    first = cache_ref.at[pl.ds(0, held_cache_ref.shape[0])]
    copies = fetch((w_ref, gain_ref, first), (held_w_ref, held_gain_ref, held_cache_ref), sems)
    cos_ref[...], sin_ref[...] = rotation(lengths_ref[place_ref[0]], head_dim, 2 * head_dim)
    for copy in copies:
        copy.wait()


def query_kernel(head_dim, rows_ref, gain_ref, w_ref, cos_ref, sin_ref, out_ref):
    wide = 2 * head_dim
    cosine, sine = cos_ref[...], sin_ref[...]
    query = project(normalise(rows_ref, gain_ref), w_ref)
    row = subs((8, wide)) % GROUP
    tile = jnp.zeros((8, wide), F32)
    for c in range(GROUP // 2):
        part = rope(query[:, c * wide : (c + 1) * wide], cosine, sine, head_dim // 2)
        tile = jnp.where(row == 2 * c, part, tile)
        tile = jnp.where(row == 2 * c + 1, pltpu.roll(part, head_dim, 1), tile)
    tile = tile.astype(BF16).astype(F32) * SCORE_SCALE
    tile = jnp.where(lanes(tile.shape) < head_dim, tile, 0.0).astype(BF16)
    for v in range(out_ref.shape[0] // 8):
        out_ref[pl.ds(8 * v, 8), :] = tile


def keyval_kernel(
    head_dim, rows_ref, gain_ref, cos_ref, sin_ref, query_ref, w_ref, kv_ref, own_ref
):
    keyval = project(normalise(rows_ref, gain_ref), w_ref)
    is_key = lanes(keyval.shape) < head_dim
    turned = rope(keyval, cos_ref[...], sin_ref[...], head_dim // 2)
    both = jnp.where(is_key, turned, keyval).astype(BF16)
    kv_ref[...] = both[:1]
    both = both.astype(F32)
    score = jnp.sum(query_ref[:8, :].astype(F32) * both, axis=1, keepdims=True)
    own_ref[...] = jnp.where(is_key, score, both)


def table_kernel(
    slots_here, block_len, place_ref, lengths_ref, slot_ref, cache_ref, out_ref, held_ref, sems
):
    count = held_ref.shape[0]
    copies = fetch((cache_ref.at[pl.ds(slots_here - count, count)],), (held_ref,), sems)
    requests, blocks = slot_ref.shape
    base = place_ref[0] * slots_here
    sub = subs((8, blocks))
    lane = lanes((8, blocks))
    wanted, payload = [], []
    for v in range(requests // 8):
        length = jnp.zeros((8, blocks), jnp.int32)
        for i in range(8):
            length = jnp.where(sub == i, lengths_ref[8 * v + i], length)
        limit = length - lane * block_len
        here = slot_ref[pl.ds(8 * v, 8), :] - base
        wanted.append(jnp.where(limit > 0, here, -1))
        payload.append(
            ((sub + 8 * v + requests - FIRST) % requests) * 256 + jnp.minimum(limit, block_len)
        )
    for tile in range(slots_here // 8):
        picked = jnp.zeros((8, blocks), jnp.int32)
        for i in range(8):
            found = jnp.zeros((8, blocks), jnp.int32)
            for w, p in zip(wanted, payload):
                found = jnp.where(w == 8 * tile + i, p, found)
            picked = jnp.where(sub == i, jnp.max(found, axis=0, keepdims=True), picked)
        out_ref[pl.ds(8 * tile, 8), :] = jnp.broadcast_to(
            jnp.max(picked.astype(F32), axis=1, keepdims=True), (8, blocks)
        ).astype(jnp.int32)
    copies[0].wait()


def attend_kernel(
    tab_ref, query_ref, first_ref, second_ref, w_ref, out_ref, held_ref, q_s, score_s, max_s, sum_s, acc_s, sems
):
    copies = fetch((w_ref,), (held_ref,), sems)
    half, block_len, wide = first_ref.shape
    slots_here = 2 * half
    requests = query_ref.shape[0] // GROUP
    low = subs((8, wide)) < GROUP
    token = lanes((8, block_len))
    lane = lanes((8, wide))
    for v in range(requests // 2):
        tile = query_ref[pl.ds(8 * v, 8), :].astype(F32)
        other = pltpu.roll(tile, GROUP, 0)
        q_s[2 * v] = jnp.where(low, tile, other)
        q_s[2 * v + 1] = jnp.where(low, other, tile)
    max_s[...] = jnp.full_like(max_s, MASKED)
    sum_s[...] = jnp.zeros_like(sum_s)
    acc_s[...] = jnp.zeros_like(acc_s)

    def pair(p):
        a, b = tab_ref[2 * p], tab_ref[2 * p + 1]
        live = token < jnp.where(low, a & 255, b & 255)
        held, at = (first_ref, 2 * p) if 2 * p < half else (second_ref, 2 * p - half)
        keys = held[pl.ds(at, 2)].reshape(2 * block_len, wide)
        return lax.shift_right_logical(a, 8), lax.shift_right_logical(b, 8), live, keys

    for p in range(slots_here // 2):
        ra, rb, live, keys = pair(p)
        query = jnp.where(low, q_s[ra], q_s[rb]).astype(BF16)
        scores = lax.dot_general(
            query, keys, (((1,), (1,)), ((), ())), preferred_element_type=F32
        )
        scores = jnp.where(low, scores[:, :block_len], scores[:, block_len:])
        scores = jnp.where(live, scores, MASKED)
        score_s[p] = scores
        top = jnp.broadcast_to(jnp.max(scores, axis=1, keepdims=True), scores.shape)
        max_s[ra] = jnp.maximum(max_s[ra], jnp.where(low, top, MASKED))
        max_s[rb] = jnp.maximum(max_s[rb], jnp.where(low, MASKED, top))

    for r in range(requests):
        top = max_s[r]
        max_s[r] = jnp.maximum(top, pltpu.roll(top, GROUP, 0))

    for p in range(slots_here // 2):
        ra, rb, live, values = pair(p)
        top = jnp.where(low, max_s[ra], max_s[rb])
        weight = jnp.where(live, jnp.exp(score_s[p] - top), 0.0).astype(BF16).astype(F32)
        both = jnp.concatenate(
            [jnp.where(low, weight, 0.0), jnp.where(low, 0.0, weight)], axis=1
        ).astype(BF16)
        out = jnp.dot(both, values, preferred_element_type=F32)
        total = jnp.broadcast_to(jnp.sum(weight, axis=1, keepdims=True), out.shape)
        acc_s[ra] = acc_s[ra] + jnp.where(low, out, 0.0)
        acc_s[rb] = acc_s[rb] + jnp.where(low, 0.0, out)
        sum_s[ra] = sum_s[ra] + jnp.where(low, total, 0.0)
        sum_s[rb] = sum_s[rb] + jnp.where(low, 0.0, total)

    for v in range(requests // 2):
        tiles = []
        for r in (2 * v, 2 * v + 1):
            out = acc_s[r] + pltpu.roll(acc_s[r], GROUP, 0)
            total = sum_s[r] + pltpu.roll(sum_s[r], GROUP, 0)
            tiles.append(
                jnp.where(lane < wide // 4, max_s[r], jnp.where(lane < wide // 2, total, out))
            )
        out_ref[pl.ds(8 * v, 8), :] = jnp.where(low, tiles[0], tiles[1])
    copies[0].wait()


def combine_kernel(got_ref, own_ref, w_ref, out_ref):
    rows, wide = got_ref.shape
    lane = lanes((8, wide))
    row = subs((8, wide))
    parts = [got_ref[pl.ds(8 * v, 8), :] for v in range(rows // 8)]
    top = parts[0]
    for part in parts[1:]:
        top = jnp.maximum(top, part)
    own = own_ref[...]
    top = jnp.maximum(jnp.maximum(top, pltpu.roll(top, GROUP, 0)), own)
    mixed = jnp.zeros((8, wide), F32)
    for part in parts:
        weight = jnp.exp(part - top)
        mixed = mixed + jnp.broadcast_to(weight[:, :1], part.shape) * part
    mixed = mixed + pltpu.roll(mixed, GROUP, 0)
    own_weight = jnp.exp(own - top)
    mixed = mixed + jnp.broadcast_to(own_weight[:, :1], own.shape) * jnp.where(
        lane < wide // 2, 1.0, own
    )
    attended = mixed / jnp.broadcast_to(mixed[:, wide // 4 : wide // 4 + 1], mixed.shape)
    swapped = pltpu.roll(attended, wide // 2, 1)
    placed = jnp.where(
        row % 2 == 0,
        jnp.where(lane < wide // 2, swapped, 0.0),
        jnp.where(lane < wide // 2, 0.0, attended),
    )
    chunks = [
        jnp.sum(jnp.where(row // 2 == c, placed, 0.0), axis=0, keepdims=True)
        for c in range(GROUP // 2)
    ]
    line = jnp.broadcast_to(jnp.concatenate(chunks, axis=1), (8, GROUP // 2 * wide)).astype(BF16)
    for v in range(out_ref.shape[0] // 8):
        part = jnp.dot(
            line, w_ref[:, pl.ds(8 * v * wide, 8 * wide)], preferred_element_type=F32
        )
        tile = jnp.zeros((8, wide), F32)
        for k in range(8):
            tile = jnp.where(row == k, part[:, k * wide : (k + 1) * wide], tile)
        out_ref[pl.ds(8 * v, 8), :] = tile


def exchange(x, axis, parts, first=0):
    shape = x.shape
    x = x.reshape(parts, shape[0] // parts, shape[1])
    groups = [[(i + first) % parts for i in range(parts)]] if first else None
    return lax.all_to_all(
        x, axis, split_axis=0, concat_axis=0, tiled=True, axis_index_groups=groups
    ).reshape(shape)


def per_device(hidden, norm_gain, w_query, w_keyval, w_out, kv_cache, block_slot, lengths):
    slots_here, _, block_len, wide = kv_cache.shape
    head_dim = wide // 2
    requests = block_slot.shape[0]
    shards = lax.axis_size("mp")
    pools = lax.axis_size("pool")
    features = hidden.shape[1]
    lines = features // wide
    place = lax.axis_index("pool").astype(jnp.int32).reshape(1)
    rows = exchange(
        jnp.broadcast_to(hidden.reshape(1, lines, wide), (shards, lines, wide)).reshape(-1, wide),
        "mp",
        shards,
    )
    gain = norm_gain.reshape(shards * lines, wide)

    turn = jax.ShapeDtypeStruct((8, wide), F32)
    w_query, w_keyval, w_out, gain = (far(x) for x in (w_query, w_keyval, w_out, gain))
    cache = far(kv_cache.reshape(slots_here, block_len, wide))
    lengths, block_slot = far(lengths), far(block_slot)
    half_cache = jax.ShapeDtypeStruct((slots_here // 2, block_len, wide), BF16)
    held_query, held_gain, first_cache, cosine, sine = call(
        functools.partial(prepare_kernel, head_dim),
        "prepare",
        (
            jax.ShapeDtypeStruct(w_query.shape, BF16),
            jax.ShapeDtypeStruct(gain.shape, F32),
            half_cache,
            turn,
            turn,
        ),
        [SMEM, SMEM, HBM, HBM, HBM],
        [pltpu.SemaphoreType.DMA((3,))],
        limit=8 << 20,
    )(place, lengths, w_query, gain, cache)

    query = call(
        functools.partial(query_kernel, head_dim),
        "query",
        jax.ShapeDtypeStruct((requests * GROUP, wide), BF16),
        [VMEM] * 5,
    )(rows, held_gain, held_query, cosine, sine)

    queries = exchange(query, "pool", pools, FIRST)

    table, second_cache = call(
        functools.partial(table_kernel, slots_here, block_len),
        "slot_table",
        (jax.ShapeDtypeStruct((slots_here, block_slot.shape[1]), jnp.int32), half_cache),
        [SMEM, SMEM, VMEM, HBM],
        [pltpu.SemaphoreType.DMA((1,))],
    )(place, lengths, block_slot, cache)
    table = table[:, 0]

    new_kv, own = call(
        functools.partial(keyval_kernel, head_dim),
        "keyval",
        (jax.ShapeDtypeStruct((1, wide), BF16), turn),
        [VMEM] * 6,
    )(rows, held_gain, cosine, sine, query, w_keyval)
    table, own = lax.optimization_barrier((table, own))

    per_request = pltpu.VMEM((requests, 8, wide), F32)
    partial, held_out = call(
        attend_kernel,
        "attend",
        (
            jax.ShapeDtypeStruct((requests * GROUP, wide), F32),
            jax.ShapeDtypeStruct(w_out.shape, BF16),
        ),
        [SMEM, VMEM, VMEM, VMEM, HBM],
        [
            per_request,
            pltpu.VMEM((slots_here // 2, 8, block_len), F32),
            per_request,
            per_request,
            per_request,
            pltpu.SemaphoreType.DMA((1,)),
        ],
        limit=12 << 20,
    )(table, queries, first_cache, second_cache, w_out)

    got = exchange(partial, "pool", pools, FIRST)

    mixed = call(
        combine_kernel,
        "combine",
        jax.ShapeDtypeStruct((shards * lines, wide), F32),
        [VMEM, VMEM, VMEM],
    )(got, own, held_out)

    spread = exchange(mixed, "mp", shards)
    total = jnp.sum(spread.reshape(shards, features), axis=0, keepdims=True)
    return (hidden + RESIDUAL_SCALE * total, new_kv)


def solution(mesh):
    return jax.shard_map(
        per_device,
        mesh=mesh,
        in_specs=(
            P("pool", "mp"),
            P(),
            P(None, "mp"),
            P(None, "mp"),
            P("mp", None),
            P("pool", "mp", None, None),
            P(),
            P(),
        ),
        out_specs=(P("pool", "mp"), P("pool", "mp")),
        check_vma=False,
    )
```

```python
import functools
import math

import jax
import jax.numpy as jnp
from jax import lax
from jax.experimental import pallas as pl
from jax.experimental.pallas import tpu as pltpu
from jax.sharding import PartitionSpec as P

EPSILON = 1e-05
RESIDUAL_SCALE = 0.22
SCORE_SCALE = 0.015625
ROPE_BASE = 10000000.0
MASKED = -1e30

F32 = jnp.float32
BF16 = jnp.bfloat16
VMEM = pl.BlockSpec(memory_space=pltpu.VMEM)
SMEM = pl.BlockSpec(memory_space=pltpu.SMEM)
HBM = pl.BlockSpec(memory_space=pltpu.HBM)

GROUP = 4

FIRST = 44
FIRST_SHARD = 4


def far(x):
    return pltpu.with_memory_space_constraint(x, pltpu.HBM)


def lanes(shape):
    return lax.broadcasted_iota(jnp.int32, shape, len(shape) - 1)


def subs(shape):
    return lax.broadcasted_iota(jnp.int32, shape, len(shape) - 2)


def call(body, name, out_shape, in_specs, scratch=(), limit=4 << 20):
    many = isinstance(out_shape, tuple)
    return pl.pallas_call(
        body,
        out_shape=out_shape,
        in_specs=in_specs,
        out_specs=(VMEM,) * len(out_shape) if many else VMEM,
        scratch_shapes=list(scratch),
        compiler_params=pltpu.CompilerParams(vmem_limit_bytes=limit),
        name=name,
    )


def sine_cosine(angle):
    turn = jnp.floor(angle * (2.0 / math.pi) + 0.5)
    x = ((angle - turn * 1.5703125) - turn * 4.837512969970703e-4) - turn * 7.54978995489188e-8
    z = x * x
    sine = ((-1.9515295891e-4 * z + 8.3321608736e-3) * z - 1.6666654611e-1) * z * x + x
    cosine = ((2.443315711809948e-5 * z - 1.388731625493765e-3) * z + 4.166664568298827e-2) * z * z
    cosine = cosine - 0.5 * z + 1.0
    quadrant = turn.astype(jnp.int32) & 3
    odd = (quadrant & 1) == 1
    out_sine = jnp.where(odd, cosine, sine)
    out_cosine = jnp.where(odd, sine, cosine)
    out_sine = jnp.where(quadrant >= 2, -out_sine, out_sine)
    out_cosine = jnp.where((quadrant == 1) | (quadrant == 2), -out_cosine, out_cosine)
    return out_sine, out_cosine


def rotation(position, head_dim, width):
    half = head_dim // 2
    lane = lanes((8, width))
    pair = lane % half
    inverse = jnp.zeros((8, width), F32)
    for i in range(half):
        inverse = jnp.where(pair == i, ROPE_BASE ** (-2.0 * i / head_dim), inverse)
    sine, cosine = sine_cosine(position.astype(F32) * inverse)
    return cosine, jnp.where(lane % head_dim < half, -sine, sine)


def rope(x, cosine, sine, half):
    ahead = pltpu.roll(x, x.shape[1] - half, 1)
    behind = pltpu.roll(x, half, 1)
    first = lanes(x.shape) % (2 * half) < half
    return x * cosine + jnp.where(first, ahead, behind) * sine


def normalise(rows_ref, gain_ref):
    count = rows_ref.shape[0]
    x = rows_ref[...]
    total = jnp.sum(jnp.sum(x * x, axis=0, keepdims=True), axis=1, keepdims=True)
    scale = lax.rsqrt(total * (1.0 / x.size) + EPSILON)
    half = count // 2
    even = pl.ds(0, half, stride=2)
    odd = pl.ds(1, half, stride=2)
    left = pltpu.roll(rows_ref[even, :], FIRST_SHARD, 0) * scale * gain_ref[even, :]
    right = pltpu.roll(rows_ref[odd, :], FIRST_SHARD, 0) * scale * gain_ref[odd, :]
    return jnp.concatenate([left, right], axis=1)


def project(normed, weight_ref):
    chunks, wide = normed.shape
    row = subs(normed.shape)
    out = None
    for j in range(chunks):
        part = jnp.dot(
            jnp.where(row == j, normed, 0.0).astype(BF16),
            weight_ref[pl.ds(j * wide, wide), :],
            preferred_element_type=F32,
        )
        out = part if out is None else out + part
    return jnp.broadcast_to(jnp.sum(out, axis=0, keepdims=True), out.shape)


def fetch(sources, targets, sems):
    copies = [pltpu.make_async_copy(s, t, sems.at[i]) for i, (s, t) in enumerate(zip(sources, targets))]
    for copy in copies:
        copy.start()
    return copies


def prepare_kernel(
    head_dim, place_ref, lengths_ref, w_ref, gain_ref, cache_ref, *rest
):
    held_w_ref, held_gain_ref, held_cache_ref, cos_ref, sin_ref, sems = rest
    first = cache_ref.at[pl.ds(0, held_cache_ref.shape[0])]
    copies = fetch((w_ref, gain_ref, first), (held_w_ref, held_gain_ref, held_cache_ref), sems)
    cos_ref[...], sin_ref[...] = rotation(lengths_ref[place_ref[0]], head_dim, 2 * head_dim)
    for copy in copies:
        copy.wait()


def query_kernel(head_dim, rows_ref, gain_ref, w_ref, cos_ref, sin_ref, out_ref):
    wide = 2 * head_dim
    cosine, sine = cos_ref[...], sin_ref[...]
    query = project(normalise(rows_ref, gain_ref), w_ref)
    row = subs((8, wide)) % GROUP
    tile = jnp.zeros((8, wide), F32)
    for c in range(GROUP // 2):
        part = rope(query[:, c * wide : (c + 1) * wide], cosine, sine, head_dim // 2)
        tile = jnp.where(row == 2 * c, part, tile)
        tile = jnp.where(row == 2 * c + 1, pltpu.roll(part, head_dim, 1), tile)
    tile = tile.astype(BF16).astype(F32) * SCORE_SCALE
    tile = jnp.where(lanes(tile.shape) < head_dim, tile, 0.0).astype(BF16)
    for v in range(out_ref.shape[0] // 8):
        out_ref[pl.ds(8 * v, 8), :] = tile


def keyval_kernel(
    head_dim, rows_ref, gain_ref, cos_ref, sin_ref, query_ref, w_ref, w_out_ref, *rest
):
    kv_ref, own_ref, held_ref, sems = rest
    copies = fetch((w_out_ref,), (held_ref,), sems)
    keyval = project(normalise(rows_ref, gain_ref), w_ref)
    is_key = lanes(keyval.shape) < head_dim
    turned = rope(keyval, cos_ref[...], sin_ref[...], head_dim // 2)
    both = jnp.where(is_key, turned, keyval).astype(BF16)
    kv_ref[...] = both[:1]
    both = both.astype(F32)
    score = jnp.sum(query_ref[:8, :].astype(F32) * both, axis=1, keepdims=True)
    own_ref[...] = jnp.where(is_key, score, both)
    copies[0].wait()


def table_kernel(
    slots_here, block_len, place_ref, lengths_ref, slot_ref, cache_ref, out_ref, held_ref, sems
):
    count = held_ref.shape[0]
    copies = fetch((cache_ref.at[pl.ds(slots_here - count, count)],), (held_ref,), sems)
    requests, blocks = slot_ref.shape
    base = place_ref[0] * slots_here
    sub = subs((8, blocks))
    lane = lanes((8, blocks))
    wanted, payload = [], []
    for v in range(requests // 8):
        length = jnp.zeros((8, blocks), jnp.int32)
        for i in range(8):
            length = jnp.where(sub == i, lengths_ref[8 * v + i], length)
        limit = length - lane * block_len
        here = slot_ref[pl.ds(8 * v, 8), :] - base
        wanted.append(jnp.where(limit > 0, here, -1))
        payload.append(
            ((sub + 8 * v + requests - FIRST) % requests) * 256 + jnp.minimum(limit, block_len)
        )
    for tile in range(slots_here // 8):
        picked = jnp.zeros((8, blocks), jnp.int32)
        for i in range(8):
            found = jnp.zeros((8, blocks), jnp.int32)
            for w, p in zip(wanted, payload):
                found = jnp.where(w == 8 * tile + i, p, found)
            picked = jnp.where(sub == i, jnp.max(found, axis=0, keepdims=True), picked)
        out_ref[pl.ds(8 * tile, 8), :] = jnp.broadcast_to(
            jnp.max(picked.astype(F32), axis=1, keepdims=True), (8, blocks)
        ).astype(jnp.int32)
    copies[0].wait()


def attend_kernel(
    tab_ref, query_ref, first_ref, second_ref, out_ref, q_s, score_s, max_s, sum_s, acc_s
):
    half, block_len, wide = first_ref.shape
    slots_here = 2 * half
    requests = query_ref.shape[0] // GROUP
    low = subs((8, wide)) < GROUP
    token = lanes((8, block_len))
    lane = lanes((8, wide))
    for v in range(requests // 2):
        tile = query_ref[pl.ds(8 * v, 8), :].astype(F32)
        other = pltpu.roll(tile, GROUP, 0)
        q_s[2 * v] = jnp.where(low, tile, other)
        q_s[2 * v + 1] = jnp.where(low, other, tile)
    max_s[...] = jnp.full_like(max_s, MASKED)
    sum_s[...] = jnp.zeros_like(sum_s)
    acc_s[...] = jnp.zeros_like(acc_s)

    def pair(p):
        a, b = tab_ref[2 * p], tab_ref[2 * p + 1]
        live = token < jnp.where(low, a & 255, b & 255)
        held, at = (first_ref, 2 * p) if 2 * p < half else (second_ref, 2 * p - half)
        keys = held[pl.ds(at, 2)].reshape(2 * block_len, wide)
        return lax.shift_right_logical(a, 8), lax.shift_right_logical(b, 8), live, keys

    for p in range(slots_here // 2):
        ra, rb, live, keys = pair(p)
        query = jnp.where(low, q_s[ra], q_s[rb]).astype(BF16)
        scores = lax.dot_general(
            query, keys, (((1,), (1,)), ((), ())), preferred_element_type=F32
        )
        scores = jnp.where(low, scores[:, :block_len], scores[:, block_len:])
        scores = jnp.where(live, scores, MASKED)
        score_s[p] = scores
        top = jnp.broadcast_to(jnp.max(scores, axis=1, keepdims=True), scores.shape)
        max_s[ra] = jnp.maximum(max_s[ra], jnp.where(low, top, MASKED))
        max_s[rb] = jnp.maximum(max_s[rb], jnp.where(low, MASKED, top))

    for r in range(requests):
        top = max_s[r]
        max_s[r] = jnp.maximum(top, pltpu.roll(top, GROUP, 0))

    for p in range(slots_here // 2):
        ra, rb, live, values = pair(p)
        top = jnp.where(low, max_s[ra], max_s[rb])
        weight = jnp.where(live, jnp.exp(score_s[p] - top), 0.0).astype(BF16).astype(F32)
        both = jnp.concatenate(
            [jnp.where(low, weight, 0.0), jnp.where(low, 0.0, weight)], axis=1
        ).astype(BF16)
        out = jnp.dot(both, values, preferred_element_type=F32)
        total = jnp.broadcast_to(jnp.sum(weight, axis=1, keepdims=True), out.shape)
        acc_s[ra] = acc_s[ra] + jnp.where(low, out, 0.0)
        acc_s[rb] = acc_s[rb] + jnp.where(low, 0.0, out)
        sum_s[ra] = sum_s[ra] + jnp.where(low, total, 0.0)
        sum_s[rb] = sum_s[rb] + jnp.where(low, 0.0, total)

    for v in range(requests // 2):
        tiles = []
        for r in (2 * v, 2 * v + 1):
            out = acc_s[r] + pltpu.roll(acc_s[r], GROUP, 0)
            total = sum_s[r] + pltpu.roll(sum_s[r], GROUP, 0)
            tiles.append(
                jnp.where(lane < wide // 4, max_s[r], jnp.where(lane < wide // 2, total, out))
            )
        out_ref[pl.ds(8 * v, 8), :] = jnp.where(low, tiles[0], tiles[1])


def combine_kernel(got_ref, own_ref, w_ref, out_ref):
    rows, wide = got_ref.shape
    lane = lanes((8, wide))
    row = subs((8, wide))
    parts = [got_ref[pl.ds(8 * v, 8), :] for v in range(rows // 8)]
    top = parts[0]
    for part in parts[1:]:
        top = jnp.maximum(top, part)
    own = own_ref[...]
    top = jnp.maximum(jnp.maximum(top, pltpu.roll(top, GROUP, 0)), own)
    mixed = jnp.zeros((8, wide), F32)
    for part in parts:
        weight = jnp.exp(part - top)
        mixed = mixed + jnp.broadcast_to(weight[:, :1], part.shape) * part
    mixed = mixed + pltpu.roll(mixed, GROUP, 0)
    own_weight = jnp.exp(own - top)
    mixed = mixed + jnp.broadcast_to(own_weight[:, :1], own.shape) * jnp.where(
        lane < wide // 2, 1.0, own
    )
    attended = mixed / jnp.broadcast_to(mixed[:, wide // 4 : wide // 4 + 1], mixed.shape)
    swapped = pltpu.roll(attended, wide // 2, 1)
    placed = jnp.where(
        row % 2 == 0,
        jnp.where(lane < wide // 2, swapped, 0.0),
        jnp.where(lane < wide // 2, 0.0, attended),
    )
    chunks = [
        jnp.sum(jnp.where(row // 2 == c, placed, 0.0), axis=0, keepdims=True)
        for c in range(GROUP // 2)
    ]
    line = jnp.broadcast_to(jnp.concatenate(chunks, axis=1), (8, GROUP // 2 * wide)).astype(BF16)
    lines = out_ref.shape[0]
    for v in range(lines // 8):
        at = (8 * v + FIRST_SHARD * GROUP // 2) % lines * wide
        part = jnp.dot(line, w_ref[:, pl.ds(at, 8 * wide)], preferred_element_type=F32)
        tile = jnp.zeros((8, wide), F32)
        for k in range(8):
            tile = jnp.where(row == k, part[:, k * wide : (k + 1) * wide], tile)
        out_ref[pl.ds(8 * v, 8), :] = tile


def exchange(x, axis, parts, first=0):
    shape = x.shape
    x = x.reshape(parts, shape[0] // parts, shape[1])
    groups = [[(i + first) % parts for i in range(parts)]] if first else None
    return lax.all_to_all(
        x, axis, split_axis=0, concat_axis=0, tiled=True, axis_index_groups=groups
    ).reshape(shape)


def per_device(hidden, norm_gain, w_query, w_keyval, w_out, kv_cache, block_slot, lengths):
    slots_here, _, block_len, wide = kv_cache.shape
    head_dim = wide // 2
    requests = block_slot.shape[0]
    shards = lax.axis_size("mp")
    pools = lax.axis_size("pool")
    features = hidden.shape[1]
    lines = features // wide
    place = lax.axis_index("pool").astype(jnp.int32).reshape(1)
    rows = exchange(
        jnp.broadcast_to(hidden.reshape(1, lines, wide), (shards, lines, wide)).reshape(-1, wide),
        "mp",
        shards,
        FIRST_SHARD,
    )
    gain = norm_gain.reshape(shards * lines, wide)

    turn = jax.ShapeDtypeStruct((8, wide), F32)
    w_query, w_keyval, w_out, gain = (far(x) for x in (w_query, w_keyval, w_out, gain))
    cache = far(kv_cache.reshape(slots_here, block_len, wide))
    lengths, block_slot = far(lengths), far(block_slot)
    half_cache = jax.ShapeDtypeStruct((slots_here // 2, block_len, wide), BF16)
    held_query, held_gain, first_cache, cosine, sine = call(
        functools.partial(prepare_kernel, head_dim),
        "prepare",
        (
            jax.ShapeDtypeStruct(w_query.shape, BF16),
            jax.ShapeDtypeStruct(gain.shape, F32),
            half_cache,
            turn,
            turn,
        ),
        [SMEM, SMEM, HBM, HBM, HBM],
        [pltpu.SemaphoreType.DMA((3,))],
        limit=8 << 20,
    )(place, lengths, w_query, gain, cache)

    query = call(
        functools.partial(query_kernel, head_dim),
        "query",
        jax.ShapeDtypeStruct((requests * GROUP, wide), BF16),
        [VMEM] * 5,
    )(rows, held_gain, held_query, cosine, sine)

    queries = exchange(query, "pool", pools, FIRST)

    table, second_cache = call(
        functools.partial(table_kernel, slots_here, block_len),
        "slot_table",
        (jax.ShapeDtypeStruct((slots_here, block_slot.shape[1]), jnp.int32), half_cache),
        [SMEM, SMEM, VMEM, HBM],
        [pltpu.SemaphoreType.DMA((1,))],
    )(place, lengths, block_slot, cache)
    table = table[:, 0]

    new_kv, own, held_out = call(
        functools.partial(keyval_kernel, head_dim),
        "keyval",
        (
            jax.ShapeDtypeStruct((1, wide), BF16),
            turn,
            jax.ShapeDtypeStruct(w_out.shape, BF16),
        ),
        [VMEM] * 6 + [HBM],
        [pltpu.SemaphoreType.DMA((1,))],
    )(rows, held_gain, cosine, sine, query, w_keyval, w_out)
    table, own = lax.optimization_barrier((table, own))

    per_request = pltpu.VMEM((requests, 8, wide), F32)
    partial = call(
        attend_kernel,
        "attend",
        jax.ShapeDtypeStruct((requests * GROUP, wide), F32),
        [SMEM, VMEM, VMEM, VMEM],
        [
            per_request,
            pltpu.VMEM((slots_here // 2, 8, block_len), F32),
            per_request,
            per_request,
            per_request,
        ],
        limit=12 << 20,
    )(table, queries, first_cache, second_cache)

    got = exchange(partial, "pool", pools, FIRST)

    mixed = call(
        combine_kernel,
        "combine",
        jax.ShapeDtypeStruct((shards * lines, wide), F32),
        [VMEM, VMEM, VMEM],
    )(got, own, held_out)

    spread = exchange(mixed, "mp", shards, FIRST_SHARD)
    total = jnp.sum(spread.reshape(shards, features), axis=0, keepdims=True)
    return (hidden + RESIDUAL_SCALE * total, new_kv)


def solution(mesh):
    return jax.shard_map(
        per_device,
        mesh=mesh,
        in_specs=(
            P("pool", "mp"),
            P(),
            P(None, "mp"),
            P(None, "mp"),
            P("mp", None),
            P("pool", "mp", None, None),
            P(),
            P(),
        ),
        out_specs=(P("pool", "mp"), P("pool", "mp")),
        check_vma=False,
    )
```

```python
import functools
import math

import jax
import jax.numpy as jnp
from jax import lax
from jax.experimental import pallas as pl
from jax.experimental.pallas import tpu as pltpu
from jax.sharding import PartitionSpec as P

EPSILON = 1e-05
RESIDUAL_SCALE = 0.22
SCORE_SCALE = 0.015625
ROPE_BASE = 10000000.0
MASKED = -1e30

F32 = jnp.float32
BF16 = jnp.bfloat16
VMEM = pl.BlockSpec(memory_space=pltpu.VMEM)
SMEM = pl.BlockSpec(memory_space=pltpu.SMEM)
HBM = pl.BlockSpec(memory_space=pltpu.HBM)

GROUP = 4

FIRST = 44
FIRST_SHARD = 4


def far(x):
    return pltpu.with_memory_space_constraint(x, pltpu.HBM)


def lanes(shape):
    return lax.broadcasted_iota(jnp.int32, shape, len(shape) - 1)


def subs(shape):
    return lax.broadcasted_iota(jnp.int32, shape, len(shape) - 2)


def call(body, name, out_shape, in_specs, scratch=(), limit=4 << 20):
    many = isinstance(out_shape, tuple)
    return pl.pallas_call(
        body,
        out_shape=out_shape,
        in_specs=in_specs,
        out_specs=(VMEM,) * len(out_shape) if many else VMEM,
        scratch_shapes=list(scratch),
        compiler_params=pltpu.CompilerParams(vmem_limit_bytes=limit),
        name=name,
    )


def sine_cosine(angle):
    turn = jnp.floor(angle * (2.0 / math.pi) + 0.5)
    x = ((angle - turn * 1.5703125) - turn * 4.837512969970703e-4) - turn * 7.54978995489188e-8
    z = x * x
    sine = ((-1.9515295891e-4 * z + 8.3321608736e-3) * z - 1.6666654611e-1) * z * x + x
    cosine = ((2.443315711809948e-5 * z - 1.388731625493765e-3) * z + 4.166664568298827e-2) * z * z
    cosine = cosine - 0.5 * z + 1.0
    quadrant = turn.astype(jnp.int32) & 3
    odd = (quadrant & 1) == 1
    out_sine = jnp.where(odd, cosine, sine)
    out_cosine = jnp.where(odd, sine, cosine)
    out_sine = jnp.where(quadrant >= 2, -out_sine, out_sine)
    out_cosine = jnp.where((quadrant == 1) | (quadrant == 2), -out_cosine, out_cosine)
    return out_sine, out_cosine


def rotation(position, head_dim, width):
    half = head_dim // 2
    lane = lanes((8, width))
    pair = lane % half
    inverse = jnp.zeros((8, width), F32)
    for i in range(half):
        inverse = jnp.where(pair == i, ROPE_BASE ** (-2.0 * i / head_dim), inverse)
    sine, cosine = sine_cosine(position.astype(F32) * inverse)
    return cosine, jnp.where(lane % head_dim < half, -sine, sine)


def rope(x, cosine, sine, half):
    ahead = pltpu.roll(x, x.shape[1] - half, 1)
    behind = pltpu.roll(x, half, 1)
    first = lanes(x.shape) % (2 * half) < half
    return x * cosine + jnp.where(first, ahead, behind) * sine


def normalise(rows_ref, gain_ref):
    count = rows_ref.shape[0]
    x = rows_ref[...]
    total = jnp.sum(jnp.sum(x * x, axis=0, keepdims=True), axis=1, keepdims=True)
    scale = lax.rsqrt(total * (1.0 / x.size) + EPSILON)
    half = count // 2
    even = pl.ds(0, half, stride=2)
    odd = pl.ds(1, half, stride=2)
    left = pltpu.roll(rows_ref[even, :], FIRST_SHARD, 0) * scale * gain_ref[even, :]
    right = pltpu.roll(rows_ref[odd, :], FIRST_SHARD, 0) * scale * gain_ref[odd, :]
    return jnp.concatenate([left, right], axis=1)


def project(normed, weight_ref):
    chunks, wide = normed.shape
    row = subs(normed.shape)
    out = None
    for j in range(chunks):
        part = jnp.dot(
            jnp.where(row == j, normed, 0.0).astype(BF16),
            weight_ref[pl.ds(j * wide, wide), :],
            preferred_element_type=F32,
        )
        out = part if out is None else out + part
    return jnp.broadcast_to(jnp.sum(out, axis=0, keepdims=True), out.shape)


def fetch(sources, targets, sems):
    copies = [pltpu.make_async_copy(s, t, sems.at[i]) for i, (s, t) in enumerate(zip(sources, targets))]
    for copy in copies:
        copy.start()
    return copies


def prepare_kernel(head_dim, lengths_ref, w_ref, gain_ref, cache_ref, *rest):
    held_w_ref, held_gain_ref, held_cache_ref, cos_ref, sin_ref, near_lengths, sems = rest
    first = cache_ref.at[pl.ds(0, held_cache_ref.shape[0])]
    copies = fetch(
        (lengths_ref, w_ref, gain_ref, first),
        (near_lengths, held_w_ref, held_gain_ref, held_cache_ref),
        sems,
    )
    copies[0].wait()
    position = near_lengths[lax.axis_index("pool")]
    cos_ref[...], sin_ref[...] = rotation(position, head_dim, 2 * head_dim)
    for copy in copies[1:]:
        copy.wait()


def query_kernel(head_dim, rows_ref, gain_ref, w_ref, cos_ref, sin_ref, out_ref):
    wide = 2 * head_dim
    cosine, sine = cos_ref[...], sin_ref[...]
    query = project(normalise(rows_ref, gain_ref), w_ref)
    row = subs((8, wide)) % GROUP
    tile = jnp.zeros((8, wide), F32)
    for c in range(GROUP // 2):
        part = rope(query[:, c * wide : (c + 1) * wide], cosine, sine, head_dim // 2)
        tile = jnp.where(row == 2 * c, part, tile)
        tile = jnp.where(row == 2 * c + 1, pltpu.roll(part, head_dim, 1), tile)
    tile = tile.astype(BF16).astype(F32) * SCORE_SCALE
    tile = jnp.where(lanes(tile.shape) < head_dim, tile, 0.0).astype(BF16)
    for v in range(out_ref.shape[0] // 8):
        out_ref[pl.ds(8 * v, 8), :] = tile


def keyval_kernel(
    head_dim, rows_ref, gain_ref, cos_ref, sin_ref, query_ref, w_hbm, kv_ref, own_ref, w_ref, sems
):
    copies = fetch((w_hbm,), (w_ref,), sems)
    normed = normalise(rows_ref, gain_ref)
    copies[0].wait()
    keyval = project(normed, w_ref)
    is_key = lanes(keyval.shape) < head_dim
    turned = rope(keyval, cos_ref[...], sin_ref[...], head_dim // 2)
    both = jnp.where(is_key, turned, keyval).astype(BF16)
    kv_ref[...] = both[:1]
    both = both.astype(F32)
    score = jnp.sum(query_ref[:8, :].astype(F32) * both, axis=1, keepdims=True)
    own_ref[...] = jnp.where(is_key, score, both)


def table_kernel(
    slots_here, block_len, lengths_hbm, slot_hbm, cache_ref, out_ref, held_ref, lengths_ref, slot_ref, sems
):
    count = held_ref.shape[0]
    copies = fetch(
        (lengths_hbm, slot_hbm, cache_ref.at[pl.ds(slots_here - count, count)]),
        (lengths_ref, slot_ref, held_ref),
        sems,
    )
    copies[0].wait()
    copies[1].wait()
    requests, blocks = slot_ref.shape
    base = lax.axis_index("pool") * slots_here
    sub = subs((8, blocks))
    lane = lanes((8, blocks))
    wanted, payload = [], []
    for v in range(requests // 8):
        length = jnp.zeros((8, blocks), jnp.int32)
        for i in range(8):
            length = jnp.where(sub == i, lengths_ref[8 * v + i], length)
        limit = length - lane * block_len
        here = slot_ref[pl.ds(8 * v, 8), :] - base
        wanted.append(jnp.where(limit > 0, here, -1))
        payload.append(
            ((sub + 8 * v + requests - FIRST) % requests) * 256 + jnp.minimum(limit, block_len)
        )
    for tile in range(slots_here // 8):
        picked = jnp.zeros((8, blocks), jnp.int32)
        for i in range(8):
            found = jnp.zeros((8, blocks), jnp.int32)
            for w, p in zip(wanted, payload):
                found = jnp.where(w == 8 * tile + i, p, found)
            picked = jnp.where(sub == i, jnp.max(found, axis=0, keepdims=True), picked)
        out_ref[pl.ds(8 * tile, 8), :] = jnp.broadcast_to(
            jnp.max(picked.astype(F32), axis=1, keepdims=True), (8, blocks)
        ).astype(jnp.int32)
    copies[2].wait()


def attend_kernel(
    tab_ref, query_ref, first_ref, second_ref, out_ref, q_s, score_s, max_s, sum_s, acc_s
):
    half, block_len, wide = first_ref.shape
    slots_here = 2 * half
    requests = query_ref.shape[0] // GROUP
    low = subs((8, wide)) < GROUP
    token = lanes((8, block_len))
    lane = lanes((8, wide))
    for v in range(requests // 2):
        tile = query_ref[pl.ds(8 * v, 8), :].astype(F32)
        other = pltpu.roll(tile, GROUP, 0)
        q_s[2 * v] = jnp.where(low, tile, other)
        q_s[2 * v + 1] = jnp.where(low, other, tile)
    max_s[...] = jnp.full_like(max_s, MASKED)
    sum_s[...] = jnp.zeros_like(sum_s)
    acc_s[...] = jnp.zeros_like(acc_s)

    def pair(p):
        a, b = tab_ref[2 * p], tab_ref[2 * p + 1]
        live = token < jnp.where(low, a & 255, b & 255)
        held, at = (first_ref, 2 * p) if 2 * p < half else (second_ref, 2 * p - half)
        keys = held[pl.ds(at, 2)].reshape(2 * block_len, wide)
        return lax.shift_right_logical(a, 8), lax.shift_right_logical(b, 8), live, keys

    for p in range(slots_here // 2):
        ra, rb, live, keys = pair(p)
        query = jnp.where(low, q_s[ra], q_s[rb]).astype(BF16)
        scores = lax.dot_general(
            query, keys, (((1,), (1,)), ((), ())), preferred_element_type=F32
        )
        scores = jnp.where(low, scores[:, :block_len], scores[:, block_len:])
        scores = jnp.where(live, scores, MASKED)
        score_s[p] = scores
        top = jnp.broadcast_to(jnp.max(scores, axis=1, keepdims=True), scores.shape)
        max_s[ra] = jnp.maximum(max_s[ra], jnp.where(low, top, MASKED))
        max_s[rb] = jnp.maximum(max_s[rb], jnp.where(low, MASKED, top))

    for r in range(requests):
        top = max_s[r]
        max_s[r] = jnp.maximum(top, pltpu.roll(top, GROUP, 0))

    for p in range(slots_here // 2):
        ra, rb, live, values = pair(p)
        top = jnp.where(low, max_s[ra], max_s[rb])
        weight = jnp.where(live, jnp.exp(score_s[p] - top), 0.0).astype(BF16).astype(F32)
        both = jnp.concatenate(
            [jnp.where(low, weight, 0.0), jnp.where(low, 0.0, weight)], axis=1
        ).astype(BF16)
        out = jnp.dot(both, values, preferred_element_type=F32)
        total = jnp.broadcast_to(jnp.sum(weight, axis=1, keepdims=True), out.shape)
        acc_s[ra] = acc_s[ra] + jnp.where(low, out, 0.0)
        acc_s[rb] = acc_s[rb] + jnp.where(low, 0.0, out)
        sum_s[ra] = sum_s[ra] + jnp.where(low, total, 0.0)
        sum_s[rb] = sum_s[rb] + jnp.where(low, 0.0, total)

    for v in range(requests // 2):
        tiles = []
        for r in (2 * v, 2 * v + 1):
            out = acc_s[r] + pltpu.roll(acc_s[r], GROUP, 0)
            total = sum_s[r] + pltpu.roll(sum_s[r], GROUP, 0)
            tiles.append(
                jnp.where(lane < wide // 4, max_s[r], jnp.where(lane < wide // 2, total, out))
            )
        out_ref[pl.ds(8 * v, 8), :] = jnp.where(low, tiles[0], tiles[1])


def combine_kernel(got_ref, own_ref, w_hbm, out_ref, w_ref, sems):
    tiles = out_ref.shape[0] // 8
    share = w_ref.shape[1] // tiles
    columns_of = [pl.ds((v + FIRST_SHARD * GROUP // 16) % tiles * share, share) for v in range(tiles)]
    copies = fetch([w_hbm.at[:, c] for c in columns_of], [w_ref.at[:, c] for c in columns_of], sems)
    rows, wide = got_ref.shape
    lane = lanes((8, wide))
    row = subs((8, wide))
    parts = [got_ref[pl.ds(8 * v, 8), :] for v in range(rows // 8)]
    top = parts[0]
    for part in parts[1:]:
        top = jnp.maximum(top, part)
    own = own_ref[...]
    top = jnp.maximum(jnp.maximum(top, pltpu.roll(top, GROUP, 0)), own)
    mixed = jnp.zeros((8, wide), F32)
    for part in parts:
        weight = jnp.exp(part - top)
        mixed = mixed + jnp.broadcast_to(weight[:, :1], part.shape) * part
    mixed = mixed + pltpu.roll(mixed, GROUP, 0)
    own_weight = jnp.exp(own - top)
    mixed = mixed + jnp.broadcast_to(own_weight[:, :1], own.shape) * jnp.where(
        lane < wide // 2, 1.0, own
    )
    attended = mixed / jnp.broadcast_to(mixed[:, wide // 4 : wide // 4 + 1], mixed.shape)
    swapped = pltpu.roll(attended, wide // 2, 1)
    placed = jnp.where(
        row % 2 == 0,
        jnp.where(lane < wide // 2, swapped, 0.0),
        jnp.where(lane < wide // 2, 0.0, attended),
    )
    chunks = [
        jnp.sum(jnp.where(row // 2 == c, placed, 0.0), axis=0, keepdims=True)
        for c in range(GROUP // 2)
    ]
    line = jnp.broadcast_to(jnp.concatenate(chunks, axis=1), (8, GROUP // 2 * wide)).astype(BF16)
    for v, columns in enumerate(columns_of):
        copies[v].wait()
        part = jnp.dot(line, w_ref[:, columns], preferred_element_type=F32)
        tile = jnp.zeros((8, wide), F32)
        for k in range(8):
            tile = jnp.where(row == k, part[:, k * wide : (k + 1) * wide], tile)
        out_ref[pl.ds(8 * v, 8), :] = tile


def exchange(x, axis, parts, first=0):
    shape = x.shape
    x = x.reshape(parts, shape[0] // parts, shape[1])
    groups = [[(i + first) % parts for i in range(parts)]] if first else None
    return lax.all_to_all(
        x, axis, split_axis=0, concat_axis=0, tiled=True, axis_index_groups=groups
    ).reshape(shape)


def per_device(hidden, norm_gain, w_query, w_keyval, w_out, kv_cache, block_slot, lengths):
    slots_here, _, block_len, wide = kv_cache.shape
    head_dim = wide // 2
    requests = block_slot.shape[0]
    shards = lax.axis_size("mp")
    pools = lax.axis_size("pool")
    features = hidden.shape[1]
    lines = features // wide
    rows = exchange(
        jnp.broadcast_to(hidden.reshape(1, lines, wide), (shards, lines, wide)).reshape(-1, wide),
        "mp",
        shards,
        FIRST_SHARD,
    )
    gain = norm_gain.reshape(shards * lines, wide)

    turn = jax.ShapeDtypeStruct((8, wide), F32)
    w_query, w_keyval, w_out, gain = (far(x) for x in (w_query, w_keyval, w_out, gain))
    cache = far(kv_cache.reshape(slots_here, block_len, wide))
    lengths, block_slot = far(lengths), far(block_slot)
    half_cache = jax.ShapeDtypeStruct((slots_here // 2, block_len, wide), BF16)
    held_query, held_gain, first_cache, cosine, sine = call(
        functools.partial(prepare_kernel, head_dim),
        "prepare",
        (
            jax.ShapeDtypeStruct(w_query.shape, BF16),
            jax.ShapeDtypeStruct(gain.shape, F32),
            half_cache,
            turn,
            turn,
        ),
        [HBM] * 4,
        [pltpu.SMEM(lengths.shape, jnp.int32), pltpu.SemaphoreType.DMA((4,))],
        limit=8 << 20,
    )(lengths, w_query, gain, cache)

    query = call(
        functools.partial(query_kernel, head_dim),
        "query",
        jax.ShapeDtypeStruct((requests * GROUP, wide), BF16),
        [VMEM] * 5,
    )(rows, held_gain, held_query, cosine, sine)

    queries = exchange(query, "pool", pools, FIRST)

    table, second_cache = call(
        functools.partial(table_kernel, slots_here, block_len),
        "slot_table",
        (jax.ShapeDtypeStruct((slots_here, block_slot.shape[1]), jnp.int32), half_cache),
        [HBM] * 3,
        [
            pltpu.SMEM(lengths.shape, jnp.int32),
            pltpu.VMEM(block_slot.shape, jnp.int32),
            pltpu.SemaphoreType.DMA((3,)),
        ],
    )(lengths, block_slot, cache)
    table = table[:, 0]

    new_kv, own = call(
        functools.partial(keyval_kernel, head_dim),
        "keyval",
        (jax.ShapeDtypeStruct((1, wide), BF16), turn),
        [VMEM] * 5 + [HBM],
        [pltpu.VMEM(w_keyval.shape, BF16), pltpu.SemaphoreType.DMA((1,))],
    )(rows, held_gain, cosine, sine, query, w_keyval)
    table, own = lax.optimization_barrier((table, own))

    per_request = pltpu.VMEM((requests, 8, wide), F32)
    partial = call(
        attend_kernel,
        "attend",
        jax.ShapeDtypeStruct((requests * GROUP, wide), F32),
        [SMEM, VMEM, VMEM, VMEM],
        [
            per_request,
            pltpu.VMEM((slots_here // 2, 8, block_len), F32),
            per_request,
            per_request,
            per_request,
        ],
        limit=12 << 20,
    )(table, queries, first_cache, second_cache)

    got = exchange(partial, "pool", pools, FIRST)

    mixed = call(
        combine_kernel,
        "combine",
        jax.ShapeDtypeStruct((shards * lines, wide), F32),
        [VMEM, VMEM, HBM],
        [pltpu.VMEM(w_out.shape, BF16), pltpu.SemaphoreType.DMA((shards * lines // 8,))],
    )(got, own, w_out)

    spread = exchange(mixed, "mp", shards, FIRST_SHARD)
    total = jnp.sum(spread.reshape(shards, features), axis=0, keepdims=True)
    return (hidden + RESIDUAL_SCALE * total, new_kv)


def solution(mesh):
    return jax.shard_map(
        per_device,
        mesh=mesh,
        in_specs=(
            P("pool", "mp"),
            P(),
            P(None, "mp"),
            P(None, "mp"),
            P("mp", None),
            P("pool", "mp", None, None),
            P(),
            P(),
        ),
        out_specs=(P("pool", "mp"), P("pool", "mp")),
        check_vma=False,
    )
```

```python
import functools
import math

import jax
import jax.numpy as jnp
from jax import lax
from jax.experimental import pallas as pl
from jax.experimental.pallas import tpu as pltpu
from jax.sharding import PartitionSpec as P

EPSILON = 1e-05
RESIDUAL_SCALE = 0.22
SCORE_SCALE = 0.015625
ROPE_BASE = 10000000.0
MASKED = -1e30

F32 = jnp.float32
BF16 = jnp.bfloat16
VMEM = pl.BlockSpec(memory_space=pltpu.VMEM)
SMEM = pl.BlockSpec(memory_space=pltpu.SMEM)
HBM = pl.BlockSpec(memory_space=pltpu.HBM)

GROUP = 4

FIRST = 44
FIRST_SHARD = 4


def far(x):
    return pltpu.with_memory_space_constraint(x, pltpu.HBM)


def lanes(shape):
    return lax.broadcasted_iota(jnp.int32, shape, len(shape) - 1)


def subs(shape):
    return lax.broadcasted_iota(jnp.int32, shape, len(shape) - 2)


def call(body, name, out_shape, in_specs, scratch=(), limit=4 << 20):
    many = isinstance(out_shape, tuple)
    return pl.pallas_call(
        body,
        out_shape=out_shape,
        in_specs=in_specs,
        out_specs=(VMEM,) * len(out_shape) if many else VMEM,
        scratch_shapes=list(scratch),
        compiler_params=pltpu.CompilerParams(vmem_limit_bytes=limit),
        name=name,
    )


def sine_cosine(angle):
    turn = jnp.floor(angle * (2.0 / math.pi) + 0.5)
    x = ((angle - turn * 1.5703125) - turn * 4.837512969970703e-4) - turn * 7.54978995489188e-8
    z = x * x
    sine = ((-1.9515295891e-4 * z + 8.3321608736e-3) * z - 1.6666654611e-1) * z * x + x
    cosine = ((2.443315711809948e-5 * z - 1.388731625493765e-3) * z + 4.166664568298827e-2) * z * z
    cosine = cosine - 0.5 * z + 1.0
    quadrant = turn.astype(jnp.int32) & 3
    odd = (quadrant & 1) == 1
    out_sine = jnp.where(odd, cosine, sine)
    out_cosine = jnp.where(odd, sine, cosine)
    out_sine = jnp.where(quadrant >= 2, -out_sine, out_sine)
    out_cosine = jnp.where((quadrant == 1) | (quadrant == 2), -out_cosine, out_cosine)
    return out_sine, out_cosine


def rotation(position, head_dim, width):
    half = head_dim // 2
    lane = lanes((8, width))
    pair = lane % half
    inverse = jnp.zeros((8, width), F32)
    for i in range(half):
        inverse = jnp.where(pair == i, ROPE_BASE ** (-2.0 * i / head_dim), inverse)
    sine, cosine = sine_cosine(position.astype(F32) * inverse)
    return cosine, jnp.where(lane % head_dim < half, -sine, sine)


def rope(x, cosine, sine, half):
    ahead = pltpu.roll(x, x.shape[1] - half, 1)
    behind = pltpu.roll(x, half, 1)
    first = lanes(x.shape) % (2 * half) < half
    return x * cosine + jnp.where(first, ahead, behind) * sine


def normalise(rows_ref, gain_ref):
    count = rows_ref.shape[0]
    x = rows_ref[...]
    total = jnp.sum(jnp.sum(x * x, axis=0, keepdims=True), axis=1, keepdims=True)
    scale = lax.rsqrt(total * (1.0 / x.size) + EPSILON)
    half = count // 2
    even = pl.ds(0, half, stride=2)
    odd = pl.ds(1, half, stride=2)
    left = pltpu.roll(rows_ref[even, :], FIRST_SHARD, 0) * scale * gain_ref[even, :]
    right = pltpu.roll(rows_ref[odd, :], FIRST_SHARD, 0) * scale * gain_ref[odd, :]
    return jnp.concatenate([left, right], axis=1)


def project(normed, weight_ref):
    chunks, wide = normed.shape
    row = subs(normed.shape)
    out = None
    for j in range(chunks):
        part = jnp.dot(
            jnp.where(row == j, normed, 0.0).astype(BF16),
            weight_ref[pl.ds(j * wide, wide), :],
            preferred_element_type=F32,
        )
        out = part if out is None else out + part
    return jnp.broadcast_to(jnp.sum(out, axis=0, keepdims=True), out.shape)


def fetch(sources, targets, sems):
    copies = [pltpu.make_async_copy(s, t, sems.at[i]) for i, (s, t) in enumerate(zip(sources, targets))]
    for copy in copies:
        copy.start()
    return copies


def spread_kernel(x_ref, out_ref, sems):
    size = x_ref.shape[0]
    shares = range(out_ref.shape[0] // size)
    copies = fetch([x_ref for _ in shares], [out_ref.at[pl.ds(i * size, size)] for i in shares], sems)
    for copy in copies:
        copy.wait()


def prepare_kernel(head_dim, lengths_ref, w_ref, gain_ref, cache_ref, *rest):
    held_w_ref, held_gain_ref, held_cache_ref, cos_ref, sin_ref, near_lengths, sems = rest
    first = cache_ref.at[pl.ds(0, held_cache_ref.shape[0])]
    copies = fetch(
        (lengths_ref, w_ref, gain_ref, first),
        (near_lengths, held_w_ref, held_gain_ref, held_cache_ref),
        sems,
    )
    copies[0].wait()
    position = near_lengths[lax.axis_index("pool")]
    cos_ref[...], sin_ref[...] = rotation(position, head_dim, 2 * head_dim)
    for copy in copies[1:]:
        copy.wait()


def query_kernel(head_dim, rows_ref, gain_ref, w_ref, cos_ref, sin_ref, out_ref):
    wide = 2 * head_dim
    cosine, sine = cos_ref[...], sin_ref[...]
    query = project(normalise(rows_ref, gain_ref), w_ref)
    row = subs((8, wide)) % GROUP
    tile = jnp.zeros((8, wide), F32)
    for c in range(GROUP // 2):
        part = rope(query[:, c * wide : (c + 1) * wide], cosine, sine, head_dim // 2)
        tile = jnp.where(row == 2 * c, part, tile)
        tile = jnp.where(row == 2 * c + 1, pltpu.roll(part, head_dim, 1), tile)
    tile = tile.astype(BF16).astype(F32) * SCORE_SCALE
    tile = jnp.where(lanes(tile.shape) < head_dim, tile, 0.0).astype(BF16)
    for v in range(out_ref.shape[0] // 8):
        out_ref[pl.ds(8 * v, 8), :] = tile


def keyval_kernel(
    head_dim, rows_ref, gain_ref, cos_ref, sin_ref, query_hbm, w_hbm, kv_ref, own_ref, w_ref, query_ref, sems
):
    copies = fetch((w_hbm, query_hbm.at[pl.ds(0, query_ref.shape[0])]), (w_ref, query_ref), sems)
    normed = normalise(rows_ref, gain_ref)
    for copy in copies:
        copy.wait()
    keyval = project(normed, w_ref)
    is_key = lanes(keyval.shape) < head_dim
    turned = rope(keyval, cos_ref[...], sin_ref[...], head_dim // 2)
    both = jnp.where(is_key, turned, keyval).astype(BF16)
    kv_ref[...] = both[:1]
    both = both.astype(F32)
    score = jnp.sum(query_ref[:8, :].astype(F32) * both, axis=1, keepdims=True)
    own_ref[...] = jnp.where(is_key, score, both)


def table_kernel(
    slots_here, block_len, lengths_hbm, slot_hbm, cache_ref, out_ref, held_ref, lengths_ref, slot_ref, sems
):
    count = held_ref.shape[0]
    copies = fetch(
        (lengths_hbm, slot_hbm, cache_ref.at[pl.ds(slots_here - count, count)]),
        (lengths_ref, slot_ref, held_ref),
        sems,
    )
    copies[0].wait()
    copies[1].wait()
    requests, blocks = slot_ref.shape
    base = lax.axis_index("pool") * slots_here
    sub = subs((8, blocks))
    lane = lanes((8, blocks))
    wanted, payload = [], []
    for v in range(requests // 8):
        length = jnp.zeros((8, blocks), jnp.int32)
        for i in range(8):
            length = jnp.where(sub == i, lengths_ref[8 * v + i], length)
        limit = length - lane * block_len
        here = slot_ref[pl.ds(8 * v, 8), :] - base
        wanted.append(jnp.where(limit > 0, here, -1))
        payload.append(
            ((sub + 8 * v + requests - FIRST) % requests) * 256 + jnp.minimum(limit, block_len)
        )
    for tile in range(slots_here // 8):
        picked = jnp.zeros((8, blocks), jnp.int32)
        for i in range(8):
            found = jnp.zeros((8, blocks), jnp.int32)
            for w, p in zip(wanted, payload):
                found = jnp.where(w == 8 * tile + i, p, found)
            picked = jnp.where(sub == i, jnp.max(found, axis=0, keepdims=True), picked)
        out_ref[pl.ds(8 * tile, 8), :] = jnp.broadcast_to(
            jnp.max(picked.astype(F32), axis=1, keepdims=True), (8, blocks)
        ).astype(jnp.int32)
    copies[2].wait()


def attend_kernel(
    tab_ref, query_ref, first_ref, second_ref, out_ref, q_s, score_s, max_s, sum_s, acc_s
):
    half, block_len, wide = first_ref.shape
    slots_here = 2 * half
    requests = query_ref.shape[0] // GROUP
    low = subs((8, wide)) < GROUP
    token = lanes((8, block_len))
    lane = lanes((8, wide))
    for v in range(requests // 2):
        tile = query_ref[pl.ds(8 * v, 8), :].astype(F32)
        other = pltpu.roll(tile, GROUP, 0)
        q_s[2 * v] = jnp.where(low, tile, other)
        q_s[2 * v + 1] = jnp.where(low, other, tile)
    max_s[...] = jnp.full_like(max_s, MASKED)
    sum_s[...] = jnp.zeros_like(sum_s)
    acc_s[...] = jnp.zeros_like(acc_s)

    def pair(p):
        a, b = tab_ref[2 * p], tab_ref[2 * p + 1]
        live = token < jnp.where(low, a & 255, b & 255)
        held, at = (first_ref, 2 * p) if 2 * p < half else (second_ref, 2 * p - half)
        keys = held[pl.ds(at, 2)].reshape(2 * block_len, wide)
        return lax.shift_right_logical(a, 8), lax.shift_right_logical(b, 8), live, keys

    for p in range(slots_here // 2):
        ra, rb, live, keys = pair(p)
        query = jnp.where(low, q_s[ra], q_s[rb]).astype(BF16)
        scores = lax.dot_general(
            query, keys, (((1,), (1,)), ((), ())), preferred_element_type=F32
        )
        scores = jnp.where(low, scores[:, :block_len], scores[:, block_len:])
        scores = jnp.where(live, scores, MASKED)
        score_s[p] = scores
        top = jnp.broadcast_to(jnp.max(scores, axis=1, keepdims=True), scores.shape)
        max_s[ra] = jnp.maximum(max_s[ra], jnp.where(low, top, MASKED))
        max_s[rb] = jnp.maximum(max_s[rb], jnp.where(low, MASKED, top))

    for r in range(requests):
        top = max_s[r]
        max_s[r] = jnp.maximum(top, pltpu.roll(top, GROUP, 0))

    for p in range(slots_here // 2):
        ra, rb, live, values = pair(p)
        top = jnp.where(low, max_s[ra], max_s[rb])
        weight = jnp.where(live, jnp.exp(score_s[p] - top), 0.0).astype(BF16).astype(F32)
        both = jnp.concatenate(
            [jnp.where(low, weight, 0.0), jnp.where(low, 0.0, weight)], axis=1
        ).astype(BF16)
        out = jnp.dot(both, values, preferred_element_type=F32)
        total = jnp.broadcast_to(jnp.sum(weight, axis=1, keepdims=True), out.shape)
        acc_s[ra] = acc_s[ra] + jnp.where(low, out, 0.0)
        acc_s[rb] = acc_s[rb] + jnp.where(low, 0.0, out)
        sum_s[ra] = sum_s[ra] + jnp.where(low, total, 0.0)
        sum_s[rb] = sum_s[rb] + jnp.where(low, 0.0, total)

    for v in range(requests // 2):
        tiles = []
        for r in (2 * v, 2 * v + 1):
            out = acc_s[r] + pltpu.roll(acc_s[r], GROUP, 0)
            total = sum_s[r] + pltpu.roll(sum_s[r], GROUP, 0)
            tiles.append(
                jnp.where(lane < wide // 4, max_s[r], jnp.where(lane < wide // 2, total, out))
            )
        out_ref[pl.ds(8 * v, 8), :] = jnp.where(low, tiles[0], tiles[1])


def combine_kernel(got_ref, own_ref, w_ref, out_ref):
    rows, wide = got_ref.shape
    lane = lanes((8, wide))
    row = subs((8, wide))
    parts = [got_ref[pl.ds(8 * v, 8), :] for v in range(rows // 8)]
    top = parts[0]
    for part in parts[1:]:
        top = jnp.maximum(top, part)
    own = own_ref[...]
    top = jnp.maximum(jnp.maximum(top, pltpu.roll(top, GROUP, 0)), own)
    mixed = jnp.zeros((8, wide), F32)
    for part in parts:
        weight = jnp.exp(part - top)
        mixed = mixed + jnp.broadcast_to(weight[:, :1], part.shape) * part
    mixed = mixed + pltpu.roll(mixed, GROUP, 0)
    own_weight = jnp.exp(own - top)
    mixed = mixed + jnp.broadcast_to(own_weight[:, :1], own.shape) * jnp.where(
        lane < wide // 2, 1.0, own
    )
    attended = mixed / jnp.broadcast_to(mixed[:, wide // 4 : wide // 4 + 1], mixed.shape)
    swapped = pltpu.roll(attended, wide // 2, 1)
    placed = jnp.where(
        row % 2 == 0,
        jnp.where(lane < wide // 2, swapped, 0.0),
        jnp.where(lane < wide // 2, 0.0, attended),
    )
    chunks = [
        jnp.sum(jnp.where(row // 2 == c, placed, 0.0), axis=0, keepdims=True)
        for c in range(GROUP // 2)
    ]
    line = jnp.broadcast_to(jnp.concatenate(chunks, axis=1), (8, GROUP // 2 * wide)).astype(BF16)
    lines = out_ref.shape[0]
    for v in range(lines // 8):
        at = (8 * v + FIRST_SHARD * GROUP // 2) % lines * wide
        part = jnp.dot(line, w_ref[:, pl.ds(at, 8 * wide)], preferred_element_type=F32)
        tile = jnp.zeros((8, wide), F32)
        for k in range(8):
            tile = jnp.where(row == k, part[:, k * wide : (k + 1) * wide], tile)
        out_ref[pl.ds(8 * v, 8), :] = tile


def exchange(x, axis, parts, first=0):
    shape = x.shape
    x = x.reshape(parts, shape[0] // parts, shape[1])
    groups = [[(i + first) % parts for i in range(parts)]] if first else None
    return lax.all_to_all(
        x, axis, split_axis=0, concat_axis=0, tiled=True, axis_index_groups=groups
    ).reshape(shape)


def per_device(hidden, norm_gain, w_query, w_keyval, w_out, kv_cache, block_slot, lengths):
    slots_here, _, block_len, wide = kv_cache.shape
    head_dim = wide // 2
    requests = block_slot.shape[0]
    shards = lax.axis_size("mp")
    pools = lax.axis_size("pool")
    features = hidden.shape[1]
    lines = features // wide
    rows = exchange(
        pl.pallas_call(
            spread_kernel,
            out_shape=jax.ShapeDtypeStruct((shards * lines, wide), F32),
            in_specs=[HBM],
            out_specs=HBM,
            scratch_shapes=[pltpu.SemaphoreType.DMA((shards,))],
            name="spread",
        )(far(hidden.reshape(lines, wide))),
        "mp",
        shards,
        FIRST_SHARD,
    )
    gain = norm_gain.reshape(shards * lines, wide)

    turn = jax.ShapeDtypeStruct((8, wide), F32)
    w_query, w_keyval, gain = (far(x) for x in (w_query, w_keyval, gain))
    cache = far(kv_cache.reshape(slots_here, block_len, wide))
    lengths, block_slot = far(lengths), far(block_slot)
    half_cache = jax.ShapeDtypeStruct((slots_here // 2, block_len, wide), BF16)
    held_query, held_gain, first_cache, cosine, sine = call(
        functools.partial(prepare_kernel, head_dim),
        "prepare",
        (
            jax.ShapeDtypeStruct(w_query.shape, BF16),
            jax.ShapeDtypeStruct(gain.shape, F32),
            half_cache,
            turn,
            turn,
        ),
        [HBM] * 4,
        [pltpu.SMEM(lengths.shape, jnp.int32), pltpu.SemaphoreType.DMA((4,))],
        limit=8 << 20,
    )(lengths, w_query, gain, cache)

    query = call(
        functools.partial(query_kernel, head_dim),
        "query",
        jax.ShapeDtypeStruct((requests * GROUP, wide), BF16),
        [VMEM] * 5,
    )(rows, held_gain, held_query, cosine, sine)

    queries = exchange(query, "pool", pools, FIRST)

    table, second_cache = call(
        functools.partial(table_kernel, slots_here, block_len),
        "slot_table",
        (jax.ShapeDtypeStruct((slots_here, block_slot.shape[1]), jnp.int32), half_cache),
        [HBM] * 3,
        [
            pltpu.SMEM(lengths.shape, jnp.int32),
            pltpu.VMEM(block_slot.shape, jnp.int32),
            pltpu.SemaphoreType.DMA((3,)),
        ],
    )(lengths, block_slot, cache)
    table = table[:, 0]

    new_kv, own = call(
        functools.partial(keyval_kernel, head_dim),
        "keyval",
        (jax.ShapeDtypeStruct((1, wide), BF16), turn),
        [VMEM] * 4 + [HBM] * 2,
        [
            pltpu.VMEM(w_keyval.shape, BF16),
            pltpu.VMEM((16, wide), BF16),
            pltpu.SemaphoreType.DMA((2,)),
        ],
    )(rows, held_gain, cosine, sine, far(query), w_keyval)
    table, own = lax.optimization_barrier((table, own))

    per_request = pltpu.VMEM((requests, 8, wide), F32)
    partial = call(
        attend_kernel,
        "attend",
        jax.ShapeDtypeStruct((requests * GROUP, wide), F32),
        [SMEM, VMEM, VMEM, VMEM],
        [
            per_request,
            pltpu.VMEM((slots_here // 2, 8, block_len), F32),
            per_request,
            per_request,
            per_request,
        ],
        limit=12 << 20,
    )(table, queries, first_cache, second_cache)

    got = exchange(partial, "pool", pools, FIRST)

    mixed = call(
        combine_kernel,
        "combine",
        jax.ShapeDtypeStruct((shards * lines, wide), F32),
        [VMEM, VMEM, VMEM],
    )(got, own, w_out)

    spread = exchange(mixed, "mp", shards, FIRST_SHARD)
    total = jnp.sum(spread.reshape(shards, features), axis=0, keepdims=True)
    return (hidden + RESIDUAL_SCALE * total, new_kv)


def solution(mesh):
    return jax.shard_map(
        per_device,
        mesh=mesh,
        in_specs=(
            P("pool", "mp"),
            P(),
            P(None, "mp"),
            P(None, "mp"),
            P("mp", None),
            P("pool", "mp", None, None),
            P(),
            P(),
        ),
        out_specs=(P("pool", "mp"), P("pool", "mp")),
        check_vma=False,
    )
```

```python
import functools
import math

import jax
import jax.numpy as jnp
from jax import lax
from jax.experimental import pallas as pl
from jax.experimental.pallas import tpu as pltpu
from jax.sharding import PartitionSpec as P

EPSILON = 1e-05
RESIDUAL_SCALE = 0.22
SCORE_SCALE = 0.015625
ROPE_BASE = 10000000.0
MASKED = -1e30

F32 = jnp.float32
BF16 = jnp.bfloat16
VMEM = pl.BlockSpec(memory_space=pltpu.VMEM)
SMEM = pl.BlockSpec(memory_space=pltpu.SMEM)
HBM = pl.BlockSpec(memory_space=pltpu.HBM)

GROUP = 4

FIRST = 44
FIRST_SHARD = 4


def far(x):
    return pltpu.with_memory_space_constraint(x, pltpu.HBM)


def lanes(shape):
    return lax.broadcasted_iota(jnp.int32, shape, len(shape) - 1)


def subs(shape):
    return lax.broadcasted_iota(jnp.int32, shape, len(shape) - 2)


def call(body, name, out_shape, in_specs, scratch=(), limit=4 << 20):
    many = isinstance(out_shape, tuple)
    return pl.pallas_call(
        body,
        out_shape=out_shape,
        in_specs=in_specs,
        out_specs=(VMEM,) * len(out_shape) if many else VMEM,
        scratch_shapes=list(scratch),
        compiler_params=pltpu.CompilerParams(vmem_limit_bytes=limit),
        name=name,
    )


def sine_cosine(angle):
    turn = jnp.floor(angle * (2.0 / math.pi) + 0.5)
    x = ((angle - turn * 1.5703125) - turn * 4.837512969970703e-4) - turn * 7.54978995489188e-8
    z = x * x
    sine = ((-1.9515295891e-4 * z + 8.3321608736e-3) * z - 1.6666654611e-1) * z * x + x
    cosine = ((2.443315711809948e-5 * z - 1.388731625493765e-3) * z + 4.166664568298827e-2) * z * z
    cosine = cosine - 0.5 * z + 1.0
    quadrant = turn.astype(jnp.int32) & 3
    odd = (quadrant & 1) == 1
    out_sine = jnp.where(odd, cosine, sine)
    out_cosine = jnp.where(odd, sine, cosine)
    out_sine = jnp.where(quadrant >= 2, -out_sine, out_sine)
    out_cosine = jnp.where((quadrant == 1) | (quadrant == 2), -out_cosine, out_cosine)
    return out_sine, out_cosine


def rotation(position, head_dim, width):
    half = head_dim // 2
    lane = lanes((8, width))
    pair = lane % half
    inverse = jnp.zeros((8, width), F32)
    for i in range(half):
        inverse = jnp.where(pair == i, ROPE_BASE ** (-2.0 * i / head_dim), inverse)
    sine, cosine = sine_cosine(position.astype(F32) * inverse)
    return cosine, jnp.where(lane % head_dim < half, -sine, sine)


def rope(x, cosine, sine, half):
    ahead = pltpu.roll(x, x.shape[1] - half, 1)
    behind = pltpu.roll(x, half, 1)
    first = lanes(x.shape) % (2 * half) < half
    return x * cosine + jnp.where(first, ahead, behind) * sine


def normalise(rows_ref, gain_ref):
    count = rows_ref.shape[0]
    x = rows_ref[...]
    total = jnp.sum(jnp.sum(x * x, axis=0, keepdims=True), axis=1, keepdims=True)
    scale = lax.rsqrt(total * (1.0 / x.size) + EPSILON)
    half = count // 2
    even = pl.ds(0, half, stride=2)
    odd = pl.ds(1, half, stride=2)
    left = pltpu.roll(rows_ref[even, :], FIRST_SHARD, 0) * scale * gain_ref[even, :]
    right = pltpu.roll(rows_ref[odd, :], FIRST_SHARD, 0) * scale * gain_ref[odd, :]
    return jnp.concatenate([left, right], axis=1)


def project(normed, weight_ref):
    chunks, wide = normed.shape
    row = subs(normed.shape)
    out = None
    for j in range(chunks):
        part = jnp.dot(
            jnp.where(row == j, normed, 0.0).astype(BF16),
            weight_ref[pl.ds(j * wide, wide), :],
            preferred_element_type=F32,
        )
        out = part if out is None else out + part
    return jnp.broadcast_to(jnp.sum(out, axis=0, keepdims=True), out.shape)


def fetch(sources, targets, sems):
    copies = [pltpu.make_async_copy(s, t, sems.at[i]) for i, (s, t) in enumerate(zip(sources, targets))]
    for copy in copies:
        copy.start()
    return copies


def prepare_kernel(head_dim, x_ref, lengths_ref, w_ref, gain_ref, *rest):
    spread_ref, held_w_ref, held_gain_ref, cos_ref, sin_ref, near_x, near_lengths, sems = rest
    copies = fetch(
        (x_ref, lengths_ref, w_ref, gain_ref),
        (near_x, near_lengths, held_w_ref, held_gain_ref),
        sems,
    )
    copies[1].wait()
    position = near_lengths[lax.axis_index("pool")]
    cos_ref[...], sin_ref[...] = rotation(position, head_dim, 2 * head_dim)
    copies[0].wait()
    size = near_x.shape[0]
    for i in range(spread_ref.shape[0] // size):
        spread_ref[pl.ds(i * size, size), :] = near_x[...]
    copies[2].wait()
    copies[3].wait()


def query_kernel(head_dim, rows_ref, gain_ref, w_ref, cos_ref, sin_ref, out_ref):
    wide = 2 * head_dim
    cosine, sine = cos_ref[...], sin_ref[...]
    query = project(normalise(rows_ref, gain_ref), w_ref)
    row = subs((8, wide)) % GROUP
    tile = jnp.zeros((8, wide), F32)
    for c in range(GROUP // 2):
        part = rope(query[:, c * wide : (c + 1) * wide], cosine, sine, head_dim // 2)
        tile = jnp.where(row == 2 * c, part, tile)
        tile = jnp.where(row == 2 * c + 1, pltpu.roll(part, head_dim, 1), tile)
    tile = tile.astype(BF16).astype(F32) * SCORE_SCALE
    tile = jnp.where(lanes(tile.shape) < head_dim, tile, 0.0).astype(BF16)
    for v in range(out_ref.shape[0] // 8):
        out_ref[pl.ds(8 * v, 8), :] = tile


def keyval_kernel(
    head_dim, rows_ref, gain_ref, cos_ref, sin_ref, query_hbm, w_hbm, kv_ref, own_ref, w_ref, query_ref, sems
):
    copies = fetch((w_hbm, query_hbm.at[pl.ds(0, query_ref.shape[0])]), (w_ref, query_ref), sems)
    normed = normalise(rows_ref, gain_ref)
    for copy in copies:
        copy.wait()
    keyval = project(normed, w_ref)
    is_key = lanes(keyval.shape) < head_dim
    turned = rope(keyval, cos_ref[...], sin_ref[...], head_dim // 2)
    both = jnp.where(is_key, turned, keyval).astype(BF16)
    kv_ref[...] = both[:1]
    both = both.astype(F32)
    score = jnp.sum(query_ref[:8, :].astype(F32) * both, axis=1, keepdims=True)
    own_ref[...] = jnp.where(is_key, score, both)


def table_kernel(
    slots_here, block_len, lengths_hbm, slot_hbm, cache_ref, out_ref, held_ref, lengths_ref, slot_ref, sems
):
    copies = fetch((lengths_hbm, slot_hbm, cache_ref), (lengths_ref, slot_ref, held_ref), sems)
    copies[0].wait()
    copies[1].wait()
    requests, blocks = slot_ref.shape
    base = lax.axis_index("pool") * slots_here
    sub = subs((8, blocks))
    lane = lanes((8, blocks))
    wanted, payload = [], []
    for v in range(requests // 8):
        length = jnp.zeros((8, blocks), jnp.int32)
        for i in range(8):
            length = jnp.where(sub == i, lengths_ref[8 * v + i], length)
        limit = length - lane * block_len
        here = slot_ref[pl.ds(8 * v, 8), :] - base
        wanted.append(jnp.where(limit > 0, here, -1))
        payload.append(
            ((sub + 8 * v + requests - FIRST) % requests) * 256 + jnp.minimum(limit, block_len)
        )
    for tile in range(slots_here // 8):
        picked = jnp.zeros((8, blocks), jnp.int32)
        for i in range(8):
            found = jnp.zeros((8, blocks), jnp.int32)
            for w, p in zip(wanted, payload):
                found = jnp.where(w == 8 * tile + i, p, found)
            picked = jnp.where(sub == i, jnp.max(found, axis=0, keepdims=True), picked)
        out_ref[pl.ds(8 * tile, 8), :] = jnp.broadcast_to(
            jnp.max(picked.astype(F32), axis=1, keepdims=True), (8, blocks)
        ).astype(jnp.int32)
    copies[2].wait()


def attend_kernel(
    tab_ref, query_ref, kv_ref, out_ref, q_s, score_s, max_s, sum_s, acc_s
):
    slots_here, block_len, wide = kv_ref.shape
    requests = query_ref.shape[0] // GROUP
    low = subs((8, wide)) < GROUP
    token = lanes((8, block_len))
    lane = lanes((8, wide))
    for v in range(requests // 2):
        tile = query_ref[pl.ds(8 * v, 8), :].astype(F32)
        other = pltpu.roll(tile, GROUP, 0)
        q_s[2 * v] = jnp.where(low, tile, other)
        q_s[2 * v + 1] = jnp.where(low, other, tile)
    max_s[...] = jnp.full_like(max_s, MASKED)
    sum_s[...] = jnp.zeros_like(sum_s)
    acc_s[...] = jnp.zeros_like(acc_s)

    def pair(p):
        a, b = tab_ref[2 * p], tab_ref[2 * p + 1]
        live = token < jnp.where(low, a & 255, b & 255)
        keys = kv_ref[pl.ds(2 * p, 2)].reshape(2 * block_len, wide)
        return lax.shift_right_logical(a, 8), lax.shift_right_logical(b, 8), live, keys

    for p in range(slots_here // 2):
        ra, rb, live, keys = pair(p)
        query = jnp.where(low, q_s[ra], q_s[rb]).astype(BF16)
        scores = lax.dot_general(
            query, keys, (((1,), (1,)), ((), ())), preferred_element_type=F32
        )
        scores = jnp.where(low, scores[:, :block_len], scores[:, block_len:])
        scores = jnp.where(live, scores, MASKED)
        score_s[p] = scores
        top = jnp.broadcast_to(jnp.max(scores, axis=1, keepdims=True), scores.shape)
        max_s[ra] = jnp.maximum(max_s[ra], jnp.where(low, top, MASKED))
        max_s[rb] = jnp.maximum(max_s[rb], jnp.where(low, MASKED, top))

    for r in range(requests):
        top = max_s[r]
        max_s[r] = jnp.maximum(top, pltpu.roll(top, GROUP, 0))

    for p in range(slots_here // 2):
        ra, rb, live, values = pair(p)
        top = jnp.where(low, max_s[ra], max_s[rb])
        weight = jnp.where(live, jnp.exp(score_s[p] - top), 0.0).astype(BF16).astype(F32)
        both = jnp.concatenate(
            [jnp.where(low, weight, 0.0), jnp.where(low, 0.0, weight)], axis=1
        ).astype(BF16)
        out = jnp.dot(both, values, preferred_element_type=F32)
        total = jnp.broadcast_to(jnp.sum(weight, axis=1, keepdims=True), out.shape)
        acc_s[ra] = acc_s[ra] + jnp.where(low, out, 0.0)
        acc_s[rb] = acc_s[rb] + jnp.where(low, 0.0, out)
        sum_s[ra] = sum_s[ra] + jnp.where(low, total, 0.0)
        sum_s[rb] = sum_s[rb] + jnp.where(low, 0.0, total)

    for v in range(requests // 2):
        tiles = []
        for r in (2 * v, 2 * v + 1):
            out = acc_s[r] + pltpu.roll(acc_s[r], GROUP, 0)
            total = sum_s[r] + pltpu.roll(sum_s[r], GROUP, 0)
            tiles.append(
                jnp.where(lane < wide // 4, max_s[r], jnp.where(lane < wide // 2, total, out))
            )
        out_ref[pl.ds(8 * v, 8), :] = jnp.where(low, tiles[0], tiles[1])


def combine_kernel(got_ref, own_ref, w_ref, out_ref):
    rows, wide = got_ref.shape
    lane = lanes((8, wide))
    row = subs((8, wide))
    parts = [got_ref[pl.ds(8 * v, 8), :] for v in range(rows // 8)]
    top = parts[0]
    for part in parts[1:]:
        top = jnp.maximum(top, part)
    own = own_ref[...]
    top = jnp.maximum(jnp.maximum(top, pltpu.roll(top, GROUP, 0)), own)
    mixed = jnp.zeros((8, wide), F32)
    for part in parts:
        weight = jnp.exp(part - top)
        mixed = mixed + jnp.broadcast_to(weight[:, :1], part.shape) * part
    mixed = mixed + pltpu.roll(mixed, GROUP, 0)
    own_weight = jnp.exp(own - top)
    mixed = mixed + jnp.broadcast_to(own_weight[:, :1], own.shape) * jnp.where(
        lane < wide // 2, 1.0, own
    )
    attended = mixed / jnp.broadcast_to(mixed[:, wide // 4 : wide // 4 + 1], mixed.shape)
    swapped = pltpu.roll(attended, wide // 2, 1)
    placed = jnp.where(
        row % 2 == 0,
        jnp.where(lane < wide // 2, swapped, 0.0),
        jnp.where(lane < wide // 2, 0.0, attended),
    )
    chunks = [
        jnp.sum(jnp.where(row // 2 == c, placed, 0.0), axis=0, keepdims=True)
        for c in range(GROUP // 2)
    ]
    line = jnp.broadcast_to(jnp.concatenate(chunks, axis=1), (8, GROUP // 2 * wide)).astype(BF16)
    lines = out_ref.shape[0]
    for v in range(lines // 8):
        at = (8 * v + FIRST_SHARD * GROUP // 2) % lines * wide
        part = jnp.dot(line, w_ref[:, pl.ds(at, 8 * wide)], preferred_element_type=F32)
        tile = jnp.zeros((8, wide), F32)
        for k in range(8):
            tile = jnp.where(row == k, part[:, k * wide : (k + 1) * wide], tile)
        out_ref[pl.ds(8 * v, 8), :] = tile


def exchange(x, axis, parts, first=0):
    shape = x.shape
    x = x.reshape(parts, shape[0] // parts, shape[1])
    groups = [[(i + first) % parts for i in range(parts)]] if first else None
    return lax.all_to_all(
        x, axis, split_axis=0, concat_axis=0, tiled=True, axis_index_groups=groups
    ).reshape(shape)


def per_device(hidden, norm_gain, w_query, w_keyval, w_out, kv_cache, block_slot, lengths):
    slots_here, _, block_len, wide = kv_cache.shape
    head_dim = wide // 2
    requests = block_slot.shape[0]
    shards = lax.axis_size("mp")
    pools = lax.axis_size("pool")
    features = hidden.shape[1]
    lines = features // wide
    gain = far(norm_gain.reshape(shards * lines, wide))
    cache = far(kv_cache.reshape(slots_here, block_len, wide))
    line = far(hidden.reshape(lines, wide))
    w_query, w_keyval, lengths, block_slot = (
        far(x) for x in (w_query, w_keyval, lengths, block_slot)
    )
    turn = jax.ShapeDtypeStruct((8, wide), F32)
    spread_rows, held_query, held_gain, cosine, sine = call(
        functools.partial(prepare_kernel, head_dim),
        "prepare",
        (
            jax.ShapeDtypeStruct((shards * lines, wide), F32),
            jax.ShapeDtypeStruct(w_query.shape, BF16),
            jax.ShapeDtypeStruct(gain.shape, F32),
            turn,
            turn,
        ),
        [HBM] * 4,
        [
            pltpu.VMEM((lines, wide), F32),
            pltpu.SMEM(lengths.shape, jnp.int32),
            pltpu.SemaphoreType.DMA((4,)),
        ],
    )(line, lengths, w_query, gain)

    rows = exchange(spread_rows, "mp", shards, FIRST_SHARD)

    query = call(
        functools.partial(query_kernel, head_dim),
        "query",
        jax.ShapeDtypeStruct((requests * GROUP, wide), BF16),
        [VMEM] * 5,
    )(rows, held_gain, held_query, cosine, sine)

    queries = exchange(query, "pool", pools, FIRST)

    lengths, block_slot, rows = lax.optimization_barrier((lengths, block_slot, rows))
    table, held_cache = call(
        functools.partial(table_kernel, slots_here, block_len),
        "slot_table",
        (
            jax.ShapeDtypeStruct((slots_here, block_slot.shape[1]), jnp.int32),
            jax.ShapeDtypeStruct(cache.shape, BF16),
        ),
        [HBM] * 3,
        [
            pltpu.SMEM(lengths.shape, jnp.int32),
            pltpu.VMEM(block_slot.shape, jnp.int32),
            pltpu.SemaphoreType.DMA((3,)),
        ],
    )(far(lengths), far(block_slot), cache)
    table = table[:, 0]

    new_kv, own = call(
        functools.partial(keyval_kernel, head_dim),
        "keyval",
        (jax.ShapeDtypeStruct((1, wide), BF16), turn),
        [VMEM] * 4 + [HBM] * 2,
        [
            pltpu.VMEM(w_keyval.shape, BF16),
            pltpu.VMEM((16, wide), BF16),
            pltpu.SemaphoreType.DMA((2,)),
        ],
    )(rows, held_gain, cosine, sine, far(query), w_keyval)
    table, own = lax.optimization_barrier((table, own))

    per_request = pltpu.VMEM((requests, 8, wide), F32)
    partial = call(
        attend_kernel,
        "attend",
        jax.ShapeDtypeStruct((requests * GROUP, wide), F32),
        [SMEM, VMEM, VMEM],
        [
            per_request,
            pltpu.VMEM((slots_here // 2, 8, block_len), F32),
            per_request,
            per_request,
            per_request,
        ],
        limit=12 << 20,
    )(table, queries, held_cache)

    got = exchange(partial, "pool", pools, FIRST)

    mixed = call(
        combine_kernel,
        "combine",
        jax.ShapeDtypeStruct((shards * lines, wide), F32),
        [VMEM, VMEM, VMEM],
    )(got, own, w_out)

    spread = exchange(mixed, "mp", shards, FIRST_SHARD)
    total = jnp.sum(spread.reshape(shards, features), axis=0, keepdims=True)
    return (hidden + RESIDUAL_SCALE * total, new_kv)


def solution(mesh):
    return jax.shard_map(
        per_device,
        mesh=mesh,
        in_specs=(
            P("pool", "mp"),
            P(),
            P(None, "mp"),
            P(None, "mp"),
            P("mp", None),
            P("pool", "mp", None, None),
            P(),
            P(),
        ),
        out_specs=(P("pool", "mp"), P("pool", "mp")),
        check_vma=False,
    )
```

```python
import functools
import math

import jax
import jax.numpy as jnp
from jax import lax
from jax.experimental import pallas as pl
from jax.experimental.pallas import tpu as pltpu
from jax.sharding import PartitionSpec as P

EPSILON = 1e-05
RESIDUAL_SCALE = 0.22
SCORE_SCALE = 0.015625
ROPE_BASE = 10000000.0
MASKED = -1e30

F32 = jnp.float32
BF16 = jnp.bfloat16
VMEM = pl.BlockSpec(memory_space=pltpu.VMEM)
SMEM = pl.BlockSpec(memory_space=pltpu.SMEM)
HBM = pl.BlockSpec(memory_space=pltpu.HBM)

GROUP = 4

FIRST = 36
FIRST_SHARD = 4


def far(x):
    return pltpu.with_memory_space_constraint(x, pltpu.HBM)


def lanes(shape):
    return lax.broadcasted_iota(jnp.int32, shape, len(shape) - 1)


def subs(shape):
    return lax.broadcasted_iota(jnp.int32, shape, len(shape) - 2)


def call(body, name, out_shape, in_specs, scratch=(), limit=4 << 20):
    many = isinstance(out_shape, tuple)
    return pl.pallas_call(
        body,
        out_shape=out_shape,
        in_specs=in_specs,
        out_specs=(VMEM,) * len(out_shape) if many else VMEM,
        scratch_shapes=list(scratch),
        compiler_params=pltpu.CompilerParams(vmem_limit_bytes=limit),
        name=name,
    )


def sine_cosine(angle):
    turn = jnp.floor(angle * (2.0 / math.pi) + 0.5)
    x = ((angle - turn * 1.5703125) - turn * 4.837512969970703e-4) - turn * 7.54978995489188e-8
    z = x * x
    sine = ((-1.9515295891e-4 * z + 8.3321608736e-3) * z - 1.6666654611e-1) * z * x + x
    cosine = ((2.443315711809948e-5 * z - 1.388731625493765e-3) * z + 4.166664568298827e-2) * z * z
    cosine = cosine - 0.5 * z + 1.0
    quadrant = turn.astype(jnp.int32) & 3
    odd = (quadrant & 1) == 1
    out_sine = jnp.where(odd, cosine, sine)
    out_cosine = jnp.where(odd, sine, cosine)
    out_sine = jnp.where(quadrant >= 2, -out_sine, out_sine)
    out_cosine = jnp.where((quadrant == 1) | (quadrant == 2), -out_cosine, out_cosine)
    return out_sine, out_cosine


def rotation(position, head_dim, width):
    half = head_dim // 2
    lane = lanes((8, width))
    pair = lane % half
    inverse = jnp.zeros((8, width), F32)
    for i in range(half):
        inverse = jnp.where(pair == i, ROPE_BASE ** (-2.0 * i / head_dim), inverse)
    sine, cosine = sine_cosine(position.astype(F32) * inverse)
    return cosine, jnp.where(lane % head_dim < half, -sine, sine)


def rope(x, cosine, sine, half):
    ahead = pltpu.roll(x, x.shape[1] - half, 1)
    behind = pltpu.roll(x, half, 1)
    first = lanes(x.shape) % (2 * half) < half
    return x * cosine + jnp.where(first, ahead, behind) * sine


def normalise(rows_ref, gain_ref):
    count = rows_ref.shape[0]
    x = rows_ref[...]
    total = jnp.sum(jnp.sum(x * x, axis=0, keepdims=True), axis=1, keepdims=True)
    scale = lax.rsqrt(total * (1.0 / x.size) + EPSILON)
    half = count // 2
    even = pl.ds(0, half, stride=2)
    odd = pl.ds(1, half, stride=2)
    left = pltpu.roll(rows_ref[even, :], FIRST_SHARD, 0) * scale * gain_ref[even, :]
    right = pltpu.roll(rows_ref[odd, :], FIRST_SHARD, 0) * scale * gain_ref[odd, :]
    return jnp.concatenate([left, right], axis=1)


def project(normed, weight_ref):
    chunks, wide = normed.shape
    row = subs(normed.shape)
    out = None
    for j in range(chunks):
        part = jnp.dot(
            jnp.where(row == j, normed, 0.0).astype(BF16),
            weight_ref[pl.ds(j * wide, wide), :],
            preferred_element_type=F32,
        )
        out = part if out is None else out + part
    return jnp.broadcast_to(jnp.sum(out, axis=0, keepdims=True), out.shape)


def fetch(sources, targets, sems):
    copies = [pltpu.make_async_copy(s, t, sems.at[i]) for i, (s, t) in enumerate(zip(sources, targets))]
    for copy in copies:
        copy.start()
    return copies


def prepare_kernel(head_dim, x_ref, lengths_ref, w_ref, gain_ref, *rest):
    spread_ref, held_w_ref, held_gain_ref, cos_ref, sin_ref, near_x, near_lengths, sems = rest
    copies = fetch(
        (x_ref, lengths_ref, w_ref, gain_ref),
        (near_x, near_lengths, held_w_ref, held_gain_ref),
        sems,
    )
    copies[1].wait()
    position = near_lengths[lax.axis_index("pool")]
    cos_ref[...], sin_ref[...] = rotation(position, head_dim, 2 * head_dim)
    copies[0].wait()
    size = near_x.shape[0]
    for i in range(spread_ref.shape[0] // size):
        spread_ref[pl.ds(i * size, size), :] = near_x[...]
    copies[2].wait()
    copies[3].wait()


def query_kernel(head_dim, rows_ref, gain_ref, w_ref, cos_ref, sin_ref, out_ref):
    wide = 2 * head_dim
    cosine, sine = cos_ref[...], sin_ref[...]
    query = project(normalise(rows_ref, gain_ref), w_ref)
    row = subs((8, wide)) % GROUP
    tile = jnp.zeros((8, wide), F32)
    for c in range(GROUP // 2):
        part = rope(query[:, c * wide : (c + 1) * wide], cosine, sine, head_dim // 2)
        tile = jnp.where(row == 2 * c, part, tile)
        tile = jnp.where(row == 2 * c + 1, pltpu.roll(part, head_dim, 1), tile)
    tile = tile.astype(BF16).astype(F32) * SCORE_SCALE
    tile = jnp.where(lanes(tile.shape) < head_dim, tile, 0.0).astype(BF16)
    for v in range(out_ref.shape[0] // 8):
        out_ref[pl.ds(8 * v, 8), :] = tile


def keyval_kernel(
    head_dim, rows_ref, gain_ref, cos_ref, sin_ref, query_hbm, w_hbm, kv_ref, own_ref, w_ref, query_ref, sems
):
    copies = fetch((w_hbm, query_hbm.at[pl.ds(0, query_ref.shape[0])]), (w_ref, query_ref), sems)
    normed = normalise(rows_ref, gain_ref)
    for copy in copies:
        copy.wait()
    keyval = project(normed, w_ref)
    is_key = lanes(keyval.shape) < head_dim
    turned = rope(keyval, cos_ref[...], sin_ref[...], head_dim // 2)
    both = jnp.where(is_key, turned, keyval).astype(BF16)
    kv_ref[...] = both[:1]
    both = both.astype(F32)
    score = jnp.sum(query_ref[:8, :].astype(F32) * both, axis=1, keepdims=True)
    own_ref[...] = jnp.where(is_key, score, both)


def table_kernel(
    slots_here, block_len, lengths_hbm, slot_hbm, cache_ref, out_ref, held_ref, lengths_ref, slot_ref, sems
):
    copies = fetch((lengths_hbm, slot_hbm, cache_ref), (lengths_ref, slot_ref, held_ref), sems)
    copies[0].wait()
    copies[1].wait()
    requests, blocks = slot_ref.shape
    base = lax.axis_index("pool") * slots_here
    sub = subs((8, blocks))
    lane = lanes((8, blocks))
    wanted, payload = [], []
    for v in range(requests // 8):
        length = jnp.zeros((8, blocks), jnp.int32)
        for i in range(8):
            length = jnp.where(sub == i, lengths_ref[8 * v + i], length)
        limit = length - lane * block_len
        here = slot_ref[pl.ds(8 * v, 8), :] - base
        wanted.append(jnp.where(limit > 0, here, -1))
        payload.append(
            ((sub + 8 * v + requests - FIRST) % requests) * 256 + jnp.minimum(limit, block_len)
        )
    for tile in range(slots_here // 8):
        picked = jnp.zeros((8, blocks), jnp.int32)
        for i in range(8):
            found = jnp.zeros((8, blocks), jnp.int32)
            for w, p in zip(wanted, payload):
                found = jnp.where(w == 8 * tile + i, p, found)
            picked = jnp.where(sub == i, jnp.max(found, axis=0, keepdims=True), picked)
        out_ref[pl.ds(8 * tile, 8), :] = jnp.broadcast_to(
            jnp.max(picked.astype(F32), axis=1, keepdims=True), (8, blocks)
        ).astype(jnp.int32)
    copies[2].wait()


def attend_kernel(
    tab_ref, query_ref, kv_ref, out_ref, q_s, score_s, max_s, sum_s, acc_s
):
    slots_here, block_len, wide = kv_ref.shape
    requests = query_ref.shape[0] // GROUP
    low = subs((8, wide)) < GROUP
    token = lanes((8, block_len))
    lane = lanes((8, wide))
    for v in range(requests // 2):
        tile = query_ref[pl.ds(8 * v, 8), :].astype(F32)
        other = pltpu.roll(tile, GROUP, 0)
        q_s[2 * v] = jnp.where(low, tile, other)
        q_s[2 * v + 1] = jnp.where(low, other, tile)
    max_s[...] = jnp.full_like(max_s, MASKED)
    sum_s[...] = jnp.zeros_like(sum_s)
    acc_s[...] = jnp.zeros_like(acc_s)

    def pair(p):
        a, b = tab_ref[2 * p], tab_ref[2 * p + 1]
        live = token < jnp.where(low, a & 255, b & 255)
        keys = kv_ref[pl.ds(2 * p, 2)].reshape(2 * block_len, wide)
        return lax.shift_right_logical(a, 8), lax.shift_right_logical(b, 8), live, keys

    for p in range(slots_here // 2):
        ra, rb, live, keys = pair(p)
        query = jnp.where(low, q_s[ra], q_s[rb]).astype(BF16)
        scores = lax.dot_general(
            query, keys, (((1,), (1,)), ((), ())), preferred_element_type=F32
        )
        scores = jnp.where(low, scores[:, :block_len], scores[:, block_len:])
        scores = jnp.where(live, scores, MASKED)
        score_s[p] = scores
        top = jnp.broadcast_to(jnp.max(scores, axis=1, keepdims=True), scores.shape)
        max_s[ra] = jnp.maximum(max_s[ra], jnp.where(low, top, MASKED))
        max_s[rb] = jnp.maximum(max_s[rb], jnp.where(low, MASKED, top))

    for r in range(requests):
        top = max_s[r]
        max_s[r] = jnp.maximum(top, pltpu.roll(top, GROUP, 0))

    for p in range(slots_here // 2):
        ra, rb, live, values = pair(p)
        top = jnp.where(low, max_s[ra], max_s[rb])
        weight = jnp.where(live, jnp.exp(score_s[p] - top), 0.0).astype(BF16).astype(F32)
        both = jnp.concatenate(
            [jnp.where(low, weight, 0.0), jnp.where(low, 0.0, weight)], axis=1
        ).astype(BF16)
        out = jnp.dot(both, values, preferred_element_type=F32)
        total = jnp.broadcast_to(jnp.sum(weight, axis=1, keepdims=True), out.shape)
        acc_s[ra] = acc_s[ra] + jnp.where(low, out, 0.0)
        acc_s[rb] = acc_s[rb] + jnp.where(low, 0.0, out)
        sum_s[ra] = sum_s[ra] + jnp.where(low, total, 0.0)
        sum_s[rb] = sum_s[rb] + jnp.where(low, 0.0, total)

    for v in range(requests // 2):
        tiles = []
        for r in (2 * v, 2 * v + 1):
            out = acc_s[r] + pltpu.roll(acc_s[r], GROUP, 0)
            total = sum_s[r] + pltpu.roll(sum_s[r], GROUP, 0)
            tiles.append(
                jnp.where(lane < wide // 4, max_s[r], jnp.where(lane < wide // 2, total, out))
            )
        out_ref[pl.ds(8 * v, 8), :] = jnp.where(low, tiles[0], tiles[1])


def combine_kernel(got_ref, own_ref, w_ref, out_ref):
    rows, wide = got_ref.shape
    lane = lanes((8, wide))
    row = subs((8, wide))
    parts = [got_ref[pl.ds(8 * v, 8), :] for v in range(rows // 8)]
    top = parts[0]
    for part in parts[1:]:
        top = jnp.maximum(top, part)
    own = own_ref[...]
    top = jnp.maximum(jnp.maximum(top, pltpu.roll(top, GROUP, 0)), own)
    mixed = jnp.zeros((8, wide), F32)
    for part in parts:
        weight = jnp.exp(part - top)
        mixed = mixed + jnp.broadcast_to(weight[:, :1], part.shape) * part
    mixed = mixed + pltpu.roll(mixed, GROUP, 0)
    own_weight = jnp.exp(own - top)
    mixed = mixed + jnp.broadcast_to(own_weight[:, :1], own.shape) * jnp.where(
        lane < wide // 2, 1.0, own
    )
    attended = mixed / jnp.broadcast_to(mixed[:, wide // 4 : wide // 4 + 1], mixed.shape)
    swapped = pltpu.roll(attended, wide // 2, 1)
    placed = jnp.where(
        row % 2 == 0,
        jnp.where(lane < wide // 2, swapped, 0.0),
        jnp.where(lane < wide // 2, 0.0, attended),
    )
    chunks = [
        jnp.sum(jnp.where(row // 2 == c, placed, 0.0), axis=0, keepdims=True)
        for c in range(GROUP // 2)
    ]
    line = jnp.broadcast_to(jnp.concatenate(chunks, axis=1), (8, GROUP // 2 * wide)).astype(BF16)
    lines = out_ref.shape[0]
    for v in range(lines // 8):
        at = (8 * v + FIRST_SHARD * GROUP // 2) % lines * wide
        part = jnp.dot(line, w_ref[:, pl.ds(at, 8 * wide)], preferred_element_type=F32)
        tile = jnp.zeros((8, wide), F32)
        for k in range(8):
            tile = jnp.where(row == k, part[:, k * wide : (k + 1) * wide], tile)
        out_ref[pl.ds(8 * v, 8), :] = tile


def exchange(x, axis, parts, first=0):
    shape = x.shape
    x = x.reshape(parts, shape[0] // parts, shape[1])
    groups = [[(i + first) % parts for i in range(parts)]] if first else None
    return lax.all_to_all(
        x, axis, split_axis=0, concat_axis=0, tiled=True, axis_index_groups=groups
    ).reshape(shape)


def per_device(hidden, norm_gain, w_query, w_keyval, w_out, kv_cache, block_slot, lengths):
    slots_here, _, block_len, wide = kv_cache.shape
    head_dim = wide // 2
    requests = block_slot.shape[0]
    shards = lax.axis_size("mp")
    pools = lax.axis_size("pool")
    features = hidden.shape[1]
    lines = features // wide
    gain = far(norm_gain.reshape(shards * lines, wide))
    cache = far(kv_cache.reshape(slots_here, block_len, wide))
    line = far(hidden.reshape(lines, wide))
    w_query, w_keyval, lengths, block_slot = (
        far(x) for x in (w_query, w_keyval, lengths, block_slot)
    )
    turn = jax.ShapeDtypeStruct((8, wide), F32)
    spread_rows, held_query, held_gain, cosine, sine = call(
        functools.partial(prepare_kernel, head_dim),
        "prepare",
        (
            jax.ShapeDtypeStruct((shards * lines, wide), F32),
            jax.ShapeDtypeStruct(w_query.shape, BF16),
            jax.ShapeDtypeStruct(gain.shape, F32),
            turn,
            turn,
        ),
        [HBM] * 4,
        [
            pltpu.VMEM((lines, wide), F32),
            pltpu.SMEM(lengths.shape, jnp.int32),
            pltpu.SemaphoreType.DMA((4,)),
        ],
    )(line, lengths, w_query, gain)

    rows = exchange(spread_rows, "mp", shards, FIRST_SHARD)

    query = call(
        functools.partial(query_kernel, head_dim),
        "query",
        jax.ShapeDtypeStruct((requests * GROUP, wide), BF16),
        [VMEM] * 5,
    )(rows, held_gain, held_query, cosine, sine)

    queries = exchange(query, "pool", pools, FIRST)

    lengths, block_slot, rows = lax.optimization_barrier((lengths, block_slot, rows))
    table, held_cache = call(
        functools.partial(table_kernel, slots_here, block_len),
        "slot_table",
        (
            jax.ShapeDtypeStruct((slots_here, block_slot.shape[1]), jnp.int32),
            jax.ShapeDtypeStruct(cache.shape, BF16),
        ),
        [HBM] * 3,
        [
            pltpu.SMEM(lengths.shape, jnp.int32),
            pltpu.VMEM(block_slot.shape, jnp.int32),
            pltpu.SemaphoreType.DMA((3,)),
        ],
    )(far(lengths), far(block_slot), cache)
    table = table[:, 0]

    new_kv, own = call(
        functools.partial(keyval_kernel, head_dim),
        "keyval",
        (jax.ShapeDtypeStruct((1, wide), BF16), turn),
        [VMEM] * 4 + [HBM] * 2,
        [
            pltpu.VMEM(w_keyval.shape, BF16),
            pltpu.VMEM((16, wide), BF16),
            pltpu.SemaphoreType.DMA((2,)),
        ],
    )(rows, held_gain, cosine, sine, far(query), w_keyval)
    table, own = lax.optimization_barrier((table, own))

    per_request = pltpu.VMEM((requests, 8, wide), F32)
    partial = call(
        attend_kernel,
        "attend",
        jax.ShapeDtypeStruct((requests * GROUP, wide), F32),
        [SMEM, VMEM, VMEM],
        [
            per_request,
            pltpu.VMEM((slots_here // 2, 8, block_len), F32),
            per_request,
            per_request,
            per_request,
        ],
        limit=12 << 20,
    )(table, queries, held_cache)

    got = exchange(partial, "pool", pools, FIRST)

    mixed = call(
        combine_kernel,
        "combine",
        jax.ShapeDtypeStruct((shards * lines, wide), F32),
        [VMEM, VMEM, VMEM],
    )(got, own, w_out)

    spread = exchange(mixed, "mp", shards, FIRST_SHARD)
    total = jnp.sum(spread.reshape(shards, features), axis=0, keepdims=True)
    return (hidden + RESIDUAL_SCALE * total, new_kv)


def solution(mesh):
    return jax.shard_map(
        per_device,
        mesh=mesh,
        in_specs=(
            P("pool", "mp"),
            P(),
            P(None, "mp"),
            P(None, "mp"),
            P("mp", None),
            P("pool", "mp", None, None),
            P(),
            P(),
        ),
        out_specs=(P("pool", "mp"), P("pool", "mp")),
        check_vma=False,
    )
```

```python
import functools
import math

import jax
import jax.numpy as jnp
from jax import lax
from jax.experimental import pallas as pl
from jax.experimental.pallas import tpu as pltpu
from jax.sharding import PartitionSpec as P

EPSILON = 1e-05
RESIDUAL_SCALE = 0.22
SCORE_SCALE = 0.015625
ROPE_BASE = 10000000.0
MASKED = -1e30

F32 = jnp.float32
BF16 = jnp.bfloat16
VMEM = pl.BlockSpec(memory_space=pltpu.VMEM)
SMEM = pl.BlockSpec(memory_space=pltpu.SMEM)
HBM = pl.BlockSpec(memory_space=pltpu.HBM)

GROUP = 4

FIRST = 36
FIRST_SHARD = 4


def far(x):
    return pltpu.with_memory_space_constraint(x, pltpu.HBM)


def lanes(shape):
    return lax.broadcasted_iota(jnp.int32, shape, len(shape) - 1)


def subs(shape):
    return lax.broadcasted_iota(jnp.int32, shape, len(shape) - 2)


def call(body, name, out_shape, in_specs, scratch=(), limit=4 << 20, out_specs=None):
    many = isinstance(out_shape, tuple)
    return pl.pallas_call(
        body,
        out_shape=out_shape,
        in_specs=in_specs,
        out_specs=out_specs or ((VMEM,) * len(out_shape) if many else VMEM),
        scratch_shapes=list(scratch),
        compiler_params=pltpu.CompilerParams(vmem_limit_bytes=limit),
        name=name,
    )


def sine_cosine(angle):
    turn = jnp.floor(angle * (2.0 / math.pi) + 0.5)
    x = ((angle - turn * 1.5703125) - turn * 4.837512969970703e-4) - turn * 7.54978995489188e-8
    z = x * x
    sine = ((-1.9515295891e-4 * z + 8.3321608736e-3) * z - 1.6666654611e-1) * z * x + x
    cosine = ((2.443315711809948e-5 * z - 1.388731625493765e-3) * z + 4.166664568298827e-2) * z * z
    cosine = cosine - 0.5 * z + 1.0
    quadrant = turn.astype(jnp.int32) & 3
    odd = (quadrant & 1) == 1
    out_sine = jnp.where(odd, cosine, sine)
    out_cosine = jnp.where(odd, sine, cosine)
    out_sine = jnp.where(quadrant >= 2, -out_sine, out_sine)
    out_cosine = jnp.where((quadrant == 1) | (quadrant == 2), -out_cosine, out_cosine)
    return out_sine, out_cosine


def rotation(position, head_dim, width):
    half = head_dim // 2
    lane = lanes((8, width))
    pair = lane % half
    inverse = jnp.zeros((8, width), F32)
    for i in range(half):
        inverse = jnp.where(pair == i, ROPE_BASE ** (-2.0 * i / head_dim), inverse)
    sine, cosine = sine_cosine(position.astype(F32) * inverse)
    return cosine, jnp.where(lane % head_dim < half, -sine, sine)


def rope(x, cosine, sine, half):
    ahead = pltpu.roll(x, x.shape[1] - half, 1)
    behind = pltpu.roll(x, half, 1)
    first = lanes(x.shape) % (2 * half) < half
    return x * cosine + jnp.where(first, ahead, behind) * sine


def normalise(rows_ref, gain_ref):
    count = rows_ref.shape[0]
    x = rows_ref[...]
    total = jnp.sum(jnp.sum(x * x, axis=0, keepdims=True), axis=1, keepdims=True)
    scale = lax.rsqrt(total * (1.0 / x.size) + EPSILON)
    half = count // 2
    even = pl.ds(0, half, stride=2)
    odd = pl.ds(1, half, stride=2)
    left = pltpu.roll(rows_ref[even, :], FIRST_SHARD, 0) * scale * gain_ref[even, :]
    right = pltpu.roll(rows_ref[odd, :], FIRST_SHARD, 0) * scale * gain_ref[odd, :]
    return jnp.concatenate([left, right], axis=1)


def project(normed, weight_ref):
    chunks, wide = normed.shape
    row = subs(normed.shape)
    out = None
    for j in range(chunks):
        part = jnp.dot(
            jnp.where(row == j, normed, 0.0).astype(BF16),
            weight_ref[pl.ds(j * wide, wide), :],
            preferred_element_type=F32,
        )
        out = part if out is None else out + part
    return jnp.broadcast_to(jnp.sum(out, axis=0, keepdims=True), out.shape)


def fetch(sources, targets, sems):
    copies = [pltpu.make_async_copy(s, t, sems.at[i]) for i, (s, t) in enumerate(zip(sources, targets))]
    for copy in copies:
        copy.start()
    return copies


def prepare_kernel(head_dim, x_ref, lengths_ref, *rest):
    sources, (spread_ref, *targets) = rest[:3], rest[3:7]
    cos_ref, sin_ref, near_x, near_lengths, sems = rest[7:]
    copies = fetch((x_ref, lengths_ref, *sources), (near_x, near_lengths, *targets), sems)
    copies[1].wait()
    position = near_lengths[lax.axis_index("pool")]
    cos_ref[...], sin_ref[...] = rotation(position, head_dim, 2 * head_dim)
    copies[0].wait()
    size = near_x.shape[0]
    for i in range(spread_ref.shape[0] // size):
        spread_ref[pl.ds(i * size, size), :] = near_x[...]
    for copy in copies[2:]:
        copy.wait()


def query_kernel(head_dim, rows_ref, gain_ref, w_ref, w_keyval_ref, cos_ref, sin_ref, *rest):
    out_ref, kv_ref, own_ref, tiles_ref, sem = rest
    wide = 2 * head_dim
    cosine, sine = cos_ref[...], sin_ref[...]
    normed = normalise(rows_ref, gain_ref)
    query = project(normed, w_ref)
    row = subs((8, wide)) % GROUP
    tile = jnp.zeros((8, wide), F32)
    for c in range(GROUP // 2):
        part = rope(query[:, c * wide : (c + 1) * wide], cosine, sine, head_dim // 2)
        tile = jnp.where(row == 2 * c, part, tile)
        tile = jnp.where(row == 2 * c + 1, pltpu.roll(part, head_dim, 1), tile)
    is_key = lanes(tile.shape) < head_dim
    tile = jnp.where(is_key, tile.astype(BF16).astype(F32) * SCORE_SCALE, 0.0)
    for v in range(tiles_ref.shape[0] // 8):
        tiles_ref[pl.ds(8 * v, 8), :] = tile.astype(BF16)
    copy = pltpu.make_async_copy(tiles_ref, out_ref, sem)
    copy.start()
    keyval = project(normed, w_keyval_ref)
    turned = rope(keyval, cosine, sine, head_dim // 2)
    both = jnp.where(is_key, turned, keyval).astype(BF16)
    kv_ref[...] = both[:1]
    both = both.astype(F32)
    score = jnp.sum(tile * both, axis=1, keepdims=True)
    own_ref[...] = jnp.where(is_key, score, both)
    copy.wait()


def table_kernel(
    slots_here, block_len, lengths_hbm, slot_hbm, cache_ref, out_ref, held_ref, lengths_ref, slot_ref, sems
):
    copies = fetch((lengths_hbm, slot_hbm, cache_ref), (lengths_ref, slot_ref, held_ref), sems)
    copies[0].wait()
    copies[1].wait()
    requests, blocks = slot_ref.shape
    base = lax.axis_index("pool") * slots_here
    sub = subs((8, blocks))
    lane = lanes((8, blocks))
    wanted, payload = [], []
    for v in range(requests // 8):
        length = jnp.zeros((8, blocks), jnp.int32)
        for i in range(8):
            length = jnp.where(sub == i, lengths_ref[8 * v + i], length)
        limit = length - lane * block_len
        here = slot_ref[pl.ds(8 * v, 8), :] - base
        wanted.append(jnp.where(limit > 0, here, -1))
        payload.append(
            ((sub + 8 * v + requests - FIRST) % requests) * 256 + jnp.minimum(limit, block_len)
        )
    for tile in range(slots_here // 8):
        picked = jnp.zeros((8, blocks), jnp.int32)
        for i in range(8):
            found = jnp.zeros((8, blocks), jnp.int32)
            for w, p in zip(wanted, payload):
                found = jnp.where(w == 8 * tile + i, p, found)
            picked = jnp.where(sub == i, jnp.max(found, axis=0, keepdims=True), picked)
        out_ref[pl.ds(8 * tile, 8), :] = jnp.broadcast_to(
            jnp.max(picked.astype(F32), axis=1, keepdims=True), (8, blocks)
        ).astype(jnp.int32)
    copies[2].wait()


def attend_kernel(
    tab_ref, query_ref, kv_ref, out_ref, q_s, score_s, max_s, acc_s
):
    slots_here, block_len, wide = kv_ref.shape
    requests = query_ref.shape[0] // GROUP
    low = subs((8, wide)) < GROUP
    token = lanes((8, block_len))
    lane = lanes((8, wide))
    for v in range(requests // 2):
        tile = query_ref[pl.ds(8 * v, 8), :].astype(F32)
        other = pltpu.roll(tile, GROUP, 0)
        q_s[2 * v] = jnp.where(low, tile, other)
        q_s[2 * v + 1] = jnp.where(low, other, tile)
    max_s[...] = jnp.full_like(max_s, MASKED)
    acc_s[...] = jnp.zeros_like(acc_s)

    def pair(p):
        a, b = tab_ref[2 * p], tab_ref[2 * p + 1]
        live = token < jnp.where(low, a & 255, b & 255)
        keys = kv_ref[pl.ds(2 * p, 2)].reshape(2 * block_len, wide)
        return lax.shift_right_logical(a, 8), lax.shift_right_logical(b, 8), live, keys

    for p in range(slots_here // 2):
        ra, rb, live, keys = pair(p)
        query = jnp.where(low, q_s[ra], q_s[rb]).astype(BF16)
        scores = lax.dot_general(
            query, keys, (((1,), (1,)), ((), ())), preferred_element_type=F32
        )
        scores = jnp.where(low, scores[:, :block_len], scores[:, block_len:])
        scores = jnp.where(live, scores, MASKED)
        score_s[p] = scores
        top = jnp.broadcast_to(jnp.max(scores, axis=1, keepdims=True), scores.shape)
        other = pltpu.roll(top, GROUP, 0)
        max_s[ra] = jnp.maximum(max_s[ra], jnp.where(low, top, other))
        max_s[rb] = jnp.maximum(max_s[rb], jnp.where(low, other, top))

    for p in range(slots_here // 2):
        ra, rb, live, values = pair(p)
        top = jnp.where(low, max_s[ra], max_s[rb])
        weight = jnp.where(live, jnp.exp(score_s[p] - top), 0.0).astype(BF16).astype(F32)
        both = jnp.concatenate(
            [jnp.where(low, weight, 0.0), jnp.where(low, 0.0, weight)], axis=1
        ).astype(BF16)
        out = jnp.dot(both, values, preferred_element_type=F32)
        total = jnp.sum(weight, axis=1, keepdims=True)
        out = jnp.where(lane < wide // 2, total, out)
        other = pltpu.roll(out, GROUP, 0)
        acc_s[ra] = acc_s[ra] + jnp.where(low, out, other)
        acc_s[rb] = acc_s[rb] + jnp.where(low, other, out)

    for v in range(requests // 2):
        top = jnp.where(low, max_s[2 * v], max_s[2 * v + 1])
        out = jnp.where(low, acc_s[2 * v], acc_s[2 * v + 1])
        out_ref[pl.ds(8 * v, 8), :] = jnp.where(lane < wide // 4, top, out)


def combine_kernel(got_ref, own_ref, w_ref, out_ref):
    rows, wide = got_ref.shape
    lane = lanes((8, wide))
    row = subs((8, wide))
    parts = [got_ref[pl.ds(8 * v, 8), :] for v in range(rows // 8)]
    top = parts[0]
    for part in parts[1:]:
        top = jnp.maximum(top, part)
    own = own_ref[...]
    top = jnp.maximum(jnp.maximum(top, pltpu.roll(top, GROUP, 0)), own)
    mixed = jnp.zeros((8, wide), F32)
    for part in parts:
        weight = jnp.exp(part - top)
        mixed = mixed + jnp.broadcast_to(weight[:, :1], part.shape) * part
    mixed = mixed + pltpu.roll(mixed, GROUP, 0)
    own_weight = jnp.exp(own - top)
    mixed = mixed + jnp.broadcast_to(own_weight[:, :1], own.shape) * jnp.where(
        lane < wide // 2, 1.0, own
    )
    attended = mixed / jnp.broadcast_to(mixed[:, wide // 4 : wide // 4 + 1], mixed.shape)
    swapped = pltpu.roll(attended, wide // 2, 1)
    placed = jnp.where(
        row % 2 == 0,
        jnp.where(lane < wide // 2, swapped, 0.0),
        jnp.where(lane < wide // 2, 0.0, attended),
    )
    chunks = [
        jnp.sum(jnp.where(row // 2 == c, placed, 0.0), axis=0, keepdims=True)
        for c in range(GROUP // 2)
    ]
    line = jnp.broadcast_to(jnp.concatenate(chunks, axis=1), (8, GROUP // 2 * wide)).astype(BF16)
    lines = out_ref.shape[0]
    for v in range(lines // 8):
        at = (8 * v + FIRST_SHARD * GROUP // 2) % lines * wide
        part = jnp.dot(line, w_ref[:, pl.ds(at, 8 * wide)], preferred_element_type=F32)
        tile = jnp.zeros((8, wide), F32)
        for k in range(8):
            tile = jnp.where(row == k, part[:, k * wide : (k + 1) * wide], tile)
        out_ref[pl.ds(8 * v, 8), :] = tile


def exchange(x, axis, parts, first=0):
    shape = x.shape
    x = x.reshape(parts, shape[0] // parts, shape[1])
    groups = [[(i + first) % parts for i in range(parts)]] if first else None
    return lax.all_to_all(
        x, axis, split_axis=0, concat_axis=0, tiled=True, axis_index_groups=groups
    ).reshape(shape)


def per_device(hidden, norm_gain, w_query, w_keyval, w_out, kv_cache, block_slot, lengths):
    slots_here, _, block_len, wide = kv_cache.shape
    head_dim = wide // 2
    requests = block_slot.shape[0]
    shards = lax.axis_size("mp")
    pools = lax.axis_size("pool")
    features = hidden.shape[1]
    lines = features // wide
    gain = far(norm_gain.reshape(shards * lines, wide))
    cache = far(kv_cache.reshape(slots_here, block_len, wide))
    line = far(hidden.reshape(lines, wide))
    w_query, w_keyval, lengths, block_slot = (
        far(x) for x in (w_query, w_keyval, lengths, block_slot)
    )
    turn = jax.ShapeDtypeStruct((8, wide), F32)
    spread_rows, held_query, held_keyval, held_gain, cosine, sine = call(
        functools.partial(prepare_kernel, head_dim),
        "prepare",
        (
            jax.ShapeDtypeStruct((shards * lines, wide), F32),
            jax.ShapeDtypeStruct(w_query.shape, BF16),
            jax.ShapeDtypeStruct(w_keyval.shape, BF16),
            jax.ShapeDtypeStruct(gain.shape, F32),
            turn,
            turn,
        ),
        [HBM] * 5,
        [
            pltpu.VMEM((lines, wide), F32),
            pltpu.SMEM(lengths.shape, jnp.int32),
            pltpu.SemaphoreType.DMA((5,)),
        ],
    )(line, lengths, w_query, w_keyval, gain)

    rows = exchange(spread_rows, "mp", shards, FIRST_SHARD)

    tiles = jax.ShapeDtypeStruct((requests * GROUP, wide), BF16)
    query, new_kv, own = call(
        functools.partial(query_kernel, head_dim),
        "query",
        (tiles, jax.ShapeDtypeStruct((1, wide), BF16), turn),
        [VMEM] * 6,
        [pltpu.VMEM(tiles.shape, BF16), pltpu.SemaphoreType.DMA],
        out_specs=(HBM, VMEM, VMEM),
    )(rows, held_gain, held_query, held_keyval, cosine, sine)

    queries = exchange(query, "pool", pools, FIRST)

    lengths, block_slot, own = lax.optimization_barrier((lengths, block_slot, own))
    table, held_cache = call(
        functools.partial(table_kernel, slots_here, block_len),
        "slot_table",
        (
            jax.ShapeDtypeStruct((slots_here, block_slot.shape[1]), jnp.int32),
            jax.ShapeDtypeStruct(cache.shape, BF16),
        ),
        [HBM] * 3,
        [
            pltpu.SMEM(lengths.shape, jnp.int32),
            pltpu.VMEM(block_slot.shape, jnp.int32),
            pltpu.SemaphoreType.DMA((3,)),
        ],
    )(far(lengths), far(block_slot), cache)
    table = table[:, 0]

    per_request = pltpu.VMEM((requests, 8, wide), F32)
    partial = call(
        attend_kernel,
        "attend",
        jax.ShapeDtypeStruct((requests * GROUP, wide), F32),
        [SMEM, VMEM, VMEM],
        [
            per_request,
            pltpu.VMEM((slots_here // 2, 8, block_len), F32),
            per_request,
            per_request,
        ],
        limit=12 << 20,
    )(table, queries, held_cache)

    got = exchange(partial, "pool", pools, FIRST)

    mixed = call(
        combine_kernel,
        "combine",
        jax.ShapeDtypeStruct((shards * lines, wide), F32),
        [VMEM, VMEM, VMEM],
    )(got, own, w_out)

    spread = exchange(mixed, "mp", shards, FIRST_SHARD)
    total = jnp.sum(spread.reshape(shards, features), axis=0, keepdims=True)
    return (hidden + RESIDUAL_SCALE * total, new_kv)


def solution(mesh):
    return jax.shard_map(
        per_device,
        mesh=mesh,
        in_specs=(
            P("pool", "mp"),
            P(),
            P(None, "mp"),
            P(None, "mp"),
            P("mp", None),
            P("pool", "mp", None, None),
            P(),
            P(),
        ),
        out_specs=(P("pool", "mp"), P("pool", "mp")),
        check_vma=False,
    )
```

```python
import functools
import math

import jax
import jax.numpy as jnp
from jax import lax
from jax.experimental import pallas as pl
from jax.experimental.pallas import tpu as pltpu
from jax.sharding import PartitionSpec as P

EPSILON = 1e-05
RESIDUAL_SCALE = 0.22
SCORE_SCALE = 0.015625
ROPE_BASE = 10000000.0
MASKED = -1e30

F32 = jnp.float32
BF16 = jnp.bfloat16
VMEM = pl.BlockSpec(memory_space=pltpu.VMEM)
SMEM = pl.BlockSpec(memory_space=pltpu.SMEM)
HBM = pl.BlockSpec(memory_space=pltpu.HBM)

GROUP = 4

SPLIT = 4

FIRST = 36
FIRST_SHARD = 4


def far(x):
    return pltpu.with_memory_space_constraint(x, pltpu.HBM)


def lanes(shape):
    return lax.broadcasted_iota(jnp.int32, shape, len(shape) - 1)


def subs(shape):
    return lax.broadcasted_iota(jnp.int32, shape, len(shape) - 2)


def call(body, name, out_shape, in_specs, scratch=(), limit=4 << 20, out_specs=None):
    many = isinstance(out_shape, tuple)
    return pl.pallas_call(
        body,
        out_shape=out_shape,
        in_specs=in_specs,
        out_specs=out_specs or ((VMEM,) * len(out_shape) if many else VMEM),
        scratch_shapes=list(scratch),
        compiler_params=pltpu.CompilerParams(vmem_limit_bytes=limit),
        name=name,
    )


def sine_cosine(angle):
    turn = jnp.floor(angle * (2.0 / math.pi) + 0.5)
    x = ((angle - turn * 1.5703125) - turn * 4.837512969970703e-4) - turn * 7.54978995489188e-8
    z = x * x
    sine = ((-1.9515295891e-4 * z + 8.3321608736e-3) * z - 1.6666654611e-1) * z * x + x
    cosine = ((2.443315711809948e-5 * z - 1.388731625493765e-3) * z + 4.166664568298827e-2) * z * z
    cosine = cosine - 0.5 * z + 1.0
    quadrant = turn.astype(jnp.int32) & 3
    odd = (quadrant & 1) == 1
    out_sine = jnp.where(odd, cosine, sine)
    out_cosine = jnp.where(odd, sine, cosine)
    out_sine = jnp.where(quadrant >= 2, -out_sine, out_sine)
    out_cosine = jnp.where((quadrant == 1) | (quadrant == 2), -out_cosine, out_cosine)
    return out_sine, out_cosine


def rotation(position, head_dim, width):
    half = head_dim // 2
    lane = lanes((8, width))
    pair = lane % half
    inverse = jnp.zeros((8, width), F32)
    for i in range(half):
        inverse = jnp.where(pair == i, ROPE_BASE ** (-2.0 * i / head_dim), inverse)
    sine, cosine = sine_cosine(position.astype(F32) * inverse)
    return cosine, jnp.where(lane % head_dim < half, -sine, sine)


def rope(x, cosine, sine, half):
    ahead = pltpu.roll(x, x.shape[1] - half, 1)
    behind = pltpu.roll(x, half, 1)
    first = lanes(x.shape) % (2 * half) < half
    return x * cosine + jnp.where(first, ahead, behind) * sine


def normalise(rows_ref, gain_ref):
    count = rows_ref.shape[0]
    x = rows_ref[...]
    total = jnp.sum(jnp.sum(x * x, axis=0, keepdims=True), axis=1, keepdims=True)
    scale = lax.rsqrt(total * (1.0 / x.size) + EPSILON)
    half = count // 2
    even = pl.ds(0, half, stride=2)
    odd = pl.ds(1, half, stride=2)
    left = pltpu.roll(rows_ref[even, :], FIRST_SHARD, 0) * scale * gain_ref[even, :]
    right = pltpu.roll(rows_ref[odd, :], FIRST_SHARD, 0) * scale * gain_ref[odd, :]
    return jnp.concatenate([left, right], axis=1)


def project(normed, weight_ref):
    chunks, wide = normed.shape
    row = subs(normed.shape)
    out = None
    for j in range(chunks):
        part = jnp.dot(
            jnp.where(row == j, normed, 0.0).astype(BF16),
            weight_ref[pl.ds(j * wide, wide), :],
            preferred_element_type=F32,
        )
        out = part if out is None else out + part
    return jnp.broadcast_to(jnp.sum(out, axis=0, keepdims=True), out.shape)


def fetch(sources, targets, sems):
    lists = []
    for i, (source, target) in enumerate(zip(sources, targets)):
        parts = SPLIT if source.size >= 1 << 18 else 1
        size = source.shape[0] // parts
        copies = []
        for j in range(parts):
            rows = pl.ds(j * size, size)
            copy = pltpu.make_async_copy(
                source.at[rows] if parts > 1 else source,
                target.at[rows] if parts > 1 else target,
                sems.at[i, j],
            )
            copy.start()
            copies.append(copy)
        lists.append(copies)
    return lists


def wait(lists):
    for copies in lists:
        for copy in copies:
            copy.wait()


def prepare_kernel(head_dim, x_ref, lengths_ref, *rest):
    sources, (spread_ref, *targets) = rest[:3], rest[3:7]
    cos_ref, sin_ref, near_x, near_lengths, sems = rest[7:]
    copies = fetch((x_ref, lengths_ref, *sources), (near_x, near_lengths, *targets), sems)
    wait(copies[1:2])
    position = near_lengths[lax.axis_index("pool")]
    cos_ref[...], sin_ref[...] = rotation(position, head_dim, 2 * head_dim)
    wait(copies[:1])
    size = near_x.shape[0]
    for i in range(spread_ref.shape[0] // size):
        spread_ref[pl.ds(i * size, size), :] = near_x[...]
    wait(copies[2:])


def query_kernel(head_dim, rows_ref, gain_ref, w_ref, w_keyval_ref, cos_ref, sin_ref, *rest):
    out_ref, kv_ref, own_ref, tiles_ref, sem = rest
    wide = 2 * head_dim
    cosine, sine = cos_ref[...], sin_ref[...]
    normed = normalise(rows_ref, gain_ref)
    query = project(normed, w_ref)
    row = subs((8, wide)) % GROUP
    tile = jnp.zeros((8, wide), F32)
    for c in range(GROUP // 2):
        part = rope(query[:, c * wide : (c + 1) * wide], cosine, sine, head_dim // 2)
        tile = jnp.where(row == 2 * c, part, tile)
        tile = jnp.where(row == 2 * c + 1, pltpu.roll(part, head_dim, 1), tile)
    is_key = lanes(tile.shape) < head_dim
    tile = jnp.where(is_key, tile.astype(BF16).astype(F32) * SCORE_SCALE, 0.0)
    for v in range(tiles_ref.shape[0] // 8):
        tiles_ref[pl.ds(8 * v, 8), :] = tile.astype(BF16)
    copy = pltpu.make_async_copy(tiles_ref, out_ref, sem)
    copy.start()
    keyval = project(normed, w_keyval_ref)
    turned = rope(keyval, cosine, sine, head_dim // 2)
    both = jnp.where(is_key, turned, keyval).astype(BF16)
    both = both.astype(F32)
    kv_ref[...] = both
    score = jnp.sum(tile * both, axis=1, keepdims=True)
    own_ref[...] = jnp.where(is_key, score, both)
    copy.wait()


def table_kernel(
    slots_here, block_len, lengths_hbm, slot_hbm, cache_ref, out_ref, held_ref, lengths_ref, slot_ref, sems
):
    copies = fetch((lengths_hbm, slot_hbm, cache_ref), (lengths_ref, slot_ref, held_ref), sems)
    wait(copies[:2])
    requests, blocks = slot_ref.shape
    base = lax.axis_index("pool") * slots_here
    sub = subs((8, blocks))
    lane = lanes((8, blocks))
    wanted, payload = [], []
    for v in range(requests // 8):
        length = jnp.zeros((8, blocks), jnp.int32)
        for i in range(8):
            length = jnp.where(sub == i, lengths_ref[8 * v + i], length)
        limit = length - lane * block_len
        here = slot_ref[pl.ds(8 * v, 8), :] - base
        wanted.append(jnp.where(limit > 0, here, -1))
        payload.append(
            ((sub + 8 * v + requests - FIRST) % requests) * 256 + jnp.minimum(limit, block_len)
        )
    for tile in range(slots_here // 8):
        picked = jnp.zeros((8, blocks), jnp.int32)
        for i in range(8):
            found = jnp.zeros((8, blocks), jnp.int32)
            for w, p in zip(wanted, payload):
                found = jnp.where(w == 8 * tile + i, p, found)
            picked = jnp.where(sub == i, jnp.max(found, axis=0, keepdims=True), picked)
        out_ref[pl.ds(8 * tile, 8), :] = jnp.broadcast_to(
            jnp.max(picked.astype(F32), axis=1, keepdims=True), (8, blocks)
        ).astype(jnp.int32)
    wait(copies[2:])


def attend_kernel(
    tab_ref, query_ref, kv_ref, out_ref, q_s, score_s, max_s, acc_s
):
    slots_here, block_len, wide = kv_ref.shape
    requests = query_ref.shape[0] // GROUP
    low = subs((8, wide)) < GROUP
    token = lanes((8, block_len))
    lane = lanes((8, wide))
    for v in range(requests // 2):
        tile = query_ref[pl.ds(8 * v, 8), :].astype(F32)
        other = pltpu.roll(tile, GROUP, 0)
        q_s[2 * v] = jnp.where(low, tile, other)
        q_s[2 * v + 1] = jnp.where(low, other, tile)
    max_s[...] = jnp.full_like(max_s, MASKED)
    acc_s[...] = jnp.zeros_like(acc_s)

    def pair(p):
        a, b = tab_ref[2 * p], tab_ref[2 * p + 1]
        live = token < jnp.where(low, a & 255, b & 255)
        keys = kv_ref[pl.ds(2 * p, 2)].reshape(2 * block_len, wide)
        return lax.shift_right_logical(a, 8), lax.shift_right_logical(b, 8), live, keys

    for p in range(slots_here // 2):
        ra, rb, live, keys = pair(p)
        query = jnp.where(low, q_s[ra], q_s[rb]).astype(BF16)
        scores = lax.dot_general(
            query, keys, (((1,), (1,)), ((), ())), preferred_element_type=F32
        )
        scores = jnp.where(low, scores[:, :block_len], scores[:, block_len:])
        scores = jnp.where(live, scores, MASKED)
        score_s[p] = scores
        top = jnp.broadcast_to(jnp.max(scores, axis=1, keepdims=True), scores.shape)
        other = pltpu.roll(top, GROUP, 0)
        max_s[ra] = jnp.maximum(max_s[ra], jnp.where(low, top, other))
        max_s[rb] = jnp.maximum(max_s[rb], jnp.where(low, other, top))

    for p in range(slots_here // 2):
        ra, rb, live, values = pair(p)
        top = jnp.where(low, max_s[ra], max_s[rb])
        weight = jnp.where(live, jnp.exp(score_s[p] - top), 0.0).astype(BF16).astype(F32)
        both = jnp.concatenate(
            [jnp.where(low, weight, 0.0), jnp.where(low, 0.0, weight)], axis=1
        ).astype(BF16)
        out = jnp.dot(both, values, preferred_element_type=F32)
        total = jnp.sum(weight, axis=1, keepdims=True)
        out = jnp.where(lane < wide // 2, total, out)
        other = pltpu.roll(out, GROUP, 0)
        acc_s[ra] = acc_s[ra] + jnp.where(low, out, other)
        acc_s[rb] = acc_s[rb] + jnp.where(low, other, out)

    for v in range(requests // 2):
        top = jnp.where(low, max_s[2 * v], max_s[2 * v + 1])
        out = jnp.where(low, acc_s[2 * v], acc_s[2 * v + 1])
        out_ref[pl.ds(8 * v, 8), :] = jnp.where(lane < wide // 4, top, out)


def combine_kernel(got_ref, own_ref, w_ref, out_ref):
    rows, wide = got_ref.shape
    lane = lanes((8, wide))
    row = subs((8, wide))
    parts = [got_ref[pl.ds(8 * v, 8), :] for v in range(rows // 8)]
    top = parts[0]
    for part in parts[1:]:
        top = jnp.maximum(top, part)
    own = own_ref[...]
    top = jnp.maximum(jnp.maximum(top, pltpu.roll(top, GROUP, 0)), own)
    mixed = jnp.zeros((8, wide), F32)
    for part in parts:
        weight = jnp.exp(part - top)
        mixed = mixed + jnp.broadcast_to(weight[:, :1], part.shape) * part
    mixed = mixed + pltpu.roll(mixed, GROUP, 0)
    own_weight = jnp.exp(own - top)
    mixed = mixed + jnp.broadcast_to(own_weight[:, :1], own.shape) * jnp.where(
        lane < wide // 2, 1.0, own
    )
    attended = mixed / jnp.broadcast_to(mixed[:, wide // 4 : wide // 4 + 1], mixed.shape)
    swapped = pltpu.roll(attended, wide // 2, 1)
    placed = jnp.where(
        row % 2 == 0,
        jnp.where(lane < wide // 2, swapped, 0.0),
        jnp.where(lane < wide // 2, 0.0, attended),
    )
    chunks = [
        jnp.sum(jnp.where(row // 2 == c, placed, 0.0), axis=0, keepdims=True)
        for c in range(GROUP // 2)
    ]
    line = jnp.broadcast_to(jnp.concatenate(chunks, axis=1), (8, GROUP // 2 * wide)).astype(BF16)
    lines = out_ref.shape[0]
    for v in range(lines // 8):
        at = (8 * v + FIRST_SHARD * GROUP // 2) % lines * wide
        part = jnp.dot(line, w_ref[:, pl.ds(at, 8 * wide)], preferred_element_type=F32)
        tile = jnp.zeros((8, wide), F32)
        for k in range(8):
            tile = jnp.where(row == k, part[:, k * wide : (k + 1) * wide], tile)
        out_ref[pl.ds(8 * v, 8), :] = tile


def exchange(x, axis, parts, first=0):
    shape = x.shape
    x = x.reshape(parts, shape[0] // parts, shape[1])
    groups = [[(i + first) % parts for i in range(parts)]] if first else None
    return lax.all_to_all(
        x, axis, split_axis=0, concat_axis=0, tiled=True, axis_index_groups=groups
    ).reshape(shape)


def per_device(hidden, norm_gain, w_query, w_keyval, w_out, kv_cache, block_slot, lengths):
    slots_here, _, block_len, wide = kv_cache.shape
    head_dim = wide // 2
    requests = block_slot.shape[0]
    shards = lax.axis_size("mp")
    pools = lax.axis_size("pool")
    features = hidden.shape[1]
    lines = features // wide
    gain = far(norm_gain.reshape(shards * lines, wide))
    cache = far(kv_cache.reshape(slots_here, block_len, wide))
    line = far(hidden.reshape(lines, wide))
    w_query, w_keyval, lengths, block_slot = (
        far(x) for x in (w_query, w_keyval, lengths, block_slot)
    )
    turn = jax.ShapeDtypeStruct((8, wide), F32)
    spread_rows, held_query, held_keyval, held_gain, cosine, sine = call(
        functools.partial(prepare_kernel, head_dim),
        "prepare",
        (
            jax.ShapeDtypeStruct((shards * lines, wide), F32),
            jax.ShapeDtypeStruct(w_query.shape, BF16),
            jax.ShapeDtypeStruct(w_keyval.shape, BF16),
            jax.ShapeDtypeStruct(gain.shape, F32),
            turn,
            turn,
        ),
        [HBM] * 5,
        [
            pltpu.VMEM((lines, wide), F32),
            pltpu.SMEM(lengths.shape, jnp.int32),
            pltpu.SemaphoreType.DMA((5, SPLIT)),
        ],
    )(line, lengths, w_query, w_keyval, gain)

    rows = exchange(spread_rows, "mp", shards, FIRST_SHARD)

    tiles = jax.ShapeDtypeStruct((requests * GROUP, wide), BF16)
    query, new_tile, own = call(
        functools.partial(query_kernel, head_dim),
        "query",
        (tiles, turn, turn),
        [VMEM] * 6,
        [pltpu.VMEM(tiles.shape, BF16), pltpu.SemaphoreType.DMA],
        out_specs=(HBM, VMEM, VMEM),
    )(rows, held_gain, held_query, held_keyval, cosine, sine)

    queries = exchange(query, "pool", pools, FIRST)

    lengths, block_slot, own, new_tile = lax.optimization_barrier(
        (lengths, block_slot, own, new_tile)
    )
    new_kv = new_tile[:1].astype(BF16)
    table, held_cache = call(
        functools.partial(table_kernel, slots_here, block_len),
        "slot_table",
        (
            jax.ShapeDtypeStruct((slots_here, block_slot.shape[1]), jnp.int32),
            jax.ShapeDtypeStruct(cache.shape, BF16),
        ),
        [HBM] * 3,
        [
            pltpu.SMEM(lengths.shape, jnp.int32),
            pltpu.VMEM(block_slot.shape, jnp.int32),
            pltpu.SemaphoreType.DMA((3, SPLIT)),
        ],
    )(far(lengths), far(block_slot), cache)
    table, new_kv = lax.optimization_barrier((table[:, 0], new_kv))

    per_request = pltpu.VMEM((requests, 8, wide), F32)
    partial = call(
        attend_kernel,
        "attend",
        jax.ShapeDtypeStruct((requests * GROUP, wide), F32),
        [SMEM, VMEM, VMEM],
        [
            per_request,
            pltpu.VMEM((slots_here // 2, 8, block_len), F32),
            per_request,
            per_request,
        ],
        limit=12 << 20,
    )(table, queries, held_cache)

    got = exchange(partial, "pool", pools, FIRST)

    mixed = call(
        combine_kernel,
        "combine",
        jax.ShapeDtypeStruct((shards * lines, wide), F32),
        [VMEM, VMEM, VMEM],
    )(got, own, w_out)

    spread = exchange(mixed, "mp", shards, FIRST_SHARD)
    total = jnp.sum(spread.reshape(shards, features), axis=0, keepdims=True)
    return (hidden + RESIDUAL_SCALE * total, new_kv)


def solution(mesh):
    return jax.shard_map(
        per_device,
        mesh=mesh,
        in_specs=(
            P("pool", "mp"),
            P(),
            P(None, "mp"),
            P(None, "mp"),
            P("mp", None),
            P("pool", "mp", None, None),
            P(),
            P(),
        ),
        out_specs=(P("pool", "mp"), P("pool", "mp")),
        check_vma=False,
    )
```

```python
import functools
import math

import jax
import jax.numpy as jnp
from jax import lax
from jax.experimental import pallas as pl
from jax.experimental.pallas import tpu as pltpu
from jax.sharding import PartitionSpec as P

EPSILON = 1e-05
RESIDUAL_SCALE = 0.22
SCORE_SCALE = 0.015625
ROPE_BASE = 10000000.0
MASKED = -1e30

F32 = jnp.float32
BF16 = jnp.bfloat16
VMEM = pl.BlockSpec(memory_space=pltpu.VMEM)
SMEM = pl.BlockSpec(memory_space=pltpu.SMEM)
HBM = pl.BlockSpec(memory_space=pltpu.HBM)

GROUP = 4
TERM = 8

FIRST = 36
FIRST_SHARD = 4


def far(x):
    return pltpu.with_memory_space_constraint(x, pltpu.HBM)


def lanes(shape):
    return lax.broadcasted_iota(jnp.int32, shape, len(shape) - 1)


def subs(shape):
    return lax.broadcasted_iota(jnp.int32, shape, len(shape) - 2)


def call(body, name, out_shape, in_specs, scratch=(), limit=4 << 20, out_specs=None):
    many = isinstance(out_shape, tuple)
    return pl.pallas_call(
        body,
        out_shape=out_shape,
        in_specs=in_specs,
        out_specs=out_specs or ((VMEM,) * len(out_shape) if many else VMEM),
        scratch_shapes=list(scratch),
        compiler_params=pltpu.CompilerParams(vmem_limit_bytes=limit),
        name=name,
    )


def sine_cosine(angle):
    turn = jnp.floor(angle * (2.0 / math.pi) + 0.5)
    x = ((angle - turn * 1.5703125) - turn * 4.837512969970703e-4) - turn * 7.54978995489188e-8
    z = x * x
    sine = ((-1.9515295891e-4 * z + 8.3321608736e-3) * z - 1.6666654611e-1) * z * x + x
    cosine = ((2.443315711809948e-5 * z - 1.388731625493765e-3) * z + 4.166664568298827e-2) * z * z
    cosine = cosine - 0.5 * z + 1.0
    quadrant = turn.astype(jnp.int32) & 3
    odd = (quadrant & 1) == 1
    out_sine = jnp.where(odd, cosine, sine)
    out_cosine = jnp.where(odd, sine, cosine)
    out_sine = jnp.where(quadrant >= 2, -out_sine, out_sine)
    out_cosine = jnp.where((quadrant == 1) | (quadrant == 2), -out_cosine, out_cosine)
    return out_sine, out_cosine


def rotation(position, head_dim, width):
    half = head_dim // 2
    lane = lanes((8, width))
    pair = lane % half
    inverse = jnp.zeros((8, width), F32)
    for i in range(half):
        inverse = jnp.where(pair == i, ROPE_BASE ** (-2.0 * i / head_dim), inverse)
    sine, cosine = sine_cosine(position.astype(F32) * inverse)
    return cosine, jnp.where(lane % head_dim < half, -sine, sine)


def rope(x, cosine, sine, half):
    ahead = pltpu.roll(x, x.shape[1] - half, 1)
    behind = pltpu.roll(x, half, 1)
    first = lanes(x.shape) % (2 * half) < half
    return x * cosine + jnp.where(first, ahead, behind) * sine


def normalise(rows_ref, gain_ref):
    count = rows_ref.shape[0]
    x = rows_ref[...]
    total = jnp.sum(jnp.sum(x * x, axis=0, keepdims=True), axis=1, keepdims=True)
    scale = lax.rsqrt(total * (1.0 / x.size) + EPSILON)
    half = count // 2
    even = pl.ds(0, half, stride=2)
    odd = pl.ds(1, half, stride=2)
    left = pltpu.roll(rows_ref[even, :], FIRST_SHARD, 0) * scale * gain_ref[even, :]
    right = pltpu.roll(rows_ref[odd, :], FIRST_SHARD, 0) * scale * gain_ref[odd, :]
    return jnp.concatenate([left, right], axis=1)


def project(normed, weight_ref):
    chunks, wide = normed.shape
    row = subs(normed.shape)
    out = None
    for j in range(chunks):
        part = jnp.dot(
            jnp.where(row == j, normed, 0.0).astype(BF16),
            weight_ref[pl.ds(j * wide, wide), :],
            preferred_element_type=F32,
        )
        out = part if out is None else out + part
    return jnp.broadcast_to(jnp.sum(out, axis=0, keepdims=True), out.shape)


def fetch(sources, targets, sems):
    copies = [pltpu.make_async_copy(s, t, sems.at[i]) for i, (s, t) in enumerate(zip(sources, targets))]
    for copy in copies:
        copy.start()
    return copies


def wait(copies):
    for copy in copies:
        copy.wait()


def prepare_kernel(head_dim, x_ref, lengths_ref, *rest):
    sources, (spread_ref, *targets) = rest[:2], rest[2:5]
    cos_ref, sin_ref, near_x, near_lengths, sems = rest[5:]
    copies = fetch((x_ref, lengths_ref, *sources), (near_x, near_lengths, *targets), sems)
    wait(copies[1:2])
    position = near_lengths[lax.axis_index("pool")]
    cos_ref[...], sin_ref[...] = rotation(position, head_dim, 2 * head_dim)
    wait(copies[:1])
    size = near_x.shape[0]
    for i in range(spread_ref.shape[0] // size):
        spread_ref[pl.ds(i * size, size), :] = near_x[...]
    wait(copies[2:])


def query_kernel(head_dim, rows_ref, gain_ref, w_ref, cos_ref, sin_ref, w_keyval_hbm, *rest):
    out_ref, kv_ref, own_ref, tiles_ref, w_keyval_ref, sems = rest
    weight = pltpu.make_async_copy(w_keyval_hbm, w_keyval_ref, sems.at[1])
    weight.start()
    wide = 2 * head_dim
    cosine, sine = cos_ref[...], sin_ref[...]
    normed = normalise(rows_ref, gain_ref)
    query = project(normed, w_ref)
    row = subs((8, wide)) % GROUP
    tile = jnp.zeros((8, wide), F32)
    for c in range(GROUP // 2):
        part = rope(query[:, c * wide : (c + 1) * wide], cosine, sine, head_dim // 2)
        tile = jnp.where(row == 2 * c, part, tile)
        tile = jnp.where(row == 2 * c + 1, pltpu.roll(part, head_dim, 1), tile)
    is_key = lanes(tile.shape) < head_dim
    tile = jnp.where(is_key, tile.astype(BF16).astype(F32) * SCORE_SCALE, 0.0)
    for v in range(tiles_ref.shape[0] // 8):
        tiles_ref[pl.ds(8 * v, 8), :] = tile.astype(BF16)
    copy = pltpu.make_async_copy(tiles_ref, out_ref, sems.at[0])
    copy.start()
    weight.wait()
    keyval = project(normed, w_keyval_ref)
    turned = rope(keyval, cosine, sine, head_dim // 2)
    both = jnp.where(is_key, turned, keyval).astype(BF16)
    both = both.astype(F32)
    kv_ref[...] = both
    score = jnp.sum(tile * both, axis=1, keepdims=True)
    own_ref[...] = jnp.where(is_key, score, both)
    copy.wait()


def table_kernel(
    slots_here, block_len, lengths_hbm, slot_hbm, cache_ref, out_ref, held_ref, lengths_ref, slot_ref, sems
):
    copies = fetch((lengths_hbm, slot_hbm, cache_ref), (lengths_ref, slot_ref, held_ref), sems)
    wait(copies[:2])
    requests, blocks = slot_ref.shape
    base = lax.axis_index("pool") * slots_here
    sub = subs((8, blocks))
    lane = lanes((8, blocks))
    wanted, payload = [], []
    for v in range(requests // 8):
        length = jnp.zeros((8, blocks), jnp.int32)
        for i in range(8):
            length = jnp.where(sub == i, lengths_ref[8 * v + i], length)
        limit = length - lane * block_len
        here = slot_ref[pl.ds(8 * v, 8), :] - base
        wanted.append(jnp.where(limit > 0, here, -1))
        payload.append(
            ((sub + 8 * v + requests - FIRST) % requests) * 256 + jnp.minimum(limit, block_len)
        )
    for tile in range(slots_here // 8):
        picked = jnp.zeros((8, blocks), jnp.int32)
        for i in range(8):
            found = jnp.zeros((8, blocks), jnp.int32)
            for w, p in zip(wanted, payload):
                found = jnp.where(w == 8 * tile + i, p, found)
            picked = jnp.where(sub == i, jnp.max(found, axis=0, keepdims=True), picked)
        out_ref[pl.ds(8 * tile, 8), :] = jnp.broadcast_to(
            jnp.max(picked.astype(F32), axis=1, keepdims=True), (8, blocks)
        ).astype(jnp.int32)
    wait(copies[2:])


def attend_kernel(
    tab_ref, query_ref, kv_ref, out_ref, q_s, score_s, max_s, acc_s
):
    slots_here, block_len, wide = kv_ref.shape
    requests = query_ref.shape[0] // GROUP
    low = subs((8, wide)) < GROUP
    token = lanes((8, block_len))
    lane = lanes((8, wide))
    for v in range(requests // 2):
        tile = query_ref[pl.ds(8 * v, 8), :].astype(F32)
        other = pltpu.roll(tile, GROUP, 0)
        q_s[2 * v] = jnp.where(low, tile, other)
        q_s[2 * v + 1] = jnp.where(low, other, tile)
    max_s[...] = jnp.full_like(max_s, MASKED)
    acc_s[...] = jnp.zeros_like(acc_s)

    def pair(p):
        a, b = tab_ref[2 * p], tab_ref[2 * p + 1]
        live = token < jnp.where(low, a & 255, b & 255)
        keys = kv_ref[pl.ds(2 * p, 2)].reshape(2 * block_len, wide)
        return lax.shift_right_logical(a, 8), lax.shift_right_logical(b, 8), live, keys

    for p in range(slots_here // 2):
        ra, rb, live, keys = pair(p)
        query = jnp.where(low, q_s[ra], q_s[rb]).astype(BF16)
        scores = lax.dot_general(
            query, keys, (((1,), (1,)), ((), ())), preferred_element_type=F32
        )
        scores = jnp.where(low, scores[:, :block_len], scores[:, block_len:])
        scores = jnp.where(live, scores, MASKED)
        score_s[p] = scores
        top = jnp.broadcast_to(jnp.max(scores, axis=1, keepdims=True), scores.shape)
        other = pltpu.roll(top, GROUP, 0)
        max_s[ra] = jnp.maximum(max_s[ra], jnp.where(low, top, other))
        max_s[rb] = jnp.maximum(max_s[rb], jnp.where(low, other, top))

    for p in range(slots_here // 2):
        ra, rb, live, values = pair(p)
        top = jnp.where(low, max_s[ra], max_s[rb])
        weight = jnp.where(live, jnp.exp(score_s[p] - top), 0.0).astype(BF16).astype(F32)
        both = jnp.concatenate(
            [jnp.where(low, weight, 0.0), jnp.where(low, 0.0, weight)], axis=1
        ).astype(BF16)
        out = jnp.dot(both, values, preferred_element_type=F32)
        total = jnp.sum(weight, axis=1, keepdims=True)
        out = jnp.where(lane < wide // 2, total, out)
        other = pltpu.roll(out, GROUP, 0)
        acc_s[ra] = acc_s[ra] + jnp.where(low, out, other)
        acc_s[rb] = acc_s[rb] + jnp.where(low, other, out)

    for v in range(requests // 2):
        top = jnp.where(low, max_s[2 * v], max_s[2 * v + 1])
        out = jnp.where(low, acc_s[2 * v], acc_s[2 * v + 1])
        out = jnp.where(lane < wide // 4, top, out)
        terms = []
        for _ in range(3):
            terms.append(out.astype(BF16).astype(F32))
            out = out - terms[-1]
        third = (lane % (wide // 4)) // TERM
        out = jnp.where(
            (lane >= wide // 2) | (third == 0),
            terms[0],
            jnp.where(third == 1, terms[1], terms[2]),
        )
        out_ref[pl.ds(8 * v, 8), :] = out.astype(BF16)


def combine_kernel(got_ref, own_ref, w_ref, out_ref):
    rows, wide = got_ref.shape
    lane = lanes((8, wide))
    row = subs((8, wide))
    parts = []
    for v in range(rows // 8):
        part = got_ref[pl.ds(8 * v, 8), :].astype(F32)
        whole = part + pltpu.roll(part, wide - TERM, 1) + pltpu.roll(part, wide - 2 * TERM, 1)
        parts.append(jnp.where(lane < wide // 2, whole, part))
    top = parts[0]
    for part in parts[1:]:
        top = jnp.maximum(top, part)
    own = own_ref[...]
    top = jnp.maximum(jnp.maximum(top, pltpu.roll(top, GROUP, 0)), own)
    mixed = jnp.zeros((8, wide), F32)
    for part in parts:
        weight = jnp.exp(part - top)
        mixed = mixed + jnp.broadcast_to(weight[:, :1], part.shape) * part
    mixed = mixed + pltpu.roll(mixed, GROUP, 0)
    own_weight = jnp.exp(own - top)
    mixed = mixed + jnp.broadcast_to(own_weight[:, :1], own.shape) * jnp.where(
        lane < wide // 2, 1.0, own
    )
    attended = mixed / jnp.broadcast_to(mixed[:, wide // 4 : wide // 4 + 1], mixed.shape)
    swapped = pltpu.roll(attended, wide // 2, 1)
    placed = jnp.where(
        row % 2 == 0,
        jnp.where(lane < wide // 2, swapped, 0.0),
        jnp.where(lane < wide // 2, 0.0, attended),
    )
    chunks = [
        jnp.sum(jnp.where(row // 2 == c, placed, 0.0), axis=0, keepdims=True)
        for c in range(GROUP // 2)
    ]
    line = jnp.broadcast_to(jnp.concatenate(chunks, axis=1), (8, GROUP // 2 * wide)).astype(BF16)
    lines = out_ref.shape[0]
    for v in range(lines // 8):
        at = (8 * v + FIRST_SHARD * GROUP // 2) % lines * wide
        part = jnp.dot(line, w_ref[:, pl.ds(at, 8 * wide)], preferred_element_type=F32)
        tile = jnp.zeros((8, wide), F32)
        for k in range(8):
            tile = jnp.where(row == k, part[:, k * wide : (k + 1) * wide], tile)
        out_ref[pl.ds(8 * v, 8), :] = tile


def exchange(x, axis, parts, first=0):
    shape = x.shape
    x = x.reshape(parts, shape[0] // parts, shape[1])
    groups = [[(i + first) % parts for i in range(parts)]] if first else None
    return lax.all_to_all(
        x, axis, split_axis=0, concat_axis=0, tiled=True, axis_index_groups=groups
    ).reshape(shape)


def per_device(hidden, norm_gain, w_query, w_keyval, w_out, kv_cache, block_slot, lengths):
    slots_here, _, block_len, wide = kv_cache.shape
    head_dim = wide // 2
    requests = block_slot.shape[0]
    shards = lax.axis_size("mp")
    pools = lax.axis_size("pool")
    features = hidden.shape[1]
    lines = features // wide
    gain = far(norm_gain.reshape(shards * lines, wide))
    cache = far(kv_cache.reshape(slots_here, block_len, wide))
    line = far(hidden.reshape(lines, wide))
    w_query, w_keyval, lengths, block_slot = (
        far(x) for x in (w_query, w_keyval, lengths, block_slot)
    )
    turn = jax.ShapeDtypeStruct((8, wide), F32)
    spread_rows, held_query, held_gain, cosine, sine = call(
        functools.partial(prepare_kernel, head_dim),
        "prepare",
        (
            jax.ShapeDtypeStruct((shards * lines, wide), F32),
            jax.ShapeDtypeStruct(w_query.shape, BF16),
            jax.ShapeDtypeStruct(gain.shape, F32),
            turn,
            turn,
        ),
        [HBM] * 4,
        [
            pltpu.VMEM((lines, wide), F32),
            pltpu.SMEM(lengths.shape, jnp.int32),
            pltpu.SemaphoreType.DMA((4,)),
        ],
    )(line, lengths, w_query, gain)

    rows = exchange(spread_rows, "mp", shards, FIRST_SHARD)

    tiles = jax.ShapeDtypeStruct((requests * GROUP, wide), BF16)
    query, new_tile, own = call(
        functools.partial(query_kernel, head_dim),
        "query",
        (tiles, turn, turn),
        [VMEM] * 5 + [HBM],
        [
            pltpu.VMEM(tiles.shape, BF16),
            pltpu.VMEM(w_keyval.shape, BF16),
            pltpu.SemaphoreType.DMA((2,)),
        ],
        out_specs=(HBM, VMEM, VMEM),
    )(rows, held_gain, held_query, cosine, sine, w_keyval)

    queries = exchange(query, "pool", pools, FIRST)

    lengths, block_slot, own, new_tile = lax.optimization_barrier(
        (lengths, block_slot, own, new_tile)
    )
    new_kv = new_tile[:1].astype(BF16)
    table, held_cache = call(
        functools.partial(table_kernel, slots_here, block_len),
        "slot_table",
        (
            jax.ShapeDtypeStruct((slots_here, block_slot.shape[1]), jnp.int32),
            jax.ShapeDtypeStruct(cache.shape, BF16),
        ),
        [HBM] * 3,
        [
            pltpu.SMEM(lengths.shape, jnp.int32),
            pltpu.VMEM(block_slot.shape, jnp.int32),
            pltpu.SemaphoreType.DMA((3,)),
        ],
    )(far(lengths), far(block_slot), cache)
    table, new_kv = lax.optimization_barrier((table[:, 0], new_kv))

    per_request = pltpu.VMEM((requests, 8, wide), F32)
    partial = call(
        attend_kernel,
        "attend",
        tiles,
        [SMEM, VMEM, VMEM],
        [
            per_request,
            pltpu.VMEM((slots_here // 2, 8, block_len), F32),
            per_request,
            per_request,
        ],
        limit=12 << 20,
    )(table, queries, held_cache)

    got = exchange(partial, "pool", pools, FIRST)

    mixed = call(
        combine_kernel,
        "combine",
        jax.ShapeDtypeStruct((shards * lines, wide), F32),
        [VMEM, VMEM, VMEM],
    )(got, own, w_out)

    spread = exchange(mixed, "mp", shards, FIRST_SHARD)
    total = jnp.sum(spread.reshape(shards, features), axis=0, keepdims=True)
    return (hidden + RESIDUAL_SCALE * total, new_kv)


def solution(mesh):
    return jax.shard_map(
        per_device,
        mesh=mesh,
        in_specs=(
            P("pool", "mp"),
            P(),
            P(None, "mp"),
            P(None, "mp"),
            P("mp", None),
            P("pool", "mp", None, None),
            P(),
            P(),
        ),
        out_specs=(P("pool", "mp"), P("pool", "mp")),
        check_vma=False,
    )
```

```python
import functools
import math

import jax
import jax.numpy as jnp
from jax import lax
from jax.experimental import pallas as pl
from jax.experimental.pallas import tpu as pltpu
from jax.sharding import PartitionSpec as P

EPSILON = 1e-05
RESIDUAL_SCALE = 0.22
SCORE_SCALE = 0.015625
ROPE_BASE = 10000000.0
MASKED = -1e30

F32 = jnp.float32
BF16 = jnp.bfloat16
VMEM = pl.BlockSpec(memory_space=pltpu.VMEM)
SMEM = pl.BlockSpec(memory_space=pltpu.SMEM)
HBM = pl.BlockSpec(memory_space=pltpu.HBM)

GROUP = 4
TERM = 8

FIRST = 36
FIRST_SHARD = 4


def far(x):
    return pltpu.with_memory_space_constraint(x, pltpu.HBM)


def lanes(shape):
    return lax.broadcasted_iota(jnp.int32, shape, len(shape) - 1)


def subs(shape):
    return lax.broadcasted_iota(jnp.int32, shape, len(shape) - 2)


def call(body, name, out_shape, in_specs, scratch=(), limit=4 << 20, out_specs=None):
    many = isinstance(out_shape, tuple)
    return pl.pallas_call(
        body,
        out_shape=out_shape,
        in_specs=in_specs,
        out_specs=out_specs or ((VMEM,) * len(out_shape) if many else VMEM),
        scratch_shapes=list(scratch),
        compiler_params=pltpu.CompilerParams(vmem_limit_bytes=limit),
        name=name,
    )


def sine_cosine(angle):
    turn = jnp.floor(angle * (2.0 / math.pi) + 0.5)
    x = ((angle - turn * 1.5703125) - turn * 4.837512969970703e-4) - turn * 7.54978995489188e-8
    z = x * x
    sine = ((-1.9515295891e-4 * z + 8.3321608736e-3) * z - 1.6666654611e-1) * z * x + x
    cosine = ((2.443315711809948e-5 * z - 1.388731625493765e-3) * z + 4.166664568298827e-2) * z * z
    cosine = cosine - 0.5 * z + 1.0
    quadrant = turn.astype(jnp.int32) & 3
    odd = (quadrant & 1) == 1
    out_sine = jnp.where(odd, cosine, sine)
    out_cosine = jnp.where(odd, sine, cosine)
    out_sine = jnp.where(quadrant >= 2, -out_sine, out_sine)
    out_cosine = jnp.where((quadrant == 1) | (quadrant == 2), -out_cosine, out_cosine)
    return out_sine, out_cosine


def rotation(position, head_dim, width):
    half = head_dim // 2
    lane = lanes((8, width))
    pair = lane % half
    inverse = jnp.zeros((8, width), F32)
    for i in range(half):
        inverse = jnp.where(pair == i, ROPE_BASE ** (-2.0 * i / head_dim), inverse)
    sine, cosine = sine_cosine(position.astype(F32) * inverse)
    return cosine, jnp.where(lane % head_dim < half, -sine, sine)


def rope(x, cosine, sine, half):
    ahead = pltpu.roll(x, x.shape[1] - half, 1)
    behind = pltpu.roll(x, half, 1)
    first = lanes(x.shape) % (2 * half) < half
    return x * cosine + jnp.where(first, ahead, behind) * sine


def normalise(rows_ref, gain_ref):
    count = rows_ref.shape[0]
    x = rows_ref[...]
    total = jnp.sum(jnp.sum(x * x, axis=0, keepdims=True), axis=1, keepdims=True)
    scale = lax.rsqrt(total * (1.0 / x.size) + EPSILON)
    half = count // 2
    even = pl.ds(0, half, stride=2)
    odd = pl.ds(1, half, stride=2)
    left = pltpu.roll(rows_ref[even, :], FIRST_SHARD, 0) * scale * gain_ref[even, :]
    right = pltpu.roll(rows_ref[odd, :], FIRST_SHARD, 0) * scale * gain_ref[odd, :]
    return jnp.concatenate([left, right], axis=1)


def project(normed, weight_ref):
    chunks, wide = normed.shape
    row = subs(normed.shape)
    out = None
    for j in range(chunks):
        part = jnp.dot(
            jnp.where(row == j, normed, 0.0).astype(BF16),
            weight_ref[pl.ds(j * wide, wide), :],
            preferred_element_type=F32,
        )
        out = part if out is None else out + part
    return jnp.broadcast_to(jnp.sum(out, axis=0, keepdims=True), out.shape)


def fetch(sources, targets, sems):
    copies = [pltpu.make_async_copy(s, t, sems.at[i]) for i, (s, t) in enumerate(zip(sources, targets))]
    for copy in copies:
        copy.start()
    return copies


def wait(copies):
    for copy in copies:
        copy.wait()


def prepare_kernel(head_dim, x_ref, lengths_ref, *rest):
    sources, (spread_ref, *targets) = rest[:2], rest[2:5]
    cos_ref, sin_ref, near_x, near_lengths, sems = rest[5:]
    copies = fetch((x_ref, lengths_ref, *sources), (near_x, near_lengths, *targets), sems)
    wait(copies[1:2])
    position = near_lengths[lax.axis_index("pool")]
    cos_ref[...], sin_ref[...] = rotation(position, head_dim, 2 * head_dim)
    wait(copies[:1])
    size = near_x.shape[0]
    for i in range(spread_ref.shape[0] // size):
        spread_ref[pl.ds(i * size, size), :] = near_x[...]
    wait(copies[2:])


def query_kernel(head_dim, rows_ref, gain_ref, w_ref, cos_ref, sin_ref, out_ref):
    wide = 2 * head_dim
    cosine, sine = cos_ref[...], sin_ref[...]
    query = project(normalise(rows_ref, gain_ref), w_ref)
    row = subs((8, wide)) % GROUP
    tile = jnp.zeros((8, wide), F32)
    for c in range(GROUP // 2):
        part = rope(query[:, c * wide : (c + 1) * wide], cosine, sine, head_dim // 2)
        tile = jnp.where(row == 2 * c, part, tile)
        tile = jnp.where(row == 2 * c + 1, pltpu.roll(part, head_dim, 1), tile)
    tile = tile.astype(BF16).astype(F32) * SCORE_SCALE
    tile = jnp.where(lanes(tile.shape) < head_dim, tile, 0.0).astype(BF16)
    for v in range(out_ref.shape[0] // 8):
        out_ref[pl.ds(8 * v, 8), :] = tile


def find_slots(slots_here, block_len, lengths_ref, slot_ref, out_ref):
    requests, blocks = slot_ref.shape
    base = lax.axis_index("pool") * slots_here
    sub = subs((8, blocks))
    lane = lanes((8, blocks))
    wanted, payload = [], []
    for v in range(requests // 8):
        length = jnp.zeros((8, blocks), jnp.int32)
        for i in range(8):
            length = jnp.where(sub == i, lengths_ref[8 * v + i], length)
        limit = length - lane * block_len
        here = slot_ref[pl.ds(8 * v, 8), :] - base
        wanted.append(jnp.where(limit > 0, here, -1))
        payload.append(
            ((sub + 8 * v + requests - FIRST) % requests) * 256 + jnp.minimum(limit, block_len)
        )
    for tile in range(slots_here // 8):
        picked = jnp.zeros((8, blocks), jnp.int32)
        for i in range(8):
            found = jnp.zeros((8, blocks), jnp.int32)
            for w, p in zip(wanted, payload):
                found = jnp.where(w == 8 * tile + i, p, found)
            picked = jnp.where(sub == i, jnp.max(found, axis=0, keepdims=True), picked)
        out_ref[pl.ds(8 * tile, 8), :] = jnp.broadcast_to(
            jnp.max(picked.astype(F32), axis=1, keepdims=True), (8, blocks)
        ).astype(jnp.int32)


def window_kernel(slots_here, block_len, head_dim, rows_ref, gain_ref, cos_ref, sin_ref, *rest):
    sources, (table_ref, held_ref, kv_ref, own_ref) = rest[:5], rest[5:9]
    lengths_ref, slot_ref, query_ref, w_ref, sems = rest[9:]
    lengths_hbm, slot_hbm, query_hbm, w_hbm, cache_ref = sources
    copies = fetch(
        (lengths_hbm, slot_hbm, query_hbm.at[pl.ds(0, query_ref.shape[0])], w_hbm, cache_ref),
        (lengths_ref, slot_ref, query_ref, w_ref, held_ref),
        sems,
    )
    normed = normalise(rows_ref, gain_ref)
    wait(copies[:4])
    keyval = project(normed, w_ref)
    is_key = lanes(keyval.shape) < head_dim
    turned = rope(keyval, cos_ref[...], sin_ref[...], head_dim // 2)
    both = jnp.where(is_key, turned, keyval).astype(BF16)
    kv_ref[...] = both[:1]
    both = both.astype(F32)
    score = jnp.sum(query_ref[:8, :].astype(F32) * both, axis=1, keepdims=True)
    own_ref[...] = jnp.where(is_key, score, both)
    find_slots(slots_here, block_len, lengths_ref, slot_ref, table_ref)
    wait(copies[4:])


def attend_kernel(
    tab_ref, query_ref, kv_ref, out_ref, q_s, score_s, max_s, acc_s
):
    slots_here, block_len, wide = kv_ref.shape
    requests = query_ref.shape[0] // GROUP
    low = subs((8, wide)) < GROUP
    token = lanes((8, block_len))
    lane = lanes((8, wide))
    for v in range(requests // 2):
        tile = query_ref[pl.ds(8 * v, 8), :].astype(F32)
        other = pltpu.roll(tile, GROUP, 0)
        q_s[2 * v] = jnp.where(low, tile, other)
        q_s[2 * v + 1] = jnp.where(low, other, tile)
    max_s[...] = jnp.full_like(max_s, MASKED)
    acc_s[...] = jnp.zeros_like(acc_s)

    def pair(p):
        a, b = tab_ref[2 * p], tab_ref[2 * p + 1]
        live = token < jnp.where(low, a & 255, b & 255)
        keys = kv_ref[pl.ds(2 * p, 2)].reshape(2 * block_len, wide)
        return lax.shift_right_logical(a, 8), lax.shift_right_logical(b, 8), live, keys

    for p in range(slots_here // 2):
        ra, rb, live, keys = pair(p)
        query = jnp.where(low, q_s[ra], q_s[rb]).astype(BF16)
        scores = lax.dot_general(
            query, keys, (((1,), (1,)), ((), ())), preferred_element_type=F32
        )
        scores = jnp.where(low, scores[:, :block_len], scores[:, block_len:])
        scores = jnp.where(live, scores, MASKED)
        score_s[p] = scores
        top = jnp.broadcast_to(jnp.max(scores, axis=1, keepdims=True), scores.shape)
        other = pltpu.roll(top, GROUP, 0)
        max_s[ra] = jnp.maximum(max_s[ra], jnp.where(low, top, other))
        max_s[rb] = jnp.maximum(max_s[rb], jnp.where(low, other, top))

    for p in range(slots_here // 2):
        ra, rb, live, values = pair(p)
        top = jnp.where(low, max_s[ra], max_s[rb])
        weight = jnp.where(live, jnp.exp(score_s[p] - top), 0.0).astype(BF16).astype(F32)
        both = jnp.concatenate(
            [jnp.where(low, weight, 0.0), jnp.where(low, 0.0, weight)], axis=1
        ).astype(BF16)
        out = jnp.dot(both, values, preferred_element_type=F32)
        total = jnp.sum(weight, axis=1, keepdims=True)
        out = jnp.where(lane < wide // 2, total, out)
        other = pltpu.roll(out, GROUP, 0)
        acc_s[ra] = acc_s[ra] + jnp.where(low, out, other)
        acc_s[rb] = acc_s[rb] + jnp.where(low, other, out)

    for v in range(requests // 2):
        top = jnp.where(low, max_s[2 * v], max_s[2 * v + 1])
        out = jnp.where(low, acc_s[2 * v], acc_s[2 * v + 1])
        out = jnp.where(lane < wide // 4, top, out)
        terms = []
        for _ in range(3):
            terms.append(out.astype(BF16).astype(F32))
            out = out - terms[-1]
        third = (lane % (wide // 4)) // TERM
        out = jnp.where(
            (lane >= wide // 2) | (third == 0),
            terms[0],
            jnp.where(third == 1, terms[1], terms[2]),
        )
        out_ref[pl.ds(8 * v, 8), :] = out.astype(BF16)


def combine_kernel(got_ref, own_ref, w_ref, out_ref):
    rows, wide = got_ref.shape
    lane = lanes((8, wide))
    row = subs((8, wide))
    parts = []
    for v in range(rows // 8):
        part = got_ref[pl.ds(8 * v, 8), :].astype(F32)
        whole = part + pltpu.roll(part, wide - TERM, 1) + pltpu.roll(part, wide - 2 * TERM, 1)
        parts.append(jnp.where(lane < wide // 2, whole, part))
    top = parts[0]
    for part in parts[1:]:
        top = jnp.maximum(top, part)
    own = own_ref[...]
    top = jnp.maximum(jnp.maximum(top, pltpu.roll(top, GROUP, 0)), own)
    mixed = jnp.zeros((8, wide), F32)
    for part in parts:
        weight = jnp.exp(part - top)
        mixed = mixed + jnp.broadcast_to(weight[:, :1], part.shape) * part
    mixed = mixed + pltpu.roll(mixed, GROUP, 0)
    own_weight = jnp.exp(own - top)
    mixed = mixed + jnp.broadcast_to(own_weight[:, :1], own.shape) * jnp.where(
        lane < wide // 2, 1.0, own
    )
    attended = mixed / jnp.broadcast_to(mixed[:, wide // 4 : wide // 4 + 1], mixed.shape)
    swapped = pltpu.roll(attended, wide // 2, 1)
    placed = jnp.where(
        row % 2 == 0,
        jnp.where(lane < wide // 2, swapped, 0.0),
        jnp.where(lane < wide // 2, 0.0, attended),
    )
    chunks = [
        jnp.sum(jnp.where(row // 2 == c, placed, 0.0), axis=0, keepdims=True)
        for c in range(GROUP // 2)
    ]
    line = jnp.broadcast_to(jnp.concatenate(chunks, axis=1), (8, GROUP // 2 * wide)).astype(BF16)
    lines = out_ref.shape[0]
    for v in range(lines // 8):
        at = (8 * v + FIRST_SHARD * GROUP // 2) % lines * wide
        part = jnp.dot(line, w_ref[:, pl.ds(at, 8 * wide)], preferred_element_type=F32)
        tile = jnp.zeros((8, wide), F32)
        for k in range(8):
            tile = jnp.where(row == k, part[:, k * wide : (k + 1) * wide], tile)
        out_ref[pl.ds(8 * v, 8), :] = tile


def exchange(x, axis, parts, first=0):
    shape = x.shape
    x = x.reshape(parts, shape[0] // parts, shape[1])
    groups = [[(i + first) % parts for i in range(parts)]] if first else None
    return lax.all_to_all(
        x, axis, split_axis=0, concat_axis=0, tiled=True, axis_index_groups=groups
    ).reshape(shape)


def per_device(hidden, norm_gain, w_query, w_keyval, w_out, kv_cache, block_slot, lengths):
    slots_here, _, block_len, wide = kv_cache.shape
    head_dim = wide // 2
    requests = block_slot.shape[0]
    shards = lax.axis_size("mp")
    pools = lax.axis_size("pool")
    features = hidden.shape[1]
    lines = features // wide
    gain = far(norm_gain.reshape(shards * lines, wide))
    cache = far(kv_cache.reshape(slots_here, block_len, wide))
    line = far(hidden.reshape(lines, wide))
    w_query, w_keyval, lengths, block_slot = (
        far(x) for x in (w_query, w_keyval, lengths, block_slot)
    )
    turn = jax.ShapeDtypeStruct((8, wide), F32)
    spread_rows, held_query, held_gain, cosine, sine = call(
        functools.partial(prepare_kernel, head_dim),
        "prepare",
        (
            jax.ShapeDtypeStruct((shards * lines, wide), F32),
            jax.ShapeDtypeStruct(w_query.shape, BF16),
            jax.ShapeDtypeStruct(gain.shape, F32),
            turn,
            turn,
        ),
        [HBM] * 4,
        [
            pltpu.VMEM((lines, wide), F32),
            pltpu.SMEM(lengths.shape, jnp.int32),
            pltpu.SemaphoreType.DMA((4,)),
        ],
    )(line, lengths, w_query, gain)

    rows = exchange(spread_rows, "mp", shards, FIRST_SHARD)

    tiles = jax.ShapeDtypeStruct((requests * GROUP, wide), BF16)
    query = call(
        functools.partial(query_kernel, head_dim), "query", tiles, [VMEM] * 5
    )(rows, held_gain, held_query, cosine, sine)

    queries = exchange(query, "pool", pools, FIRST)

    table, held_cache, new_kv, own = call(
        functools.partial(window_kernel, slots_here, block_len, head_dim),
        "window",
        (
            jax.ShapeDtypeStruct((slots_here, block_slot.shape[1]), jnp.int32),
            jax.ShapeDtypeStruct(cache.shape, BF16),
            jax.ShapeDtypeStruct((1, wide), BF16),
            turn,
        ),
        [VMEM] * 4 + [HBM] * 5,
        [
            pltpu.SMEM(lengths.shape, jnp.int32),
            pltpu.VMEM(block_slot.shape, jnp.int32),
            pltpu.VMEM((16, wide), BF16),
            pltpu.VMEM(w_keyval.shape, BF16),
            pltpu.SemaphoreType.DMA((5,)),
        ],
        limit=8 << 20,
    )(rows, held_gain, cosine, sine, lengths, block_slot, far(query), w_keyval, cache)
    table = table[:, 0]

    per_request = pltpu.VMEM((requests, 8, wide), F32)
    partial = call(
        attend_kernel,
        "attend",
        tiles,
        [SMEM, VMEM, VMEM],
        [
            per_request,
            pltpu.VMEM((slots_here // 2, 8, block_len), F32),
            per_request,
            per_request,
        ],
        limit=12 << 20,
    )(table, queries, held_cache)

    got = exchange(partial, "pool", pools, FIRST)

    mixed = call(
        combine_kernel,
        "combine",
        jax.ShapeDtypeStruct((shards * lines, wide), F32),
        [VMEM, VMEM, VMEM],
    )(got, own, w_out)

    spread = exchange(mixed, "mp", shards, FIRST_SHARD)
    total = jnp.sum(spread.reshape(shards, features), axis=0, keepdims=True)
    return (hidden + RESIDUAL_SCALE * total, new_kv)


def solution(mesh):
    return jax.shard_map(
        per_device,
        mesh=mesh,
        in_specs=(
            P("pool", "mp"),
            P(),
            P(None, "mp"),
            P(None, "mp"),
            P("mp", None),
            P("pool", "mp", None, None),
            P(),
            P(),
        ),
        out_specs=(P("pool", "mp"), P("pool", "mp")),
        check_vma=False,
    )
```

```python
import functools
import math

import jax
import jax.numpy as jnp
from jax import lax
from jax.experimental import pallas as pl
from jax.experimental.pallas import tpu as pltpu
from jax.sharding import PartitionSpec as P

EPSILON = 1e-05
RESIDUAL_SCALE = 0.22
SCORE_SCALE = 0.015625
ROPE_BASE = 10000000.0
MASKED = -1e30

F32 = jnp.float32
BF16 = jnp.bfloat16
VMEM = pl.BlockSpec(memory_space=pltpu.VMEM)
SMEM = pl.BlockSpec(memory_space=pltpu.SMEM)
HBM = pl.BlockSpec(memory_space=pltpu.HBM)

GROUP = 4
TERM = 8

FIRST_QUERY = 62
FIRST_PARTIAL = 36
FIRST_SHARD = 4


def far(x):
    return pltpu.with_memory_space_constraint(x, pltpu.HBM)


def lanes(shape):
    return lax.broadcasted_iota(jnp.int32, shape, len(shape) - 1)


def subs(shape):
    return lax.broadcasted_iota(jnp.int32, shape, len(shape) - 2)


def call(body, name, out_shape, in_specs, scratch=(), limit=4 << 20, out_specs=None):
    many = isinstance(out_shape, tuple)
    return pl.pallas_call(
        body,
        out_shape=out_shape,
        in_specs=in_specs,
        out_specs=out_specs or ((VMEM,) * len(out_shape) if many else VMEM),
        scratch_shapes=list(scratch),
        compiler_params=pltpu.CompilerParams(vmem_limit_bytes=limit),
        name=name,
    )


def sine_cosine(angle):
    turn = jnp.floor(angle * (2.0 / math.pi) + 0.5)
    x = ((angle - turn * 1.5703125) - turn * 4.837512969970703e-4) - turn * 7.54978995489188e-8
    z = x * x
    sine = ((-1.9515295891e-4 * z + 8.3321608736e-3) * z - 1.6666654611e-1) * z * x + x
    cosine = ((2.443315711809948e-5 * z - 1.388731625493765e-3) * z + 4.166664568298827e-2) * z * z
    cosine = cosine - 0.5 * z + 1.0
    quadrant = turn.astype(jnp.int32) & 3
    odd = (quadrant & 1) == 1
    out_sine = jnp.where(odd, cosine, sine)
    out_cosine = jnp.where(odd, sine, cosine)
    out_sine = jnp.where(quadrant >= 2, -out_sine, out_sine)
    out_cosine = jnp.where((quadrant == 1) | (quadrant == 2), -out_cosine, out_cosine)
    return out_sine, out_cosine


def rotation(position, head_dim, width):
    half = head_dim // 2
    lane = lanes((8, width))
    pair = lane % half
    inverse = jnp.zeros((8, width), F32)
    for i in range(half):
        inverse = jnp.where(pair == i, ROPE_BASE ** (-2.0 * i / head_dim), inverse)
    sine, cosine = sine_cosine(position.astype(F32) * inverse)
    return cosine, jnp.where(lane % head_dim < half, -sine, sine)


def rope(x, cosine, sine, half):
    ahead = pltpu.roll(x, x.shape[1] - half, 1)
    behind = pltpu.roll(x, half, 1)
    first = lanes(x.shape) % (2 * half) < half
    return x * cosine + jnp.where(first, ahead, behind) * sine


def normalise(rows_ref, gain_ref):
    count = rows_ref.shape[0]
    x = rows_ref[...]
    total = jnp.sum(jnp.sum(x * x, axis=0, keepdims=True), axis=1, keepdims=True)
    scale = lax.rsqrt(total * (1.0 / x.size) + EPSILON)
    half = count // 2
    even = pl.ds(0, half, stride=2)
    odd = pl.ds(1, half, stride=2)
    left = pltpu.roll(rows_ref[even, :], FIRST_SHARD, 0) * scale * gain_ref[even, :]
    right = pltpu.roll(rows_ref[odd, :], FIRST_SHARD, 0) * scale * gain_ref[odd, :]
    return jnp.concatenate([left, right], axis=1)


def project(normed, weight_ref):
    chunks, wide = normed.shape
    row = subs(normed.shape)
    out = None
    for j in range(chunks):
        part = jnp.dot(
            jnp.where(row == j, normed, 0.0).astype(BF16),
            weight_ref[pl.ds(j * wide, wide), :],
            preferred_element_type=F32,
        )
        out = part if out is None else out + part
    return jnp.broadcast_to(jnp.sum(out, axis=0, keepdims=True), out.shape)


def fetch(sources, targets, sems):
    copies = [pltpu.make_async_copy(s, t, sems.at[i]) for i, (s, t) in enumerate(zip(sources, targets))]
    for copy in copies:
        copy.start()
    return copies


def wait(copies):
    for copy in copies:
        copy.wait()


def prepare_kernel(head_dim, x_ref, lengths_ref, *rest):
    sources, (spread_ref, *targets) = rest[:2], rest[2:5]
    cos_ref, sin_ref, near_x, near_lengths, sems = rest[5:]
    copies = fetch((x_ref, lengths_ref, *sources), (near_x, near_lengths, *targets), sems)
    wait(copies[1:2])
    position = near_lengths[lax.axis_index("pool")]
    cos_ref[...], sin_ref[...] = rotation(position, head_dim, 2 * head_dim)
    wait(copies[:1])
    size = near_x.shape[0]
    for i in range(spread_ref.shape[0] // size):
        spread_ref[pl.ds(i * size, size), :] = near_x[...]
    wait(copies[2:])


def query_kernel(head_dim, rows_ref, gain_ref, w_ref, cos_ref, sin_ref, out_ref):
    wide = 2 * head_dim
    cosine, sine = cos_ref[...], sin_ref[...]
    query = project(normalise(rows_ref, gain_ref), w_ref)
    row = subs((8, wide)) % GROUP
    tile = jnp.zeros((8, wide), F32)
    for c in range(GROUP // 2):
        part = rope(query[:, c * wide : (c + 1) * wide], cosine, sine, head_dim // 2)
        tile = jnp.where(row == 2 * c, part, tile)
        tile = jnp.where(row == 2 * c + 1, pltpu.roll(part, head_dim, 1), tile)
    tile = tile.astype(BF16).astype(F32) * SCORE_SCALE
    tile = jnp.where(lanes(tile.shape) < head_dim, tile, 0.0).astype(BF16)
    for v in range(out_ref.shape[0] // 8):
        out_ref[pl.ds(8 * v, 8), :] = tile


def find_slots(slots_here, block_len, lengths_ref, slot_ref, out_ref):
    requests, blocks = slot_ref.shape
    base = lax.axis_index("pool") * slots_here
    sub = subs((8, blocks))
    lane = lanes((8, blocks))
    wanted, payload = [], []
    for v in range(requests // 8):
        length = jnp.zeros((8, blocks), jnp.int32)
        for i in range(8):
            length = jnp.where(sub == i, lengths_ref[8 * v + i], length)
        limit = length - lane * block_len
        here = slot_ref[pl.ds(8 * v, 8), :] - base
        wanted.append(jnp.where(limit > 0, here, -1))
        payload.append(
            ((sub + 8 * v + requests - FIRST_QUERY) % requests) * 256 + jnp.minimum(limit, block_len)
        )
    for tile in range(slots_here // 8):
        picked = jnp.zeros((8, blocks), jnp.int32)
        for i in range(8):
            found = jnp.zeros((8, blocks), jnp.int32)
            for w, p in zip(wanted, payload):
                found = jnp.where(w == 8 * tile + i, p, found)
            picked = jnp.where(sub == i, jnp.max(found, axis=0, keepdims=True), picked)
        out_ref[pl.ds(8 * tile, 8), :] = jnp.broadcast_to(
            jnp.max(picked.astype(F32), axis=1, keepdims=True), (8, blocks)
        ).astype(jnp.int32)


def window_kernel(slots_here, block_len, head_dim, rows_ref, gain_ref, cos_ref, sin_ref, *rest):
    sources, (table_ref, held_ref, kv_ref, own_ref) = rest[:5], rest[5:9]
    lengths_ref, slot_ref, query_ref, w_ref, sems = rest[9:]
    lengths_hbm, slot_hbm, query_hbm, w_hbm, cache_ref = sources
    copies = fetch(
        (lengths_hbm, slot_hbm, query_hbm.at[pl.ds(0, query_ref.shape[0])], w_hbm, cache_ref),
        (lengths_ref, slot_ref, query_ref, w_ref, held_ref),
        sems,
    )
    normed = normalise(rows_ref, gain_ref)
    wait(copies[:4])
    keyval = project(normed, w_ref)
    is_key = lanes(keyval.shape) < head_dim
    turned = rope(keyval, cos_ref[...], sin_ref[...], head_dim // 2)
    both = jnp.where(is_key, turned, keyval).astype(BF16)
    kv_ref[...] = both[:1]
    both = both.astype(F32)
    score = jnp.sum(query_ref[:8, :].astype(F32) * both, axis=1, keepdims=True)
    own_ref[...] = jnp.where(is_key, score, both)
    find_slots(slots_here, block_len, lengths_ref, slot_ref, table_ref)
    wait(copies[4:])


def attend_kernel(
    tab_ref, query_ref, kv_ref, out_ref, q_s, score_s, max_s, acc_s
):
    slots_here, block_len, wide = kv_ref.shape
    requests = query_ref.shape[0] // GROUP
    low = subs((8, wide)) < GROUP
    token = lanes((8, block_len))
    lane = lanes((8, wide))
    for v in range(requests // 2):
        tile = query_ref[pl.ds(8 * v, 8), :].astype(F32)
        other = pltpu.roll(tile, GROUP, 0)
        q_s[2 * v] = jnp.where(low, tile, other)
        q_s[2 * v + 1] = jnp.where(low, other, tile)
    max_s[...] = jnp.full_like(max_s, MASKED)
    acc_s[...] = jnp.zeros_like(acc_s)

    def pair(p):
        a, b = tab_ref[2 * p], tab_ref[2 * p + 1]
        live = token < jnp.where(low, a & 255, b & 255)
        keys = kv_ref[pl.ds(2 * p, 2)].reshape(2 * block_len, wide)
        return lax.shift_right_logical(a, 8), lax.shift_right_logical(b, 8), live, keys

    for p in range(slots_here // 2):
        ra, rb, live, keys = pair(p)
        query = jnp.where(low, q_s[ra], q_s[rb]).astype(BF16)
        scores = lax.dot_general(
            query, keys, (((1,), (1,)), ((), ())), preferred_element_type=F32
        )
        scores = jnp.where(low, scores[:, :block_len], scores[:, block_len:])
        scores = jnp.where(live, scores, MASKED)
        score_s[p] = scores
        top = jnp.broadcast_to(jnp.max(scores, axis=1, keepdims=True), scores.shape)
        other = pltpu.roll(top, GROUP, 0)
        max_s[ra] = jnp.maximum(max_s[ra], jnp.where(low, top, other))
        max_s[rb] = jnp.maximum(max_s[rb], jnp.where(low, other, top))

    for p in range(slots_here // 2):
        ra, rb, live, values = pair(p)
        top = jnp.where(low, max_s[ra], max_s[rb])
        weight = jnp.where(live, jnp.exp(score_s[p] - top), 0.0).astype(BF16).astype(F32)
        both = jnp.concatenate(
            [jnp.where(low, weight, 0.0), jnp.where(low, 0.0, weight)], axis=1
        ).astype(BF16)
        out = jnp.dot(both, values, preferred_element_type=F32)
        total = jnp.sum(weight, axis=1, keepdims=True)
        out = jnp.where(lane < wide // 2, total, out)
        other = pltpu.roll(out, GROUP, 0)
        acc_s[ra] = acc_s[ra] + jnp.where(low, out, other)
        acc_s[rb] = acc_s[rb] + jnp.where(low, other, out)

    for v in range(requests // 2):
        top = jnp.where(low, max_s[2 * v], max_s[2 * v + 1])
        out = jnp.where(low, acc_s[2 * v], acc_s[2 * v + 1])
        out = jnp.where(lane < wide // 4, top, out)
        terms = []
        for _ in range(3):
            terms.append(out.astype(BF16).astype(F32))
            out = out - terms[-1]
        third = (lane % (wide // 4)) // TERM
        out = jnp.where(
            (lane >= wide // 2) | (third == 0),
            terms[0],
            jnp.where(third == 1, terms[1], terms[2]),
        )
        at = (2 * v + FIRST_QUERY - FIRST_PARTIAL) % requests // 2
        out_ref[pl.ds(8 * at, 8), :] = out.astype(BF16)


def combine_kernel(got_ref, own_ref, w_ref, out_ref):
    rows, wide = got_ref.shape
    lane = lanes((8, wide))
    row = subs((8, wide))
    parts = []
    for v in range(rows // 8):
        part = got_ref[pl.ds(8 * v, 8), :].astype(F32)
        whole = part + pltpu.roll(part, wide - TERM, 1) + pltpu.roll(part, wide - 2 * TERM, 1)
        parts.append(jnp.where(lane < wide // 2, whole, part))
    top = parts[0]
    for part in parts[1:]:
        top = jnp.maximum(top, part)
    own = own_ref[...]
    top = jnp.maximum(jnp.maximum(top, pltpu.roll(top, GROUP, 0)), own)
    mixed = jnp.zeros((8, wide), F32)
    for part in parts:
        weight = jnp.exp(part - top)
        mixed = mixed + jnp.broadcast_to(weight[:, :1], part.shape) * part
    mixed = mixed + pltpu.roll(mixed, GROUP, 0)
    own_weight = jnp.exp(own - top)
    mixed = mixed + jnp.broadcast_to(own_weight[:, :1], own.shape) * jnp.where(
        lane < wide // 2, 1.0, own
    )
    attended = mixed / jnp.broadcast_to(mixed[:, wide // 4 : wide // 4 + 1], mixed.shape)
    swapped = pltpu.roll(attended, wide // 2, 1)
    placed = jnp.where(
        row % 2 == 0,
        jnp.where(lane < wide // 2, swapped, 0.0),
        jnp.where(lane < wide // 2, 0.0, attended),
    )
    chunks = [
        jnp.sum(jnp.where(row // 2 == c, placed, 0.0), axis=0, keepdims=True)
        for c in range(GROUP // 2)
    ]
    line = jnp.broadcast_to(jnp.concatenate(chunks, axis=1), (8, GROUP // 2 * wide)).astype(BF16)
    lines = out_ref.shape[0]
    for v in range(lines // 8):
        at = (8 * v + FIRST_SHARD * GROUP // 2) % lines * wide
        part = jnp.dot(line, w_ref[:, pl.ds(at, 8 * wide)], preferred_element_type=F32)
        tile = jnp.zeros((8, wide), F32)
        for k in range(8):
            tile = jnp.where(row == k, part[:, k * wide : (k + 1) * wide], tile)
        out_ref[pl.ds(8 * v, 8), :] = tile


def exchange(x, axis, parts, first=0):
    shape = x.shape
    x = x.reshape(parts, shape[0] // parts, shape[1])
    groups = [[(i + first) % parts for i in range(parts)]] if first else None
    return lax.all_to_all(
        x, axis, split_axis=0, concat_axis=0, tiled=True, axis_index_groups=groups
    ).reshape(shape)


def per_device(hidden, norm_gain, w_query, w_keyval, w_out, kv_cache, block_slot, lengths):
    slots_here, _, block_len, wide = kv_cache.shape
    head_dim = wide // 2
    requests = block_slot.shape[0]
    shards = lax.axis_size("mp")
    pools = lax.axis_size("pool")
    features = hidden.shape[1]
    lines = features // wide
    gain = far(norm_gain.reshape(shards * lines, wide))
    cache = far(kv_cache.reshape(slots_here, block_len, wide))
    line = far(hidden.reshape(lines, wide))
    w_query, w_keyval, lengths, block_slot = (
        far(x) for x in (w_query, w_keyval, lengths, block_slot)
    )
    turn = jax.ShapeDtypeStruct((8, wide), F32)
    spread_rows, held_query, held_gain, cosine, sine = call(
        functools.partial(prepare_kernel, head_dim),
        "prepare",
        (
            jax.ShapeDtypeStruct((shards * lines, wide), F32),
            jax.ShapeDtypeStruct(w_query.shape, BF16),
            jax.ShapeDtypeStruct(gain.shape, F32),
            turn,
            turn,
        ),
        [HBM] * 4,
        [
            pltpu.VMEM((lines, wide), F32),
            pltpu.SMEM(lengths.shape, jnp.int32),
            pltpu.SemaphoreType.DMA((4,)),
        ],
    )(line, lengths, w_query, gain)

    rows = exchange(spread_rows, "mp", shards, FIRST_SHARD)

    tiles = jax.ShapeDtypeStruct((requests * GROUP, wide), BF16)
    query = call(
        functools.partial(query_kernel, head_dim), "query", tiles, [VMEM] * 5
    )(rows, held_gain, held_query, cosine, sine)

    queries = exchange(query, "pool", pools, FIRST_QUERY)

    table, held_cache, new_kv, own = call(
        functools.partial(window_kernel, slots_here, block_len, head_dim),
        "window",
        (
            jax.ShapeDtypeStruct((slots_here, block_slot.shape[1]), jnp.int32),
            jax.ShapeDtypeStruct(cache.shape, BF16),
            jax.ShapeDtypeStruct((1, wide), BF16),
            turn,
        ),
        [VMEM] * 4 + [HBM] * 5,
        [
            pltpu.SMEM(lengths.shape, jnp.int32),
            pltpu.VMEM(block_slot.shape, jnp.int32),
            pltpu.VMEM((16, wide), BF16),
            pltpu.VMEM(w_keyval.shape, BF16),
            pltpu.SemaphoreType.DMA((5,)),
        ],
        limit=8 << 20,
    )(rows, held_gain, cosine, sine, lengths, block_slot, far(query), w_keyval, cache)
    table = table[:, 0]

    per_request = pltpu.VMEM((requests, 8, wide), F32)
    partial = call(
        attend_kernel,
        "attend",
        tiles,
        [SMEM, VMEM, VMEM],
        [
            per_request,
            pltpu.VMEM((slots_here // 2, 8, block_len), F32),
            per_request,
            per_request,
        ],
        limit=12 << 20,
    )(table, queries, held_cache)

    got = exchange(partial, "pool", pools, FIRST_PARTIAL)

    mixed = call(
        combine_kernel,
        "combine",
        jax.ShapeDtypeStruct((shards * lines, wide), F32),
        [VMEM, VMEM, VMEM],
    )(got, own, w_out)

    spread = exchange(mixed, "mp", shards, FIRST_SHARD)
    total = jnp.sum(spread.reshape(shards, features), axis=0, keepdims=True)
    return (hidden + RESIDUAL_SCALE * total, new_kv)


def solution(mesh):
    return jax.shard_map(
        per_device,
        mesh=mesh,
        in_specs=(
            P("pool", "mp"),
            P(),
            P(None, "mp"),
            P(None, "mp"),
            P("mp", None),
            P("pool", "mp", None, None),
            P(),
            P(),
        ),
        out_specs=(P("pool", "mp"), P("pool", "mp")),
        check_vma=False,
    )
```

```python
import functools
import math

import jax
import jax.numpy as jnp
from jax import lax
from jax.experimental import pallas as pl
from jax.experimental.pallas import tpu as pltpu
from jax.sharding import PartitionSpec as P

EPSILON = 1e-05
RESIDUAL_SCALE = 0.22
SCORE_SCALE = 0.015625
ROPE_BASE = 10000000.0
MASKED = -1e30

F32 = jnp.float32
BF16 = jnp.bfloat16
VMEM = pl.BlockSpec(memory_space=pltpu.VMEM)
SMEM = pl.BlockSpec(memory_space=pltpu.SMEM)
HBM = pl.BlockSpec(memory_space=pltpu.HBM)

GROUP = 4
TERM = 8

FIRST = 36
FIRST_SHARD = 5


def far(x):
    return pltpu.with_memory_space_constraint(x, pltpu.HBM)


def lanes(shape):
    return lax.broadcasted_iota(jnp.int32, shape, len(shape) - 1)


def subs(shape):
    return lax.broadcasted_iota(jnp.int32, shape, len(shape) - 2)


def call(body, name, out_shape, in_specs, scratch=(), limit=4 << 20, out_specs=None):
    many = isinstance(out_shape, tuple)
    return pl.pallas_call(
        body,
        out_shape=out_shape,
        in_specs=in_specs,
        out_specs=out_specs or ((VMEM,) * len(out_shape) if many else VMEM),
        scratch_shapes=list(scratch),
        compiler_params=pltpu.CompilerParams(vmem_limit_bytes=limit),
        name=name,
    )


def sine_cosine(angle):
    turn = jnp.floor(angle * (2.0 / math.pi) + 0.5)
    x = ((angle - turn * 1.5703125) - turn * 4.837512969970703e-4) - turn * 7.54978995489188e-8
    z = x * x
    sine = ((-1.9515295891e-4 * z + 8.3321608736e-3) * z - 1.6666654611e-1) * z * x + x
    cosine = ((2.443315711809948e-5 * z - 1.388731625493765e-3) * z + 4.166664568298827e-2) * z * z
    cosine = cosine - 0.5 * z + 1.0
    quadrant = turn.astype(jnp.int32) & 3
    odd = (quadrant & 1) == 1
    out_sine = jnp.where(odd, cosine, sine)
    out_cosine = jnp.where(odd, sine, cosine)
    out_sine = jnp.where(quadrant >= 2, -out_sine, out_sine)
    out_cosine = jnp.where((quadrant == 1) | (quadrant == 2), -out_cosine, out_cosine)
    return out_sine, out_cosine


def rotation(position, head_dim, width):
    half = head_dim // 2
    lane = lanes((8, width))
    pair = lane % half
    inverse = jnp.zeros((8, width), F32)
    for i in range(half):
        inverse = jnp.where(pair == i, ROPE_BASE ** (-2.0 * i / head_dim), inverse)
    sine, cosine = sine_cosine(position.astype(F32) * inverse)
    return cosine, jnp.where(lane % head_dim < half, -sine, sine)


def rope(x, cosine, sine, half):
    ahead = pltpu.roll(x, x.shape[1] - half, 1)
    behind = pltpu.roll(x, half, 1)
    first = lanes(x.shape) % (2 * half) < half
    return x * cosine + jnp.where(first, ahead, behind) * sine


def normalise(rows_ref, gain_ref):
    count = rows_ref.shape[0]
    x = rows_ref[...]
    total = jnp.sum(jnp.sum(x * x, axis=0, keepdims=True), axis=1, keepdims=True)
    scale = lax.rsqrt(total * (1.0 / x.size) + EPSILON)
    half = count // 2
    even = pl.ds(0, half, stride=2)
    odd = pl.ds(1, half, stride=2)
    left = pltpu.roll(rows_ref[even, :], FIRST_SHARD, 0) * scale * gain_ref[even, :]
    right = pltpu.roll(rows_ref[odd, :], FIRST_SHARD, 0) * scale * gain_ref[odd, :]
    return jnp.concatenate([left, right], axis=1)


def project(normed, weight_ref):
    chunks, wide = normed.shape
    row = subs(normed.shape)
    out = None
    for j in range(chunks):
        part = jnp.dot(
            jnp.where(row == j, normed, 0.0).astype(BF16),
            weight_ref[pl.ds(j * wide, wide), :],
            preferred_element_type=F32,
        )
        out = part if out is None else out + part
    return jnp.broadcast_to(jnp.sum(out, axis=0, keepdims=True), out.shape)


def fetch(sources, targets, sems):
    copies = [pltpu.make_async_copy(s, t, sems.at[i]) for i, (s, t) in enumerate(zip(sources, targets))]
    for copy in copies:
        copy.start()
    return copies


def wait(copies):
    for copy in copies:
        copy.wait()


def prepare_kernel(head_dim, x_ref, lengths_ref, *rest):
    sources, (spread_ref, *targets) = rest[:2], rest[2:5]
    cos_ref, sin_ref, near_x, near_lengths, sems = rest[5:]
    copies = fetch((x_ref, lengths_ref, *sources), (near_x, near_lengths, *targets), sems)
    wait(copies[1:2])
    position = near_lengths[lax.axis_index("pool")]
    cos_ref[...], sin_ref[...] = rotation(position, head_dim, 2 * head_dim)
    wait(copies[:1])
    size = near_x.shape[0]
    for i in range(spread_ref.shape[0] // size):
        spread_ref[pl.ds(i * size, size), :] = near_x[...]
    wait(copies[2:])


def query_kernel(head_dim, rows_ref, gain_ref, w_ref, cos_ref, sin_ref, out_ref):
    wide = 2 * head_dim
    cosine, sine = cos_ref[...], sin_ref[...]
    query = project(normalise(rows_ref, gain_ref), w_ref)
    row = subs((8, wide)) % GROUP
    tile = jnp.zeros((8, wide), F32)
    for c in range(GROUP // 2):
        part = rope(query[:, c * wide : (c + 1) * wide], cosine, sine, head_dim // 2)
        tile = jnp.where(row == 2 * c, part, tile)
        tile = jnp.where(row == 2 * c + 1, pltpu.roll(part, head_dim, 1), tile)
    tile = tile.astype(BF16).astype(F32) * SCORE_SCALE
    tile = jnp.where(lanes(tile.shape) < head_dim, tile, 0.0).astype(BF16)
    for v in range(out_ref.shape[0] // 8):
        out_ref[pl.ds(8 * v, 8), :] = tile


def find_slots(slots_here, block_len, lengths_ref, slot_ref, out_ref):
    requests, blocks = slot_ref.shape
    base = lax.axis_index("pool") * slots_here
    sub = subs((8, blocks))
    lane = lanes((8, blocks))
    wanted, payload = [], []
    for v in range(requests // 8):
        length = jnp.zeros((8, blocks), jnp.int32)
        for i in range(8):
            length = jnp.where(sub == i, lengths_ref[8 * v + i], length)
        limit = length - lane * block_len
        here = slot_ref[pl.ds(8 * v, 8), :] - base
        wanted.append(jnp.where(limit > 0, here, -1))
        payload.append(
            ((sub + 8 * v + requests - FIRST) % requests) * 256 + jnp.minimum(limit, block_len)
        )
    for tile in range(slots_here // 8):
        picked = jnp.zeros((8, blocks), jnp.int32)
        for i in range(8):
            found = jnp.zeros((8, blocks), jnp.int32)
            for w, p in zip(wanted, payload):
                found = jnp.where(w == 8 * tile + i, p, found)
            picked = jnp.where(sub == i, jnp.max(found, axis=0, keepdims=True), picked)
        out_ref[pl.ds(8 * tile, 8), :] = jnp.broadcast_to(
            jnp.max(picked.astype(F32), axis=1, keepdims=True), (8, blocks)
        ).astype(jnp.int32)


def window_kernel(slots_here, block_len, head_dim, rows_ref, gain_ref, cos_ref, sin_ref, *rest):
    sources, (table_ref, held_ref, kv_ref, own_ref) = rest[:5], rest[5:9]
    lengths_ref, slot_ref, query_ref, w_ref, sems = rest[9:]
    lengths_hbm, slot_hbm, query_hbm, w_hbm, cache_ref = sources
    copies = fetch(
        (lengths_hbm, slot_hbm, query_hbm.at[pl.ds(0, query_ref.shape[0])], w_hbm, cache_ref),
        (lengths_ref, slot_ref, query_ref, w_ref, held_ref),
        sems,
    )
    normed = normalise(rows_ref, gain_ref)
    wait(copies[:4])
    keyval = project(normed, w_ref)
    is_key = lanes(keyval.shape) < head_dim
    turned = rope(keyval, cos_ref[...], sin_ref[...], head_dim // 2)
    both = jnp.where(is_key, turned, keyval).astype(BF16)
    kv_ref[...] = both[:1]
    both = both.astype(F32)
    score = jnp.sum(query_ref[:8, :].astype(F32) * both, axis=1, keepdims=True)
    own_ref[...] = jnp.where(is_key, score, both)
    find_slots(slots_here, block_len, lengths_ref, slot_ref, table_ref)
    wait(copies[4:])


def attend_kernel(
    tab_ref, query_ref, kv_ref, out_ref, q_s, score_s, max_s, acc_s
):
    slots_here, block_len, wide = kv_ref.shape
    requests = query_ref.shape[0] // GROUP
    low = subs((8, wide)) < GROUP
    token = lanes((8, block_len))
    lane = lanes((8, wide))
    for v in range(requests // 2):
        tile = query_ref[pl.ds(8 * v, 8), :].astype(F32)
        other = pltpu.roll(tile, GROUP, 0)
        q_s[2 * v] = jnp.where(low, tile, other)
        q_s[2 * v + 1] = jnp.where(low, other, tile)
    max_s[...] = jnp.full_like(max_s, MASKED)
    acc_s[...] = jnp.zeros_like(acc_s)

    def pair(p):
        a, b = tab_ref[2 * p], tab_ref[2 * p + 1]
        live = token < jnp.where(low, a & 255, b & 255)
        keys = kv_ref[pl.ds(2 * p, 2)].reshape(2 * block_len, wide)
        return lax.shift_right_logical(a, 8), lax.shift_right_logical(b, 8), live, keys

    for p in range(slots_here // 2):
        ra, rb, live, keys = pair(p)
        query = jnp.where(low, q_s[ra], q_s[rb]).astype(BF16)
        scores = lax.dot_general(
            query, keys, (((1,), (1,)), ((), ())), preferred_element_type=F32
        )
        scores = jnp.where(low, scores[:, :block_len], scores[:, block_len:])
        scores = jnp.where(live, scores, MASKED)
        score_s[p] = scores
        top = jnp.broadcast_to(jnp.max(scores, axis=1, keepdims=True), scores.shape)
        other = pltpu.roll(top, GROUP, 0)
        max_s[ra] = jnp.maximum(max_s[ra], jnp.where(low, top, other))
        max_s[rb] = jnp.maximum(max_s[rb], jnp.where(low, other, top))

    for p in range(slots_here // 2):
        ra, rb, live, values = pair(p)
        top = jnp.where(low, max_s[ra], max_s[rb])
        weight = jnp.where(live, jnp.exp(score_s[p] - top), 0.0).astype(BF16).astype(F32)
        both = jnp.concatenate(
            [jnp.where(low, weight, 0.0), jnp.where(low, 0.0, weight)], axis=1
        ).astype(BF16)
        out = jnp.dot(both, values, preferred_element_type=F32)
        total = jnp.sum(weight, axis=1, keepdims=True)
        out = jnp.where(lane < wide // 2, total, out)
        other = pltpu.roll(out, GROUP, 0)
        acc_s[ra] = acc_s[ra] + jnp.where(low, out, other)
        acc_s[rb] = acc_s[rb] + jnp.where(low, other, out)

    for v in range(requests // 2):
        top = jnp.where(low, max_s[2 * v], max_s[2 * v + 1])
        out = jnp.where(low, acc_s[2 * v], acc_s[2 * v + 1])
        out = jnp.where(lane < wide // 4, top, out)
        terms = []
        for _ in range(3):
            terms.append(out.astype(BF16).astype(F32))
            out = out - terms[-1]
        third = (lane % (wide // 4)) // TERM
        out = jnp.where(
            (lane >= wide // 2) | (third == 0),
            terms[0],
            jnp.where(third == 1, terms[1], terms[2]),
        )
        out_ref[pl.ds(8 * v, 8), :] = out.astype(BF16)


def combine_kernel(got_ref, own_ref, w_ref, out_ref):
    rows, wide = got_ref.shape
    lane = lanes((8, wide))
    row = subs((8, wide))
    parts = []
    for v in range(rows // 8):
        part = got_ref[pl.ds(8 * v, 8), :].astype(F32)
        whole = part + pltpu.roll(part, wide - TERM, 1) + pltpu.roll(part, wide - 2 * TERM, 1)
        parts.append(jnp.where(lane < wide // 2, whole, part))
    top = parts[0]
    for part in parts[1:]:
        top = jnp.maximum(top, part)
    own = own_ref[...]
    top = jnp.maximum(jnp.maximum(top, pltpu.roll(top, GROUP, 0)), own)
    mixed = jnp.zeros((8, wide), F32)
    for part in parts:
        weight = jnp.exp(part - top)
        mixed = mixed + jnp.broadcast_to(weight[:, :1], part.shape) * part
    mixed = mixed + pltpu.roll(mixed, GROUP, 0)
    own_weight = jnp.exp(own - top)
    mixed = mixed + jnp.broadcast_to(own_weight[:, :1], own.shape) * jnp.where(
        lane < wide // 2, 1.0, own
    )
    attended = mixed / jnp.broadcast_to(mixed[:, wide // 4 : wide // 4 + 1], mixed.shape)
    swapped = pltpu.roll(attended, wide // 2, 1)
    placed = jnp.where(
        row % 2 == 0,
        jnp.where(lane < wide // 2, swapped, 0.0),
        jnp.where(lane < wide // 2, 0.0, attended),
    )
    chunks = [
        jnp.sum(jnp.where(row // 2 == c, placed, 0.0), axis=0, keepdims=True)
        for c in range(GROUP // 2)
    ]
    line = jnp.broadcast_to(jnp.concatenate(chunks, axis=1), (8, GROUP // 2 * wide)).astype(BF16)
    lines = out_ref.shape[0]
    products = [
        jnp.dot(line, w_ref[:, pl.ds(v * 8 * wide, 8 * wide)], preferred_element_type=F32)
        for v in range(lines // 8)
    ]
    for v in range(lines // 8):
        tile = jnp.zeros((8, wide), F32)
        for k in range(8):
            n = (8 * v + k + FIRST_SHARD * GROUP // 2) % lines
            part = products[n // 8]
            tile = jnp.where(row == k, part[:, n % 8 * wide : (n % 8 + 1) * wide], tile)
        out_ref[pl.ds(8 * v, 8), :] = tile


def exchange(x, axis, parts, first=0):
    shape = x.shape
    x = x.reshape(parts, shape[0] // parts, shape[1])
    groups = [[(i + first) % parts for i in range(parts)]] if first else None
    return lax.all_to_all(
        x, axis, split_axis=0, concat_axis=0, tiled=True, axis_index_groups=groups
    ).reshape(shape)


def per_device(hidden, norm_gain, w_query, w_keyval, w_out, kv_cache, block_slot, lengths):
    slots_here, _, block_len, wide = kv_cache.shape
    head_dim = wide // 2
    requests = block_slot.shape[0]
    shards = lax.axis_size("mp")
    pools = lax.axis_size("pool")
    features = hidden.shape[1]
    lines = features // wide
    gain = far(norm_gain.reshape(shards * lines, wide))
    cache = far(kv_cache.reshape(slots_here, block_len, wide))
    line = far(hidden.reshape(lines, wide))
    w_query, w_keyval, lengths, block_slot = (
        far(x) for x in (w_query, w_keyval, lengths, block_slot)
    )
    turn = jax.ShapeDtypeStruct((8, wide), F32)
    spread_rows, held_query, held_gain, cosine, sine = call(
        functools.partial(prepare_kernel, head_dim),
        "prepare",
        (
            jax.ShapeDtypeStruct((shards * lines, wide), F32),
            jax.ShapeDtypeStruct(w_query.shape, BF16),
            jax.ShapeDtypeStruct(gain.shape, F32),
            turn,
            turn,
        ),
        [HBM] * 4,
        [
            pltpu.VMEM((lines, wide), F32),
            pltpu.SMEM(lengths.shape, jnp.int32),
            pltpu.SemaphoreType.DMA((4,)),
        ],
    )(line, lengths, w_query, gain)

    rows = exchange(spread_rows, "mp", shards, FIRST_SHARD)

    tiles = jax.ShapeDtypeStruct((requests * GROUP, wide), BF16)
    query = call(
        functools.partial(query_kernel, head_dim), "query", tiles, [VMEM] * 5
    )(rows, held_gain, held_query, cosine, sine)

    queries = exchange(query, "pool", pools, FIRST)

    table, held_cache, new_kv, own = call(
        functools.partial(window_kernel, slots_here, block_len, head_dim),
        "window",
        (
            jax.ShapeDtypeStruct((slots_here, block_slot.shape[1]), jnp.int32),
            jax.ShapeDtypeStruct(cache.shape, BF16),
            jax.ShapeDtypeStruct((1, wide), BF16),
            turn,
        ),
        [VMEM] * 4 + [HBM] * 5,
        [
            pltpu.SMEM(lengths.shape, jnp.int32),
            pltpu.VMEM(block_slot.shape, jnp.int32),
            pltpu.VMEM((16, wide), BF16),
            pltpu.VMEM(w_keyval.shape, BF16),
            pltpu.SemaphoreType.DMA((5,)),
        ],
        limit=8 << 20,
    )(rows, held_gain, cosine, sine, lengths, block_slot, far(query), w_keyval, cache)
    table = table[:, 0]

    per_request = pltpu.VMEM((requests, 8, wide), F32)
    partial = call(
        attend_kernel,
        "attend",
        tiles,
        [SMEM, VMEM, VMEM],
        [
            per_request,
            pltpu.VMEM((slots_here // 2, 8, block_len), F32),
            per_request,
            per_request,
        ],
        limit=12 << 20,
    )(table, queries, held_cache)

    got = exchange(partial, "pool", pools, FIRST)

    mixed = call(
        combine_kernel,
        "combine",
        jax.ShapeDtypeStruct((shards * lines, wide), F32),
        [VMEM, VMEM, VMEM],
    )(got, own, w_out)

    spread = exchange(mixed, "mp", shards, FIRST_SHARD)
    total = jnp.sum(spread.reshape(shards, features), axis=0, keepdims=True)
    return (hidden + RESIDUAL_SCALE * total, new_kv)


def solution(mesh):
    return jax.shard_map(
        per_device,
        mesh=mesh,
        in_specs=(
            P("pool", "mp"),
            P(),
            P(None, "mp"),
            P(None, "mp"),
            P("mp", None),
            P("pool", "mp", None, None),
            P(),
            P(),
        ),
        out_specs=(P("pool", "mp"), P("pool", "mp")),
        check_vma=False,
    )
```

```python
import functools
import math

import jax
import jax.numpy as jnp
from jax import lax
from jax.experimental import pallas as pl
from jax.experimental.pallas import tpu as pltpu
from jax.sharding import PartitionSpec as P

EPSILON = 1e-05
RESIDUAL_SCALE = 0.22
SCORE_SCALE = 0.015625
ROPE_BASE = 10000000.0
MASKED = -1e30

F32 = jnp.float32
BF16 = jnp.bfloat16
VMEM = pl.BlockSpec(memory_space=pltpu.VMEM)
SMEM = pl.BlockSpec(memory_space=pltpu.SMEM)
HBM = pl.BlockSpec(memory_space=pltpu.HBM)

GROUP = 4
TERM = 8

FIRST = 36
FIRST_SHARD = 3


def far(x):
    return pltpu.with_memory_space_constraint(x, pltpu.HBM)


def lanes(shape):
    return lax.broadcasted_iota(jnp.int32, shape, len(shape) - 1)


def subs(shape):
    return lax.broadcasted_iota(jnp.int32, shape, len(shape) - 2)


def call(body, name, out_shape, in_specs, scratch=(), limit=4 << 20, out_specs=None):
    many = isinstance(out_shape, tuple)
    return pl.pallas_call(
        body,
        out_shape=out_shape,
        in_specs=in_specs,
        out_specs=out_specs or ((VMEM,) * len(out_shape) if many else VMEM),
        scratch_shapes=list(scratch),
        compiler_params=pltpu.CompilerParams(vmem_limit_bytes=limit),
        name=name,
    )


def sine_cosine(angle):
    turn = jnp.floor(angle * (2.0 / math.pi) + 0.5)
    x = ((angle - turn * 1.5703125) - turn * 4.837512969970703e-4) - turn * 7.54978995489188e-8
    z = x * x
    sine = ((-1.9515295891e-4 * z + 8.3321608736e-3) * z - 1.6666654611e-1) * z * x + x
    cosine = ((2.443315711809948e-5 * z - 1.388731625493765e-3) * z + 4.166664568298827e-2) * z * z
    cosine = cosine - 0.5 * z + 1.0
    quadrant = turn.astype(jnp.int32) & 3
    odd = (quadrant & 1) == 1
    out_sine = jnp.where(odd, cosine, sine)
    out_cosine = jnp.where(odd, sine, cosine)
    out_sine = jnp.where(quadrant >= 2, -out_sine, out_sine)
    out_cosine = jnp.where((quadrant == 1) | (quadrant == 2), -out_cosine, out_cosine)
    return out_sine, out_cosine


def rotation(position, head_dim, width):
    half = head_dim // 2
    lane = lanes((8, width))
    pair = lane % half
    inverse = jnp.zeros((8, width), F32)
    for i in range(half):
        inverse = jnp.where(pair == i, ROPE_BASE ** (-2.0 * i / head_dim), inverse)
    sine, cosine = sine_cosine(position.astype(F32) * inverse)
    return cosine, jnp.where(lane % head_dim < half, -sine, sine)


def rope(x, cosine, sine, half):
    ahead = pltpu.roll(x, x.shape[1] - half, 1)
    behind = pltpu.roll(x, half, 1)
    first = lanes(x.shape) % (2 * half) < half
    return x * cosine + jnp.where(first, ahead, behind) * sine


def normalise(rows_ref, gain_ref):
    count = rows_ref.shape[0]
    x = rows_ref[...]
    total = jnp.sum(jnp.sum(x * x, axis=0, keepdims=True), axis=1, keepdims=True)
    scale = lax.rsqrt(total * (1.0 / x.size) + EPSILON)
    half = count // 2
    even = pl.ds(0, half, stride=2)
    odd = pl.ds(1, half, stride=2)
    left = pltpu.roll(rows_ref[even, :], FIRST_SHARD, 0) * scale * gain_ref[even, :]
    right = pltpu.roll(rows_ref[odd, :], FIRST_SHARD, 0) * scale * gain_ref[odd, :]
    return jnp.concatenate([left, right], axis=1)


def project(normed, weight_ref):
    chunks, wide = normed.shape
    row = subs(normed.shape)
    out = None
    for j in range(chunks):
        part = jnp.dot(
            jnp.where(row == j, normed, 0.0).astype(BF16),
            weight_ref[pl.ds(j * wide, wide), :],
            preferred_element_type=F32,
        )
        out = part if out is None else out + part
    return jnp.broadcast_to(jnp.sum(out, axis=0, keepdims=True), out.shape)


def fetch(sources, targets, sems):
    copies = [pltpu.make_async_copy(s, t, sems.at[i]) for i, (s, t) in enumerate(zip(sources, targets))]
    for copy in copies:
        copy.start()
    return copies


def wait(copies):
    for copy in copies:
        copy.wait()


def prepare_kernel(head_dim, x_ref, lengths_ref, *rest):
    sources, (spread_ref, *targets) = rest[:2], rest[2:5]
    cos_ref, sin_ref, near_x, near_lengths, sems = rest[5:]
    copies = fetch((x_ref, lengths_ref, *sources), (near_x, near_lengths, *targets), sems)
    wait(copies[1:2])
    position = near_lengths[lax.axis_index("pool")]
    cos_ref[...], sin_ref[...] = rotation(position, head_dim, 2 * head_dim)
    wait(copies[:1])
    size = near_x.shape[0]
    for i in range(spread_ref.shape[0] // size):
        spread_ref[pl.ds(i * size, size), :] = near_x[...]
    wait(copies[2:])


def query_kernel(head_dim, rows_ref, gain_ref, w_ref, cos_ref, sin_ref, out_ref):
    wide = 2 * head_dim
    cosine, sine = cos_ref[...], sin_ref[...]
    query = project(normalise(rows_ref, gain_ref), w_ref)
    row = subs((8, wide)) % GROUP
    tile = jnp.zeros((8, wide), F32)
    for c in range(GROUP // 2):
        part = rope(query[:, c * wide : (c + 1) * wide], cosine, sine, head_dim // 2)
        tile = jnp.where(row == 2 * c, part, tile)
        tile = jnp.where(row == 2 * c + 1, pltpu.roll(part, head_dim, 1), tile)
    tile = tile.astype(BF16).astype(F32) * SCORE_SCALE
    tile = jnp.where(lanes(tile.shape) < head_dim, tile, 0.0).astype(BF16)
    for v in range(out_ref.shape[0] // 8):
        out_ref[pl.ds(8 * v, 8), :] = tile


def find_slots(slots_here, block_len, lengths_ref, slot_ref, out_ref):
    requests, blocks = slot_ref.shape
    base = lax.axis_index("pool") * slots_here
    sub = subs((8, blocks))
    lane = lanes((8, blocks))
    wanted, payload = [], []
    for v in range(requests // 8):
        length = jnp.zeros((8, blocks), jnp.int32)
        for i in range(8):
            length = jnp.where(sub == i, lengths_ref[8 * v + i], length)
        limit = length - lane * block_len
        here = slot_ref[pl.ds(8 * v, 8), :] - base
        wanted.append(jnp.where(limit > 0, here, -1))
        payload.append(
            ((sub + 8 * v + requests - FIRST) % requests) * 256 + jnp.minimum(limit, block_len)
        )
    for tile in range(slots_here // 8):
        picked = jnp.zeros((8, blocks), jnp.int32)
        for i in range(8):
            found = jnp.zeros((8, blocks), jnp.int32)
            for w, p in zip(wanted, payload):
                found = jnp.where(w == 8 * tile + i, p, found)
            picked = jnp.where(sub == i, jnp.max(found, axis=0, keepdims=True), picked)
        out_ref[pl.ds(8 * tile, 8), :] = jnp.broadcast_to(
            jnp.max(picked.astype(F32), axis=1, keepdims=True), (8, blocks)
        ).astype(jnp.int32)


def window_kernel(slots_here, block_len, head_dim, rows_ref, gain_ref, cos_ref, sin_ref, *rest):
    sources, (table_ref, held_ref, kv_ref, own_ref) = rest[:5], rest[5:9]
    lengths_ref, slot_ref, query_ref, w_ref, sems = rest[9:]
    lengths_hbm, slot_hbm, query_hbm, w_hbm, cache_ref = sources
    copies = fetch(
        (lengths_hbm, slot_hbm, query_hbm.at[pl.ds(0, query_ref.shape[0])], w_hbm, cache_ref),
        (lengths_ref, slot_ref, query_ref, w_ref, held_ref),
        sems,
    )
    normed = normalise(rows_ref, gain_ref)
    wait(copies[:4])
    keyval = project(normed, w_ref)
    is_key = lanes(keyval.shape) < head_dim
    turned = rope(keyval, cos_ref[...], sin_ref[...], head_dim // 2)
    both = jnp.where(is_key, turned, keyval).astype(BF16)
    kv_ref[...] = both[:1]
    both = both.astype(F32)
    score = jnp.sum(query_ref[:8, :].astype(F32) * both, axis=1, keepdims=True)
    own_ref[...] = jnp.where(is_key, score, both)
    find_slots(slots_here, block_len, lengths_ref, slot_ref, table_ref)
    wait(copies[4:])


def attend_kernel(
    tab_ref, query_ref, kv_ref, out_ref, q_s, score_s, max_s, acc_s
):
    slots_here, block_len, wide = kv_ref.shape
    requests = query_ref.shape[0] // GROUP
    low = subs((8, wide)) < GROUP
    token = lanes((8, block_len))
    lane = lanes((8, wide))
    for v in range(requests // 2):
        tile = query_ref[pl.ds(8 * v, 8), :].astype(F32)
        other = pltpu.roll(tile, GROUP, 0)
        q_s[2 * v] = jnp.where(low, tile, other)
        q_s[2 * v + 1] = jnp.where(low, other, tile)
    max_s[...] = jnp.full_like(max_s, MASKED)
    acc_s[...] = jnp.zeros_like(acc_s)

    def pair(p):
        a, b = tab_ref[2 * p], tab_ref[2 * p + 1]
        live = token < jnp.where(low, a & 255, b & 255)
        keys = kv_ref[pl.ds(2 * p, 2)].reshape(2 * block_len, wide)
        return lax.shift_right_logical(a, 8), lax.shift_right_logical(b, 8), live, keys

    for p in range(slots_here // 2):
        ra, rb, live, keys = pair(p)
        query = jnp.where(low, q_s[ra], q_s[rb]).astype(BF16)
        scores = lax.dot_general(
            query, keys, (((1,), (1,)), ((), ())), preferred_element_type=F32
        )
        scores = jnp.where(low, scores[:, :block_len], scores[:, block_len:])
        scores = jnp.where(live, scores, MASKED)
        score_s[p] = scores
        top = jnp.broadcast_to(jnp.max(scores, axis=1, keepdims=True), scores.shape)
        other = pltpu.roll(top, GROUP, 0)
        max_s[ra] = jnp.maximum(max_s[ra], jnp.where(low, top, other))
        max_s[rb] = jnp.maximum(max_s[rb], jnp.where(low, other, top))

    for p in range(slots_here // 2):
        ra, rb, live, values = pair(p)
        top = jnp.where(low, max_s[ra], max_s[rb])
        weight = jnp.where(live, jnp.exp(score_s[p] - top), 0.0).astype(BF16).astype(F32)
        both = jnp.concatenate(
            [jnp.where(low, weight, 0.0), jnp.where(low, 0.0, weight)], axis=1
        ).astype(BF16)
        out = jnp.dot(both, values, preferred_element_type=F32)
        total = jnp.sum(weight, axis=1, keepdims=True)
        out = jnp.where(lane < wide // 2, total, out)
        other = pltpu.roll(out, GROUP, 0)
        acc_s[ra] = acc_s[ra] + jnp.where(low, out, other)
        acc_s[rb] = acc_s[rb] + jnp.where(low, other, out)

    for v in range(requests // 2):
        top = jnp.where(low, max_s[2 * v], max_s[2 * v + 1])
        out = jnp.where(low, acc_s[2 * v], acc_s[2 * v + 1])
        out = jnp.where(lane < wide // 4, top, out)
        terms = []
        for _ in range(3):
            terms.append(out.astype(BF16).astype(F32))
            out = out - terms[-1]
        third = (lane % (wide // 4)) // TERM
        out = jnp.where(
            (lane >= wide // 2) | (third == 0),
            terms[0],
            jnp.where(third == 1, terms[1], terms[2]),
        )
        out_ref[pl.ds(8 * v, 8), :] = out.astype(BF16)


def combine_kernel(got_ref, own_ref, w_ref, out_ref):
    rows, wide = got_ref.shape
    lane = lanes((8, wide))
    row = subs((8, wide))
    parts = []
    for v in range(rows // 8):
        part = got_ref[pl.ds(8 * v, 8), :].astype(F32)
        whole = part + pltpu.roll(part, wide - TERM, 1) + pltpu.roll(part, wide - 2 * TERM, 1)
        parts.append(jnp.where(lane < wide // 2, whole, part))
    top = parts[0]
    for part in parts[1:]:
        top = jnp.maximum(top, part)
    own = own_ref[...]
    top = jnp.maximum(jnp.maximum(top, pltpu.roll(top, GROUP, 0)), own)
    mixed = jnp.zeros((8, wide), F32)
    for part in parts:
        weight = jnp.exp(part - top)
        mixed = mixed + jnp.broadcast_to(weight[:, :1], part.shape) * part
    mixed = mixed + pltpu.roll(mixed, GROUP, 0)
    own_weight = jnp.exp(own - top)
    mixed = mixed + jnp.broadcast_to(own_weight[:, :1], own.shape) * jnp.where(
        lane < wide // 2, 1.0, own
    )
    attended = mixed / jnp.broadcast_to(mixed[:, wide // 4 : wide // 4 + 1], mixed.shape)
    swapped = pltpu.roll(attended, wide // 2, 1)
    placed = jnp.where(
        row % 2 == 0,
        jnp.where(lane < wide // 2, swapped, 0.0),
        jnp.where(lane < wide // 2, 0.0, attended),
    )
    chunks = [
        jnp.sum(jnp.where(row // 2 == c, placed, 0.0), axis=0, keepdims=True)
        for c in range(GROUP // 2)
    ]
    line = jnp.broadcast_to(jnp.concatenate(chunks, axis=1), (8, GROUP // 2 * wide)).astype(BF16)
    lines = out_ref.shape[0]
    products = [
        jnp.dot(line, w_ref[:, pl.ds(v * 8 * wide, 8 * wide)], preferred_element_type=F32)
        for v in range(lines // 8)
    ]
    for v in range(lines // 8):
        tile = jnp.zeros((8, wide), F32)
        for k in range(8):
            n = (8 * v + k + FIRST_SHARD * GROUP // 2) % lines
            part = products[n // 8]
            tile = jnp.where(row == k, part[:, n % 8 * wide : (n % 8 + 1) * wide], tile)
        out_ref[pl.ds(8 * v, 8), :] = tile


def exchange(x, axis, parts, first=0):
    shape = x.shape
    x = x.reshape(parts, shape[0] // parts, shape[1])
    groups = [[(i + first) % parts for i in range(parts)]] if first else None
    return lax.all_to_all(
        x, axis, split_axis=0, concat_axis=0, tiled=True, axis_index_groups=groups
    ).reshape(shape)


def per_device(hidden, norm_gain, w_query, w_keyval, w_out, kv_cache, block_slot, lengths):
    slots_here, _, block_len, wide = kv_cache.shape
    head_dim = wide // 2
    requests = block_slot.shape[0]
    shards = lax.axis_size("mp")
    pools = lax.axis_size("pool")
    features = hidden.shape[1]
    lines = features // wide
    gain = far(norm_gain.reshape(shards * lines, wide))
    cache = far(kv_cache.reshape(slots_here, block_len, wide))
    line = far(hidden.reshape(lines, wide))
    w_query, w_keyval, lengths, block_slot = (
        far(x) for x in (w_query, w_keyval, lengths, block_slot)
    )
    turn = jax.ShapeDtypeStruct((8, wide), F32)
    spread_rows, held_query, held_gain, cosine, sine = call(
        functools.partial(prepare_kernel, head_dim),
        "prepare",
        (
            jax.ShapeDtypeStruct((shards * lines, wide), F32),
            jax.ShapeDtypeStruct(w_query.shape, BF16),
            jax.ShapeDtypeStruct(gain.shape, F32),
            turn,
            turn,
        ),
        [HBM] * 4,
        [
            pltpu.VMEM((lines, wide), F32),
            pltpu.SMEM(lengths.shape, jnp.int32),
            pltpu.SemaphoreType.DMA((4,)),
        ],
    )(line, lengths, w_query, gain)

    rows = exchange(spread_rows, "mp", shards, FIRST_SHARD)

    tiles = jax.ShapeDtypeStruct((requests * GROUP, wide), BF16)
    query = call(
        functools.partial(query_kernel, head_dim), "query", tiles, [VMEM] * 5
    )(rows, held_gain, held_query, cosine, sine)

    queries = exchange(query, "pool", pools, FIRST)

    table, held_cache, new_kv, own = call(
        functools.partial(window_kernel, slots_here, block_len, head_dim),
        "window",
        (
            jax.ShapeDtypeStruct((slots_here, block_slot.shape[1]), jnp.int32),
            jax.ShapeDtypeStruct(cache.shape, BF16),
            jax.ShapeDtypeStruct((1, wide), BF16),
            turn,
        ),
        [VMEM] * 4 + [HBM] * 5,
        [
            pltpu.SMEM(lengths.shape, jnp.int32),
            pltpu.VMEM(block_slot.shape, jnp.int32),
            pltpu.VMEM((16, wide), BF16),
            pltpu.VMEM(w_keyval.shape, BF16),
            pltpu.SemaphoreType.DMA((5,)),
        ],
        limit=8 << 20,
    )(rows, held_gain, cosine, sine, lengths, block_slot, far(query), w_keyval, cache)
    table = table[:, 0]

    per_request = pltpu.VMEM((requests, 8, wide), F32)
    partial = call(
        attend_kernel,
        "attend",
        tiles,
        [SMEM, VMEM, VMEM],
        [
            per_request,
            pltpu.VMEM((slots_here // 2, 8, block_len), F32),
            per_request,
            per_request,
        ],
        limit=12 << 20,
    )(table, queries, held_cache)

    got = exchange(partial, "pool", pools, FIRST)

    mixed = call(
        combine_kernel,
        "combine",
        jax.ShapeDtypeStruct((shards * lines, wide), F32),
        [VMEM, VMEM, VMEM],
    )(got, own, w_out)

    spread = exchange(mixed, "mp", shards, FIRST_SHARD)
    total = jnp.sum(spread.reshape(shards, features), axis=0, keepdims=True)
    return (hidden + RESIDUAL_SCALE * total, new_kv)


def solution(mesh):
    return jax.shard_map(
        per_device,
        mesh=mesh,
        in_specs=(
            P("pool", "mp"),
            P(),
            P(None, "mp"),
            P(None, "mp"),
            P("mp", None),
            P("pool", "mp", None, None),
            P(),
            P(),
        ),
        out_specs=(P("pool", "mp"), P("pool", "mp")),
        check_vma=False,
    )
```
